512 devices in a mesh: row: 8 (over y, core), col: 16 (over z), ch: 4 (over x).
Axes of the slice: x: 4, y: 4, z: 16, core: 2. Of those that a mesh axis runs over, the one named last changes fastest.
Arguments:
- image: bfloat16 [256, 32, 2048], P('ch', 'row', 'col'), may hold values from -6 to 6
- depth_kernel: float32 [256, 49], P('ch'), may hold values from -0.875 to 0.875
- norm_gain: float32 [256], P('ch'), may hold values from 0.25 to 1.75
- norm_shift: float32 [256], P('ch'), may hold values from -3 to 3
- expand_weight: bfloat16 [256, 1024], P(None, 'ch'), may hold values from -0.375 to 0.375
- expand_bias: float32 [1024], replicated, may hold values from -3 to 3
- reduce_weight: bfloat16 [1024, 256], P('ch'), may hold values from -0.1875 to 0.1875
- cotangent: bfloat16 [256, 32, 2048], P('ch', 'row', 'col'), may hold values from -6 to 6
Outputs:
- result: bfloat16 [256, 32, 2048], P('ch', 'row', 'col')
- grad_image: bfloat16 [256, 32, 2048], P('ch', 'row', 'col')
- grad_kernel: float32 [256, 49], P('ch')
- grad_gain: float32 [256], P('ch')
- grad_shift: float32 [256], P('ch')
- grad_expand: float32 [256, 1024], P(None, 'ch')
- grad_offset: float32 [1024], P('ch')
- grad_reduce: float32 [1024, 256], P('ch')
The draws below stay inside these ranges and needn't reach their ends.
All inputs are finite; a program needn't handle non-finite values.
Results may differ from the reference program's by a relative error of at most 0.011.
Values may be sent and summed in bfloat16 or wider, within the bound.
No kernel may reach another device: no remote copies, remote signals or barrier semaphores. Data moves between devices by JAX's collectives and lax.ppermute only.
A program may use at most 64 MiB of HBM per device.

```python
import math
import jax
import jax.numpy as jnp
from jax import lax

C = 256
F = 1024
KSIZE = 7
H = 32
W = 2048
PIX = 65536


def levels(key, extent, shards, smallest, high):
    def one(axis_at, shards_of):
        steps = jax.random.uniform(jax.random.fold_in(jax.random.fold_in(key, 6), axis_at), (shards_of,), jnp.float32, smallest / len(shards), high / len(shards))
        return jnp.repeat(jnp.exp(steps), extent[axis_at] // shards_of).reshape((-1,) + (1,) * (len(extent) - axis_at - 1))

    gain = one(*shards[0])
    for cut in shards[1:]:
        gain = gain * one(*cut)
    return gain


def bell_draw(key, extent, scale, most, shards=(), held_as=jnp.bfloat16):
    entries = scale * jax.random.normal(key, extent, jnp.float32)
    if shards:
        entries = entries * levels(key, extent, shards, -0.22, 0.18)
    return jnp.clip(entries, -most, most).astype(held_as)


def setup_inputs(seed: int = 0) -> dict:
    splits = jax.random.split(jax.random.key(seed), 9)
    return {
        "image": bell_draw(splits[0], (C, H, W), 1.0, 6.0, ((0, 4), (1, 8), (2, 16))),
        "depth_kernel": bell_draw(splits[1], (C, KSIZE * KSIZE), (KSIZE * KSIZE) ** -0.5, 0.875, ((0, 4),), jnp.float32),
        "norm_gain": jnp.clip(1.0 + 0.15 * jax.random.normal(splits[2], (C,), jnp.float32), 0.25, 1.75),
        "norm_shift": bell_draw(splits[3], (C,), 0.5, 3.0, ((0, 4),), jnp.float32),
        "expand_weight": bell_draw(splits[4], (C, F), C ** -0.5, 0.375, ((1, 4),)),
        "expand_bias": bell_draw(splits[5], (F,), 0.5, 3.0, (), jnp.float32),
        "reduce_weight": bell_draw(splits[6], (F, C), F ** -0.5, 0.1875, ((0, 4),)),
        "cotangent": bell_draw(splits[7], (C, H, W), 1.0, 6.0, ((0, 4), (1, 8), (2, 16))),
    }


epsilon = 1e-06
root_two_pi = 0.7978845608028654
cubic_coef = 0.044715

def product(left, right, dims):
    return lax.dot_general(left.astype(jnp.float32), right.astype(jnp.float32), dims, preferred_element_type=jnp.float32)

def gelu_pair(hidden):
    inner = root_two_pi * (hidden + cubic_coef * hidden * hidden * hidden)
    tangent = jnp.tanh(inner)
    value = 0.5 * hidden * (1.0 + tangent)
    slope = 0.5 * (1.0 + tangent) + 0.5 * hidden * (1.0 - tangent * tangent) * root_two_pi * (1.0 + 3.0 * cubic_coef * hidden * hidden)
    return (value, slope)

def tap_window(padded, kernel, tap, first, second, tile_rows, tile_cols):
    window = lax.dynamic_slice(padded, (jnp.int32(0), first, second), (padded.shape[0], tile_rows, tile_cols))
    weight = lax.dynamic_slice_in_dim(kernel, tap, 1, 1)
    return weight[:, :, None] * window

def forward_taps(padded, kernel, span, tile_rows, tile_cols):

    def step(tap, accum):
        tap = jnp.asarray(tap).astype(jnp.int32)
        first = (tap // span).astype(jnp.int32)
        second = (tap % span).astype(jnp.int32)
        return accum + tap_window(padded, kernel, tap, first, second, tile_rows, tile_cols)
    accum = jnp.zeros((padded.shape[0], tile_rows, tile_cols), jnp.float32)
    return lax.fori_loop(0, span * span, step, accum)

def backward_taps(padded, kernel, span, tile_rows, tile_cols):
    reach = span - 1

    def step(tap, accum):
        tap = jnp.asarray(tap).astype(jnp.int32)
        first = (reach - tap // span).astype(jnp.int32)
        second = (reach - tap % span).astype(jnp.int32)
        return accum + tap_window(padded, kernel, tap, first, second, tile_rows, tile_cols)
    accum = jnp.zeros((padded.shape[0], tile_rows, tile_cols), jnp.float32)
    return lax.fori_loop(0, span * span, step, accum)

def kernel_grad(grad_mixed, padded, span, tile_rows, tile_cols):

    def step(tap, table):
        tap = jnp.asarray(tap).astype(jnp.int32)
        first = (tap // span).astype(jnp.int32)
        second = (tap % span).astype(jnp.int32)
        window = lax.dynamic_slice(padded, (jnp.int32(0), first, second), (padded.shape[0], tile_rows, tile_cols))
        column = lax.optimization_barrier(jnp.sum(grad_mixed * window, axis=(1, 2)))
        return lax.dynamic_update_slice_in_dim(table, column[:, None], tap, 1)
    table = jnp.zeros((grad_mixed.shape[0], span * span), jnp.float32)
    return lax.fori_loop(0, span * span, step, table)

def reference(image, depth_kernel, norm_gain, norm_shift, expand_weight, expand_bias, reduce_weight, cotangent):
    half = KSIZE // 2
    plain = (((1,), (0,)), ((), ()))
    last = (((1,), (1,)), ((), ()))
    padded = jnp.pad(image.astype(jnp.float32), ((0, 0), (half, half), (half, half)))
    mixed = forward_taps(padded, depth_kernel, KSIZE, H, W)
    centre = lax.optimization_barrier(jnp.mean(mixed, axis=0))
    diff = mixed - centre
    variance = lax.optimization_barrier(jnp.mean(diff * diff, axis=0))
    inverse = lax.rsqrt(variance + epsilon)
    normed = diff * inverse
    normal = (normed * norm_gain[:, None, None] + norm_shift[:, None, None]).astype(jnp.bfloat16)
    block = math.gcd(PIX, 8192)
    count = PIX // block
    panels = normal.reshape(C, count, block).transpose(1, 0, 2)
    cot_panels = cotangent.reshape(C, count, block).transpose(1, 0, 2)
    expand_t = expand_weight.T
    reduce_t = reduce_weight.T

    def step(carry, pair):
        grad_exp, grad_off, grad_red = carry
        panel, cot_panel = pair
        hidden = product(expand_t, panel, plain) + expand_bias[:, None]
        value, slope = gelu_pair(hidden)
        active = value.astype(jnp.bfloat16)
        mlp_part = product(reduce_t, active, plain)
        grad_act = product(reduce_weight, cot_panel, plain)
        grad_hidden = (grad_act * slope).astype(jnp.bfloat16)
        grad_red = grad_red + product(active, cot_panel, last)
        grad_exp = grad_exp + product(panel, grad_hidden, last)
        grad_off = grad_off + lax.optimization_barrier(jnp.sum(grad_hidden.astype(jnp.float32), axis=1))
        grad_part = product(expand_weight, grad_hidden, plain)
        return ((grad_exp, grad_off, grad_red), (mlp_part, grad_part))
    init = (jnp.zeros((C, F), jnp.float32), jnp.zeros((F,), jnp.float32), jnp.zeros((F, C), jnp.float32))
    sums, blocks = lax.scan(step, init, (panels, cot_panels))
    grad_exp, grad_off, grad_red = sums
    mlp_out = blocks[0].transpose(1, 0, 2).reshape(C, H, W)
    grad_normal = blocks[1].transpose(1, 0, 2).reshape(C, H, W)
    result = (image.astype(jnp.float32) + mlp_out).astype(jnp.bfloat16)
    grad_gain = lax.optimization_barrier(jnp.sum(grad_normal * normed, axis=(1, 2)))
    grad_shift = lax.optimization_barrier(jnp.sum(grad_normal, axis=(1, 2)))
    grad_normed = grad_normal * norm_gain[:, None, None]
    grad_mixed = inverse * (grad_normed - lax.optimization_barrier(jnp.mean(grad_normed, axis=0)) - normed * lax.optimization_barrier(jnp.mean(grad_normed * normed, axis=0)))
    grad_pad = jnp.pad(grad_mixed, ((0, 0), (half, half), (half, half)))
    grad_image = (cotangent.astype(jnp.float32) + backward_taps(grad_pad, depth_kernel, KSIZE, H, W)).astype(jnp.bfloat16)
    grad_kernel = kernel_grad(grad_mixed, padded, KSIZE, H, W)
    scale = float(PIX) ** (-0.5)
    return (result, grad_image, grad_kernel * scale, grad_gain * scale, grad_shift * scale, grad_exp * scale, grad_off * scale, grad_red * scale)
```

```python
import functools
import jax
import jax.numpy as jnp
from jax import lax
from jax.experimental import pallas as pl
from jax.experimental.pallas import tpu as pltpu
from jax.sharding import PartitionSpec as P

KSIZE = 7
HALF = 3
SPAN = KSIZE + HALF
epsilon = 1e-06
root_two_pi = 0.7978845608028654
cubic_coef = 0.044715
f32 = jnp.float32
bf16 = jnp.bfloat16
LANES = 128
CT = 16


def lane_ids(rows):
    return lax.broadcasted_iota(jnp.int32, (rows, LANES), 1)


def rolled(x, shift):
    shift = shift % LANES
    return x if shift == 0 else pltpu.roll(x, shift, 1)


def split3(x):
    hi = x.astype(bf16)
    rest = x - hi.astype(f32)
    mid = rest.astype(bf16)
    low = (rest - mid.astype(f32)).astype(bf16)
    return [hi.astype(f32), mid.astype(f32), low.astype(f32)]


def gelu_pair(hidden):
    inner = root_two_pi * (hidden + cubic_coef * hidden * hidden * hidden)
    tangent = jnp.tanh(inner)
    value = 0.5 * hidden * (1.0 + tangent)
    slope = 0.5 * (1.0 + tangent) + 0.5 * hidden * (1.0 - tangent * tangent) * root_two_pi * (
        1.0 + 3.0 * cubic_coef * hidden * hidden
    )
    return (value, slope)


def halo_rows(up, mid, down, left, right, at):
    lane = lane_ids(CT)
    l = left[at, :].astype(f32)
    r = right[at, :].astype(f32)
    rows = []
    for i in range(SPAN):
        if i < HALF:
            x = up[i, at, :]
        elif i < SPAN - HALF:
            x = mid[i - HALF, at, :]
        else:
            x = down[i - (SPAN - HALF), at, :]
        edge = jnp.where(
            lane >= 64, rolled(l, LANES - HALF - HALF * i), rolled(r, LANES - HALF * i)
        )
        rows.append((x.astype(f32), edge))
    return rows


def window(row, s):
    x, edge = row
    if s == 0:
        return x
    lane = lane_ids(CT)
    mask = (lane < -s) if s < 0 else (lane >= LANES - s)
    return jnp.where(mask, rolled(edge, -s), rolled(x, -s))


def edges_kernel(up, mid, down, first, last):
    channels = mid.shape[1]
    lane = lane_ids(CT)

    def step(t, carry):
        at = pl.ds(pl.multiple_of(t * CT, CT), CT)
        head = jnp.zeros((CT, LANES), f32)
        tail = jnp.zeros((CT, LANES), f32)
        for i in range(SPAN):
            if i < HALF:
                x = up[i, at, :]
            elif i < SPAN - HALF:
                x = mid[i - HALF, at, :]
            else:
                x = down[i - (SPAN - HALF), at, :]
            x = x.astype(f32)
            mask = (lane >= HALF * i) & (lane < HALF * i + HALF)
            head = jnp.where(mask, rolled(x, HALF * i), head)
            tail = jnp.where(mask, rolled(x, HALF * i + HALF), tail)
        first[at, :] = head.astype(bf16)
        last[at, :] = tail.astype(bf16)
        return carry

    lax.fori_loop(0, channels // CT, step, 0)


def edges(up, mid, down):
    shape = jax.ShapeDtypeStruct((mid.shape[1], LANES), bf16)
    return pl.pallas_call(edges_kernel, out_shape=(shape, shape), name="edges")(up, mid, down)


def accumulate_taps(rows, kern, at, flip):
    accum = [jnp.zeros((CT, LANES), f32) for _ in range(SPAN - KSIZE + 1)]
    weights = kern[at, :]
    for b in range(KSIZE):
        shifted = [window(row, b - HALF) for row in rows]
        for a in range(KSIZE):
            tap = a * KSIZE + b
            if flip:
                tap = KSIZE * KSIZE - 1 - tap
            w = jnp.broadcast_to(weights[:, tap : tap + 1], (CT, LANES))
            for i in range(len(accum)):
                accum[i] = accum[i] + w * shifted[i + a]
    return accum


def forward_kernel(up, mid, down, left, right, kern, gain, shift, cot, mixed, payload):
    tile_rows, channels, _ = mid.shape

    def step(t, carry):
        at = pl.ds(pl.multiple_of(t * CT, CT), CT)
        rows = halo_rows(up, mid, down, left, right, at)
        accum = accumulate_taps(rows, kern, at, False)
        for i in range(tile_rows):
            mixed[at, i * LANES : (i + 1) * LANES] = accum[i]
        return carry

    lax.fori_loop(0, channels // CT, step, 0)
    pixels = tile_rows * LANES
    for i in range(tile_rows):
        cols = slice(i * LANES, (i + 1) * LANES)
        x = mixed[:, cols]
        mean = jnp.sum(x, axis=0, keepdims=True) / channels
        dev = x - mean
        spread = jnp.sum(dev * dev, axis=0, keepdims=True)
        rows = split3(mean) + split3(spread)
        stats = jnp.concatenate(rows + [jnp.zeros((CT - 6, LANES), f32)], axis=0)
        if i == 0:
            row_id = lax.broadcasted_iota(jnp.int32, (CT, LANES), 0)
            both = jnp.concatenate([gain[...], shift[...]], axis=1)
            for k, part in enumerate(split3(both)):
                stats = jnp.where(row_id == 6 + k, jnp.broadcast_to(part, (CT, LANES)), stats)
        dev = dev.astype(bf16)
        stats = stats.astype(bf16)
        for d in range(payload.shape[0]):
            payload[d, 0:channels, cols] = dev
            payload[d, channels : 2 * channels, cols] = cot[i]
            payload[d, 2 * channels : 2 * channels + CT, cols] = stats


def forward(up, mid, down, left, right, kern, gain, shift, cot, parts):
    tile_rows, channels, _ = mid.shape
    pixels = tile_rows * LANES
    return pl.pallas_call(
        forward_kernel,
        out_shape=(
            jax.ShapeDtypeStruct((channels, pixels), f32),
            jax.ShapeDtypeStruct((parts, 2 * channels + CT, pixels), bf16),
        ),
        name="forward",
    )(up, mid, down, left, right, kern, gain, shift, cot)


def column(row, n):
    i = lax.broadcasted_iota(jnp.int32, (n, n), 0)
    j = lax.broadcasted_iota(jnp.int32, (n, n), 1)
    return jnp.sum(jnp.where(i == j, jnp.broadcast_to(row, (n, n)), 0.0), axis=1, keepdims=True)


def row_of(col, n):
    i = lax.broadcasted_iota(jnp.int32, (n, n), 0)
    j = lax.broadcasted_iota(jnp.int32, (n, n), 1)
    return jnp.sum(jnp.where(i == j, jnp.broadcast_to(col, (n, n)), 0.0), axis=0, keepdims=True)


def dot(a, b, dims):
    return lax.dot_general(a, b, (dims, ((), ())), preferred_element_type=f32)


def mlp_kernel(recv, w_exp, bias, w_red, payload, stats_out, grads, off, s_norm, s_act, s_cot, s_gh):
    parts, height, pixels = recv.shape
    ch = (height - CT) // 2
    total = parts * ch
    width = 2 * LANES
    gains, shifts = [], []
    for k in range(parts):
        head = recv[k, 2 * ch : 2 * ch + CT, 0:LANES].astype(f32)
        both = head[6:7] + head[7:8] + head[8:9]
        gains.append(column(both[:, 0:ch], ch))
        shifts.append(column(both[:, ch : 2 * ch], ch))
    bias_col = column(bias[...], bias.shape[1])
    for blk in range(pixels // width):
        cols = slice(blk * width, (blk + 1) * width)
        means, spreads = [], []
        for k in range(parts):
            st = recv[k, 2 * ch : 2 * ch + CT, cols].astype(f32)
            means.append(st[0:1] + st[1:2] + st[2:3])
            spreads.append(st[3:4] + st[4:5] + st[5:6])
        centre = sum(means) / parts
        spread = sum(spreads)
        for k in range(parts):
            gap = means[k] - centre
            spread = spread + ch * gap * gap
        inverse = lax.rsqrt(spread / total + epsilon)
        stats_out[0:1, cols] = centre
        stats_out[1:2, cols] = inverse
        for k in range(parts):
            at = slice(k * ch, (k + 1) * ch)
            dev = recv[k, 0:ch, cols].astype(f32)
            normed = (dev + (means[k] - centre)) * inverse
            s_norm[at, cols] = (normed * gains[k] + shifts[k]).astype(bf16)
            s_cot[at, cols] = recv[k, ch : 2 * ch, cols]
        hidden = dot(w_exp[...], s_norm[:, cols], ((0,), (0,))) + bias_col
        value, slope = gelu_pair(hidden)
        active = value.astype(bf16)
        s_act[:, cols] = active
        gh = (dot(w_red[...], s_cot[:, cols], ((1,), (0,))) * slope).astype(bf16)
        s_gh[:, cols] = gh
        mlp = dot(w_red[...], active, ((0,), (0,)))
        part = dot(w_exp[...], gh, ((1,), (0,)))
        plain = jnp.zeros((1, width), f32)
        cross = jnp.zeros((1, width), f32)
        for k in range(parts):
            at = slice(k * ch, (k + 1) * ch)
            dev = recv[k, 0:ch, cols].astype(f32)
            normed = (dev + (means[k] - centre)) * inverse
            scaled = part[at] * gains[k]
            plain = plain + jnp.sum(scaled, axis=0, keepdims=True)
            cross = cross + jnp.sum(scaled * normed, axis=0, keepdims=True)
            payload[k, 0:ch, cols] = mlp[at].astype(bf16)
            payload[k, ch : 2 * ch, cols] = part[at].astype(bf16)
        sums = jnp.concatenate(
            split3(plain) + split3(cross) + [jnp.zeros((CT - 6, width), f32)], axis=0
        ).astype(bf16)
        for k in range(parts):
            payload[k, 2 * ch : 2 * ch + CT, cols] = sums
    last = ((1,), (1,))
    grad_exp = dot(s_norm[...], s_gh[...], last)
    grad_red = dot(s_act[...], s_cot[...], last)
    n = grad_exp.shape[0]
    grads[0:n, :] = grad_exp[:, 0:LANES]
    grads[n : 2 * n, :] = grad_exp[:, LANES:]
    grads[2 * n : 3 * n, :] = grad_red[:, 0:LANES]
    grads[3 * n : 4 * n, :] = grad_red[:, LANES:]
    off[...] = dot(jnp.ones((8, pixels), bf16), s_gh[...], last)


def mlp(recv, w_exp, bias, w_red):
    parts, height, pixels = recv.shape
    hid = w_red.shape[0]
    total = w_exp.shape[0]
    return pl.pallas_call(
        mlp_kernel,
        out_shape=(
            jax.ShapeDtypeStruct(recv.shape, bf16),
            jax.ShapeDtypeStruct((2, pixels), f32),
            jax.ShapeDtypeStruct((4 * total, LANES), f32),
            jax.ShapeDtypeStruct((8, hid), f32),
        ),
        scratch_shapes=[
            pltpu.VMEM((total, pixels), bf16),
            pltpu.VMEM((hid, pixels), bf16),
            pltpu.VMEM((total, pixels), bf16),
            pltpu.VMEM((hid, pixels), bf16),
        ],
        name="mlp",
    )(recv, w_exp, bias, w_red)


def norm_back_kernel(recv, mixed, stats, gain, image, result, grad_mixed, rounded, small):
    parts, height, pixels = recv.shape
    ch = (height - CT) // 2
    tile_rows = image.shape[0]
    total = parts * ch
    gain_col = column(gain[...], ch)
    acc_gain = jnp.zeros((ch, LANES), f32)
    acc_shift = jnp.zeros((ch, LANES), f32)
    for i in range(tile_rows):
        cols = slice(i * LANES, (i + 1) * LANES)
        mlp_out = jnp.zeros((ch, LANES), f32)
        grad = jnp.zeros((ch, LANES), f32)
        sums = jnp.zeros((CT, LANES), f32)
        for k in range(parts):
            mlp_out = mlp_out + recv[k, 0:ch, cols].astype(f32)
            grad = grad + recv[k, ch : 2 * ch, cols].astype(f32)
            sums = sums + recv[k, 2 * ch : 2 * ch + CT, cols].astype(f32)
        result[i] = (image[i].astype(f32) + mlp_out).astype(bf16)
        plain = (sums[0:1] + sums[1:2] + sums[2:3]) / total
        cross = (sums[3:4] + sums[4:5] + sums[5:6]) / total
        inverse = stats[1:2, cols]
        normed = (mixed[:, cols] - stats[0:1, cols]) * inverse
        acc_gain = acc_gain + grad * normed
        acc_shift = acc_shift + grad
        out = inverse * (grad * gain_col - plain - normed * cross)
        grad_mixed[i] = out
        rounded[i] = out.astype(bf16)
    g = row_of(jnp.sum(acc_gain, axis=1, keepdims=True), ch)
    s = row_of(jnp.sum(acc_shift, axis=1, keepdims=True), ch)
    small[...] = jnp.broadcast_to(jnp.concatenate([g, s], axis=1), (8, LANES))


def norm_back(recv, mixed, stats, gain, image):
    tile_rows, channels, _ = image.shape
    return pl.pallas_call(
        norm_back_kernel,
        out_shape=(
            jax.ShapeDtypeStruct(image.shape, bf16),
            jax.ShapeDtypeStruct(image.shape, f32),
            jax.ShapeDtypeStruct(image.shape, bf16),
            jax.ShapeDtypeStruct((8, LANES), f32),
        ),
        name="norm_back",
    )(recv, mixed, stats, gain, image)


def tap_grad_kernel(up, mid, down, left, right, grad_mixed, small, off, out):
    tile_rows, channels, _ = mid.shape
    lane = lane_ids(CT)

    def step(t, carry):
        at = pl.ds(pl.multiple_of(t * CT, CT), CT)
        rows = halo_rows(up, mid, down, left, right, at)
        grads = [grad_mixed[i, at, :] for i in range(tile_rows)]
        table = jnp.zeros((CT, LANES), f32)
        for b in range(KSIZE):
            shifted = [window(row, b - HALF) for row in rows]
            for a in range(KSIZE):
                accum = grads[0] * shifted[a]
                for i in range(1, tile_rows):
                    accum = accum + grads[i] * shifted[a + i]
                value = jnp.sum(accum, axis=1, keepdims=True)
                table = jnp.where(lane == a * KSIZE + b, value, table)
        out[at, :] = table
        return carry

    lax.fori_loop(0, channels // CT, step, 0)
    hid = off.shape[1]
    out[channels : channels + 8, :] = small[...]
    for j in range(hid // LANES):
        out[channels + 8 * (j + 1) : channels + 8 * (j + 2), :] = off[:, j * LANES : (j + 1) * LANES]
    used = channels + 8 * (1 + hid // LANES)
    out[used:, :] = jnp.zeros((out.shape[0] - used, LANES), f32)


def tap_grad(up, mid, down, left, right, grad_mixed, small, off):
    return pl.pallas_call(
        tap_grad_kernel,
        out_shape=jax.ShapeDtypeStruct((LANES, LANES), f32),
        name="tap_grad",
    )(up, mid, down, left, right, grad_mixed, small, off)


def backward_kernel(up, mid, down, left, right, kern, cot, out):
    tile_rows, channels, _ = mid.shape

    def step(t, carry):
        at = pl.ds(pl.multiple_of(t * CT, CT), CT)
        rows = halo_rows(up, mid, down, left, right, at)
        accum = accumulate_taps(rows, kern, at, True)
        for i in range(tile_rows):
            out[i, at, :] = (cot[i, at, :].astype(f32) + accum[i]).astype(bf16)
        return carry

    lax.fori_loop(0, channels // CT, step, 0)


def backward(up, mid, down, left, right, kern, cot):
    return pl.pallas_call(
        backward_kernel,
        out_shape=jax.ShapeDtypeStruct(cot.shape, bf16),
        name="backward",
    )(up, mid, down, left, right, kern, cot)


def final_kernel(scale, flat, exp_ref, red_ref, taps_ref, vec_ref):
    n = exp_ref.shape[0]
    exp_ref[:, 0:LANES] = flat[0:n, :] * scale
    exp_ref[:, LANES:] = flat[n : 2 * n, :] * scale
    red_ref[:, 0:LANES] = flat[2 * n : 3 * n, :] * scale
    red_ref[:, LANES:] = flat[3 * n : 4 * n, :] * scale
    base = 4 * n
    channels = taps_ref.shape[0]
    taps_ref[...] = flat[base : base + channels, 0 : taps_ref.shape[1]] * scale
    vec_ref[...] = flat[base + channels : base + channels + vec_ref.shape[0], :] * scale


def final(flat, scale, total, hid, channels, taps):
    return pl.pallas_call(
        functools.partial(final_kernel, scale),
        out_shape=(
            jax.ShapeDtypeStruct((total, hid), f32),
            jax.ShapeDtypeStruct((hid, total), f32),
            jax.ShapeDtypeStruct((channels, taps), f32),
            jax.ShapeDtypeStruct((8 * (1 + hid // LANES), LANES), f32),
        ),
        name="final",
    )(flat)


def neighbours(first, last, axis):
    size = lax.axis_size(axis)
    up = [(i, i + 1) for i in range(size - 1)]
    down = [(j, i) for i, j in up]
    return lax.ppermute(last, axis, up), lax.ppermute(first, axis, down)


def halo(x):
    rows = x.shape[0]
    up, down = neighbours(x[:HALF], x[rows - HALF :], "row")
    first, last = edges(up, x, down)
    left, right = neighbours(first, last, "col")
    return up, down, left, right


def reduce_all(flat):
    rows, cols = lax.axis_size("row"), lax.axis_size("col")
    height = flat.shape[0]
    part = lax.all_to_all(flat.reshape(rows, height // rows, LANES), "row", 0, 0).sum(0)
    part = part.reshape(cols, height // rows // cols, LANES)
    part = lax.all_to_all(part, "col", 0, 0).sum(0)
    part = jnp.broadcast_to(part[None], (cols,) + part.shape)
    part = lax.all_to_all(part, "col", 0, 0).reshape(height // rows, LANES)
    return lax.all_gather(part, "row", axis=0, tiled=True)


def body(
    image, depth_kernel, norm_gain, norm_shift, expand_weight, expand_bias, reduce_weight, cotangent
):
    channels, tile_rows, tile_cols = image.shape
    pixels = tile_rows * tile_cols
    parts = lax.axis_size("ch")
    hid = reduce_weight.shape[0]
    total = expand_weight.shape[0]
    img = jnp.transpose(image, (1, 0, 2))
    cot = jnp.transpose(cotangent, (1, 0, 2))
    gain = norm_gain.reshape(1, channels)
    shift = norm_shift.reshape(1, channels)
    bias = lax.dynamic_slice_in_dim(expand_bias, lax.axis_index("ch") * hid, hid).reshape(1, hid)
    up, down, left, right = halo(img)
    mixed, send = forward(up, img, down, left, right, depth_kernel, gain, shift, cot, parts)
    recv = lax.all_to_all(send, "ch", 0, 0)
    send, stats, grads, off = mlp(recv, expand_weight, bias, reduce_weight)
    recv = lax.all_to_all(send, "ch", 0, 0)
    result, grad_mixed, rounded, small = norm_back(recv, mixed, stats, gain, img)
    g_up, g_down, g_left, g_right = halo(rounded)
    taps = tap_grad(up, img, down, left, right, grad_mixed, small, off)
    grad_image = backward(g_up, rounded, g_down, g_left, g_right, depth_kernel, cot)
    flat = reduce_all(jnp.concatenate([grads, taps], axis=0))
    pixels_all = pixels * lax.axis_size("row") * lax.axis_size("col")
    scale = float(pixels_all) ** (-0.5)
    grad_exp, grad_red, grad_taps, vec = final(
        flat, scale, total, hid, channels, depth_kernel.shape[1]
    )
    return (
        jnp.transpose(result, (1, 0, 2)),
        jnp.transpose(grad_image, (1, 0, 2)),
        grad_taps,
        vec[0, :channels],
        vec[0, channels:],
        grad_exp,
        vec[8::8].reshape(hid),
        grad_red,
    )


def solution(mesh):
    in_specs = (
        P("ch", "row", "col"),
        P("ch", None),
        P("ch"),
        P("ch"),
        P(None, "ch"),
        P(),
        P("ch", None),
        P("ch", "row", "col"),
    )
    out_specs = (
        P("ch", "row", "col"),
        P("ch", "row", "col"),
        P("ch", None),
        P("ch"),
        P("ch"),
        P(None, "ch"),
        P("ch"),
        P("ch", None),
    )
    return jax.shard_map(body, mesh=mesh, in_specs=in_specs, out_specs=out_specs, check_vma=False)
```

```python
import functools
import jax
import jax.numpy as jnp
from jax import lax
from jax.experimental import pallas as pl
from jax.experimental.pallas import tpu as pltpu
from jax.sharding import PartitionSpec as P

KSIZE = 7
HALF = 3
SPAN = KSIZE + HALF
epsilon = 1e-06
root_two_pi = 0.7978845608028654
cubic_coef = 0.044715
f32 = jnp.float32
bf16 = jnp.bfloat16
LANES = 128
CT = 16
GAIN = KSIZE * KSIZE
SHIFT = GAIN + 1
OFFSET = GAIN + 2


def vcall(kernel, out_shape, **kw):
    spec = pl.BlockSpec(memory_space=pltpu.VMEM)

    def call(*args):
        return pl.pallas_call(
            kernel,
            out_shape=out_shape,
            in_specs=[spec] * len(args),
            out_specs=jax.tree.map(lambda _: spec, out_shape),
            compiler_params=pltpu.CompilerParams(vmem_limit_bytes=8 << 20),
            **kw,
        )(*args)

    return call


def lane_ids(rows):
    return lax.broadcasted_iota(jnp.int32, (rows, LANES), 1)


def rolled(x, shift):
    shift = shift % LANES
    return x if shift == 0 else pltpu.roll(x, shift, 1)


def split3(x):
    hi = x.astype(bf16)
    rest = x - hi.astype(f32)
    mid = rest.astype(bf16)
    low = (rest - mid.astype(f32)).astype(bf16)
    return [hi.astype(f32), mid.astype(f32), low.astype(f32)]


def gelu_pair(hidden):
    inner = root_two_pi * (hidden + cubic_coef * hidden * hidden * hidden)
    tangent = jnp.tanh(inner)
    value = 0.5 * hidden * (1.0 + tangent)
    slope = 0.5 * (1.0 + tangent) + 0.5 * hidden * (1.0 - tangent * tangent) * root_two_pi * (
        1.0 + 3.0 * cubic_coef * hidden * hidden
    )
    return (value, slope)


def halo_rows(up, mid, down, left, right, at):
    lane = lane_ids(CT)
    l = left[at, :].astype(f32)
    r = right[at, :].astype(f32)
    rows = []
    for i in range(SPAN):
        if i < HALF:
            x = up[i, at, :]
        elif i < SPAN - HALF:
            x = mid[i - HALF, at, :]
        else:
            x = down[i - (SPAN - HALF), at, :]
        edge = jnp.where(
            lane >= 64, rolled(l, LANES - HALF - HALF * i), rolled(r, LANES - HALF * i)
        )
        rows.append((x.astype(f32), edge))
    return rows


def window(row, s):
    x, edge = row
    if s == 0:
        return x
    lane = lane_ids(CT)
    mask = (lane < -s) if s < 0 else (lane >= LANES - s)
    return jnp.where(mask, rolled(edge, -s), rolled(x, -s))


def edges_kernel(up, mid, down, first, last):
    channels = mid.shape[1]
    lane = lane_ids(CT)

    def step(t, carry):
        at = pl.ds(pl.multiple_of(t * CT, CT), CT)
        head = jnp.zeros((CT, LANES), f32)
        tail = jnp.zeros((CT, LANES), f32)
        for i in range(SPAN):
            if i < HALF:
                x = up[i, at, :]
            elif i < SPAN - HALF:
                x = mid[i - HALF, at, :]
            else:
                x = down[i - (SPAN - HALF), at, :]
            x = x.astype(f32)
            mask = (lane >= HALF * i) & (lane < HALF * i + HALF)
            head = jnp.where(mask, rolled(x, HALF * i), head)
            tail = jnp.where(mask, rolled(x, HALF * i + HALF), tail)
        first[at, :] = head.astype(bf16)
        last[at, :] = tail.astype(bf16)
        return carry

    lax.fori_loop(0, channels // CT, step, 0)


def edges(up, mid, down):
    shape = jax.ShapeDtypeStruct((mid.shape[1], LANES), bf16)
    return vcall(edges_kernel, out_shape=(shape, shape), name="edges")(up, mid, down)


def accumulate_taps(rows, kern, at, flip):
    accum = [jnp.zeros((CT, LANES), f32) for _ in range(SPAN - KSIZE + 1)]
    weights = kern[at, :]
    for b in range(KSIZE):
        shifted = [window(row, b - HALF) for row in rows]
        for a in range(KSIZE):
            tap = a * KSIZE + b
            if flip:
                tap = KSIZE * KSIZE - 1 - tap
            w = jnp.broadcast_to(weights[:, tap : tap + 1], (CT, LANES))
            for i in range(len(accum)):
                accum[i] = accum[i] + w * shifted[i + a]
    return accum


def forward_kernel(up, mid, down, left, right, kern, gain, shift, cot, mixed, payload):
    tile_rows, channels, _ = mid.shape

    def step(t, carry):
        at = pl.ds(pl.multiple_of(t * CT, CT), CT)
        rows = halo_rows(up, mid, down, left, right, at)
        accum = accumulate_taps(rows, kern, at, False)
        for i in range(tile_rows):
            mixed[at, i * LANES : (i + 1) * LANES] = accum[i]
        return carry

    lax.fori_loop(0, channels // CT, step, 0)
    pixels = tile_rows * LANES
    for i in range(tile_rows):
        cols = slice(i * LANES, (i + 1) * LANES)
        x = mixed[:, cols]
        mean = jnp.sum(x, axis=0, keepdims=True) / channels
        dev = x - mean
        spread = jnp.sum(dev * dev, axis=0, keepdims=True)
        rows = split3(mean) + split3(spread)
        stats = jnp.concatenate(rows + [jnp.zeros((CT - 6, LANES), f32)], axis=0)
        if i == 0:
            row_id = lax.broadcasted_iota(jnp.int32, (CT, LANES), 0)
            both = jnp.concatenate([gain[...], shift[...]], axis=1)
            for k, part in enumerate(split3(both)):
                stats = jnp.where(row_id == 6 + k, jnp.broadcast_to(part, (CT, LANES)), stats)
        dev = dev.astype(bf16)
        stats = stats.astype(bf16)
        for d in range(payload.shape[0]):
            payload[d, 0:channels, cols] = dev
            payload[d, channels : 2 * channels, cols] = cot[i]
            payload[d, 2 * channels : 2 * channels + CT, cols] = stats


def forward(up, mid, down, left, right, kern, gain, shift, cot, parts):
    tile_rows, channels, _ = mid.shape
    pixels = tile_rows * LANES
    return vcall(
        forward_kernel,
        out_shape=(
            jax.ShapeDtypeStruct((channels, pixels), f32),
            jax.ShapeDtypeStruct((parts, 2 * channels + CT, pixels), bf16),
        ),
        name="forward",
    )(up, mid, down, left, right, kern, gain, shift, cot)


def column(row, n):
    i = lax.broadcasted_iota(jnp.int32, (n, n), 0)
    j = lax.broadcasted_iota(jnp.int32, (n, n), 1)
    return jnp.sum(jnp.where(i == j, jnp.broadcast_to(row, (n, n)), 0.0), axis=1, keepdims=True)


def dot(a, b, dims):
    return lax.dot_general(a, b, (dims, ((), ())), preferred_element_type=f32)


def mlp_kernel(recv, w_exp, bias, w_red, payload, stats_out, grads, off, s_norm, s_act, s_cot, s_gh):
    parts, height, pixels = recv.shape
    ch = (height - CT) // 2
    total = parts * ch
    width = 2 * LANES
    gains, shifts = [], []
    for k in range(parts):
        head = recv[k, 2 * ch : 2 * ch + CT, 0:LANES].astype(f32)
        both = head[6:7] + head[7:8] + head[8:9]
        gains.append(column(both[:, 0:ch], ch))
        shifts.append(column(both[:, ch : 2 * ch], ch))
    bias_col = column(bias[...], bias.shape[1])
    for blk in range(pixels // width):
        cols = slice(blk * width, (blk + 1) * width)
        means, spreads = [], []
        for k in range(parts):
            st = recv[k, 2 * ch : 2 * ch + CT, cols].astype(f32)
            means.append(st[0:1] + st[1:2] + st[2:3])
            spreads.append(st[3:4] + st[4:5] + st[5:6])
        centre = sum(means) / parts
        spread = sum(spreads)
        for k in range(parts):
            gap = means[k] - centre
            spread = spread + ch * gap * gap
        inverse = lax.rsqrt(spread / total + epsilon)
        stats_out[0:1, cols] = centre
        stats_out[1:2, cols] = inverse
        for k in range(parts):
            at = slice(k * ch, (k + 1) * ch)
            dev = recv[k, 0:ch, cols].astype(f32)
            normed = (dev + (means[k] - centre)) * inverse
            s_norm[at, cols] = (normed * gains[k] + shifts[k]).astype(bf16)
            s_cot[at, cols] = recv[k, ch : 2 * ch, cols]
        hidden = dot(w_exp[...], s_norm[:, cols], ((0,), (0,))) + bias_col
        value, slope = gelu_pair(hidden)
        active = value.astype(bf16)
        s_act[:, cols] = active
        gh = (dot(w_red[...], s_cot[:, cols], ((1,), (0,))) * slope).astype(bf16)
        s_gh[:, cols] = gh
        mlp = dot(w_red[...], active, ((0,), (0,)))
        part = dot(w_exp[...], gh, ((1,), (0,)))
        plain = jnp.zeros((1, width), f32)
        cross = jnp.zeros((1, width), f32)
        for k in range(parts):
            at = slice(k * ch, (k + 1) * ch)
            dev = recv[k, 0:ch, cols].astype(f32)
            normed = (dev + (means[k] - centre)) * inverse
            scaled = part[at] * gains[k]
            plain = plain + jnp.sum(scaled, axis=0, keepdims=True)
            cross = cross + jnp.sum(scaled * normed, axis=0, keepdims=True)
            payload[k, 0:ch, cols] = mlp[at].astype(bf16)
            payload[k, ch : 2 * ch, cols] = part[at].astype(bf16)
        sums = jnp.concatenate(
            split3(plain) + split3(cross) + [jnp.zeros((CT - 6, width), f32)], axis=0
        ).astype(bf16)
        for k in range(parts):
            payload[k, 2 * ch : 2 * ch + CT, cols] = sums
    last = ((1,), (1,))
    grad_exp = dot(s_norm[...], s_gh[...], last)
    grad_red = dot(s_act[...], s_cot[...], last)
    n = grad_exp.shape[0]
    grads[0:n, :] = grad_exp[:, 0:LANES]
    grads[n : 2 * n, :] = grad_exp[:, LANES:]
    grads[2 * n : 3 * n, :] = grad_red[:, 0:LANES]
    grads[3 * n : 4 * n, :] = grad_red[:, LANES:]
    sums = dot(s_gh[...], jnp.ones((pixels, LANES), bf16), ((1,), (0,)))
    table = jnp.zeros((ch, LANES), f32)
    lane = lane_ids(ch)
    for j in range(sums.shape[0] // ch):
        table = jnp.where(lane == OFFSET + j, sums[j * ch : (j + 1) * ch], table)
    off[...] = table


def mlp(recv, w_exp, bias, w_red):
    parts, height, pixels = recv.shape
    hid = w_red.shape[0]
    total = w_exp.shape[0]
    return vcall(
        mlp_kernel,
        out_shape=(
            jax.ShapeDtypeStruct(recv.shape, bf16),
            jax.ShapeDtypeStruct((2, pixels), f32),
            jax.ShapeDtypeStruct((4 * total, LANES), f32),
            jax.ShapeDtypeStruct(((recv.shape[1] - CT) // 2, LANES), f32),
        ),
        scratch_shapes=[
            pltpu.VMEM((total, pixels), bf16),
            pltpu.VMEM((hid, pixels), bf16),
            pltpu.VMEM((total, pixels), bf16),
            pltpu.VMEM((hid, pixels), bf16),
        ],
        name="mlp",
    )(recv, w_exp, bias, w_red)


def norm_back_kernel(recv, mixed, stats, gain, image, off, result, grad_mixed, rounded, small):
    parts, height, pixels = recv.shape
    ch = (height - CT) // 2
    tile_rows = image.shape[0]
    total = parts * ch
    gain_col = column(gain[...], ch)
    acc_gain = jnp.zeros((ch, LANES), f32)
    acc_shift = jnp.zeros((ch, LANES), f32)
    for i in range(tile_rows):
        cols = slice(i * LANES, (i + 1) * LANES)
        mlp_out = jnp.zeros((ch, LANES), f32)
        grad = jnp.zeros((ch, LANES), f32)
        sums = jnp.zeros((CT, LANES), f32)
        for k in range(parts):
            mlp_out = mlp_out + recv[k, 0:ch, cols].astype(f32)
            grad = grad + recv[k, ch : 2 * ch, cols].astype(f32)
            sums = sums + recv[k, 2 * ch : 2 * ch + CT, cols].astype(f32)
        result[i] = (image[i].astype(f32) + mlp_out).astype(bf16)
        plain = (sums[0:1] + sums[1:2] + sums[2:3]) / total
        cross = (sums[3:4] + sums[4:5] + sums[5:6]) / total
        inverse = stats[1:2, cols]
        normed = (mixed[:, cols] - stats[0:1, cols]) * inverse
        acc_gain = acc_gain + grad * normed
        acc_shift = acc_shift + grad
        out = inverse * (grad * gain_col - plain - normed * cross)
        grad_mixed[i] = out
        rounded[i] = out.astype(bf16)
    g = jnp.sum(acc_gain, axis=1, keepdims=True)
    s = jnp.sum(acc_shift, axis=1, keepdims=True)
    lane = lane_ids(ch)
    small[...] = jnp.where(lane == GAIN, g, jnp.where(lane == SHIFT, s, off[...]))


def norm_back(recv, mixed, stats, gain, image, off):
    tile_rows, channels, _ = image.shape
    return vcall(
        norm_back_kernel,
        out_shape=(
            jax.ShapeDtypeStruct(image.shape, bf16),
            jax.ShapeDtypeStruct(image.shape, f32),
            jax.ShapeDtypeStruct(image.shape, bf16),
            jax.ShapeDtypeStruct((channels, LANES), f32),
        ),
        name="norm_back",
    )(recv, mixed, stats, gain, image, off)


def tap_grad_kernel(up, mid, down, left, right, grad_mixed, small, out, table_ref):
    tile_rows, channels, _ = mid.shape
    lane = lane_ids(CT)

    def step(t, carry):
        at = pl.ds(pl.multiple_of(t * CT, CT), CT)
        rows = halo_rows(up, mid, down, left, right, at)
        grads = [grad_mixed[i, at, :] for i in range(tile_rows)]
        table = small[at, :]
        for b in range(KSIZE):
            shifted = [window(row, b - HALF) for row in rows]
            for a in range(KSIZE):
                accum = grads[0] * shifted[a]
                for i in range(1, tile_rows):
                    accum = accum + grads[i] * shifted[a + i]
                value = jnp.sum(accum, axis=1, keepdims=True)
                table = jnp.where(lane == a * KSIZE + b, value, table)
        table_ref[at, :] = table
        return carry

    lax.fori_loop(0, channels // CT, step, 0)
    half = channels // 2
    out[...] = table_ref[0:half, :] + rolled(table_ref[half:channels, :], LANES // 2)


def tap_grad(up, mid, down, left, right, grad_mixed, small):
    channels = mid.shape[1]
    return vcall(
        tap_grad_kernel,
        out_shape=jax.ShapeDtypeStruct((channels // 2, LANES), f32),
        scratch_shapes=[pltpu.VMEM((channels, LANES), f32)],
        name="tap_grad",
    )(up, mid, down, left, right, grad_mixed, small)


def backward_kernel(up, mid, down, left, right, kern, cot, out):
    tile_rows, channels, _ = mid.shape

    def step(t, carry):
        at = pl.ds(pl.multiple_of(t * CT, CT), CT)
        rows = halo_rows(up, mid, down, left, right, at)
        accum = accumulate_taps(rows, kern, at, True)
        for i in range(tile_rows):
            out[i, at, :] = (cot[i, at, :].astype(f32) + accum[i]).astype(bf16)
        return carry

    lax.fori_loop(0, channels // CT, step, 0)


def backward(up, mid, down, left, right, kern, cot):
    return vcall(
        backward_kernel,
        out_shape=jax.ShapeDtypeStruct(cot.shape, bf16),
        name="backward",
    )(up, mid, down, left, right, kern, cot)


def gather_kernel(recv, out):
    cols = recv.shape[0]
    total = recv[0]
    for c in range(1, cols):
        total = total + recv[c]
    n = total.shape[0] // 2
    big, tail = total[0:n], total[n:]
    hi = tail.astype(bf16).astype(f32)
    low = tail - hi
    row = lax.broadcasted_iota(jnp.int32, tail.shape, 0)
    extra = jnp.where(row < n // 2, hi, jnp.roll(low, n // 2, 0))
    tile = jnp.concatenate([big, extra], axis=0).astype(bf16)
    for c in range(cols):
        out[c] = tile


def gather_sum(recv):
    return vcall(gather_kernel, out_shape=jax.ShapeDtypeStruct(recv.shape, bf16), name="gather_sum")(
        recv
    )


def final_kernel(scale, flat, exp_ref, red_ref, taps_ref, gain_ref, shift_ref, off_ref, small):
    rows, cols, height, _ = flat.shape
    n = exp_ref.shape[0]
    part = height // 2
    per = small.shape[0] // cols
    for r in range(rows):
        x = flat[r].astype(f32)
        block = x[:, 0:part, :].reshape(cols * part, LANES) * scale
        start = r * cols * part
        lo = 0
        while lo < cols * part:
            which, at = divmod(start + lo, n)
            size = min(cols * part - lo, n - at)
            ref = (exp_ref, red_ref)[which // 2]
            lane = (which % 2) * LANES
            ref[at : at + size, lane : lane + LANES] = block[lo : lo + size]
            lo += size
    sums = flat[0].astype(f32)[:, part:, :]
    for r in range(1, rows):
        sums = sums + flat[r].astype(f32)[:, part:, :]
    for c in range(cols):
        x = sums[c]
        small[c * per : (c + 1) * per, :] = x[0:per] + x[part // 2 : part // 2 + per]
    x = small[...] * scale
    both = jnp.concatenate([x, rolled(x, LANES // 2)], axis=0)
    wide = jnp.concatenate([both, jnp.zeros((LANES - both.shape[0], LANES), f32)], axis=0)
    flip = jnp.transpose(wide)[:, 0 : both.shape[0]]
    taps_ref[...] = flip[0 : taps_ref.shape[0], :]
    gain_ref[...] = flip[GAIN : GAIN + 1]
    shift_ref[...] = flip[SHIFT : SHIFT + 1]
    channels = flip.shape[1]
    for j in range(off_ref.shape[1] // channels):
        off_ref[:, j * channels : (j + 1) * channels] = flip[OFFSET + j : OFFSET + j + 1]


def final(flat, scale, total, hid, channels, taps):
    return vcall(
        functools.partial(final_kernel, scale),
        out_shape=(
            jax.ShapeDtypeStruct((total, hid), f32),
            jax.ShapeDtypeStruct((hid, total), f32),
            jax.ShapeDtypeStruct((taps, channels), f32),
            jax.ShapeDtypeStruct((1, channels), f32),
            jax.ShapeDtypeStruct((1, channels), f32),
            jax.ShapeDtypeStruct((1, hid), f32),
        ),
        scratch_shapes=[pltpu.VMEM((channels // 2, LANES), f32)],
        name="final",
    )(flat)


def neighbours(first, last, axis):
    size = lax.axis_size(axis)
    up = [(i, i + 1) for i in range(size - 1)]
    down = [(j, i) for i, j in up]
    return lax.ppermute(last, axis, up), lax.ppermute(first, axis, down)


def halo(x):
    rows = x.shape[0]
    up, down = neighbours(x[:HALF], x[rows - HALF :], "row")
    first, last = edges(up, x, down)
    left, right = neighbours(first, last, "col")
    return up, down, left, right


def row_sum(grads):
    rows = lax.axis_size("row")
    part = grads.reshape(rows, grads.shape[0] // rows, LANES)
    return lax.all_to_all(part, "row", 0, 0).sum(0)


def col_sum(part, taps):
    rows, cols = lax.axis_size("row"), lax.axis_size("col")
    part = part.reshape(cols, part.shape[0] // cols, LANES)
    taps = taps.reshape(cols, taps.shape[0] // cols, LANES)
    pad = jnp.zeros((cols, part.shape[1] - taps.shape[1], LANES), f32)
    part = lax.all_to_all(jnp.concatenate([part, taps, pad], axis=1), "col", 0, 0)
    part = lax.all_to_all(gather_sum(part), "col", 0, 0)
    return lax.all_gather(part, "row", axis=0)


def body(
    image, depth_kernel, norm_gain, norm_shift, expand_weight, expand_bias, reduce_weight, cotangent
):
    channels, tile_rows, tile_cols = image.shape
    pixels = tile_rows * tile_cols
    parts = lax.axis_size("ch")
    hid = reduce_weight.shape[0]
    total = expand_weight.shape[0]
    img = jnp.transpose(image, (1, 0, 2))
    cot = jnp.transpose(cotangent, (1, 0, 2))
    gain = norm_gain.reshape(1, channels)
    shift = norm_shift.reshape(1, channels)
    bias = lax.dynamic_slice_in_dim(expand_bias, lax.axis_index("ch") * hid, hid).reshape(1, hid)
    up, down, left, right = halo(img)
    mixed, send = forward(up, img, down, left, right, depth_kernel, gain, shift, cot, parts)
    recv = lax.all_to_all(send, "ch", 0, 0)
    send, stats, grads, off = mlp(recv, expand_weight, bias, reduce_weight)
    recv = lax.all_to_all(send, "ch", 0, 0)
    part = row_sum(grads)
    result, grad_mixed, rounded, small = norm_back(recv, mixed, stats, gain, img, off)
    g_up, g_down, g_left, g_right = halo(rounded)
    taps = tap_grad(up, img, down, left, right, grad_mixed, small)
    grad_image = backward(g_up, rounded, g_down, g_left, g_right, depth_kernel, cot)
    flat = col_sum(part, taps)
    pixels_all = pixels * lax.axis_size("row") * lax.axis_size("col")
    scale = float(pixels_all) ** (-0.5)
    grad_exp, grad_red, grad_taps, grad_gain, grad_shift, grad_off = final(
        flat, scale, total, hid, channels, depth_kernel.shape[1]
    )
    return (
        jnp.transpose(result, (1, 0, 2)),
        jnp.transpose(grad_image, (1, 0, 2)),
        jnp.transpose(grad_taps),
        grad_gain.reshape(channels),
        grad_shift.reshape(channels),
        grad_exp,
        grad_off.reshape(hid),
        grad_red,
    )


def solution(mesh):
    in_specs = (
        P("ch", "row", "col"),
        P("ch", None),
        P("ch"),
        P("ch"),
        P(None, "ch"),
        P(),
        P("ch", None),
        P("ch", "row", "col"),
    )
    out_specs = (
        P("ch", "row", "col"),
        P("ch", "row", "col"),
        P("ch", None),
        P("ch"),
        P("ch"),
        P(None, "ch"),
        P("ch"),
        P("ch", None),
    )
    return jax.shard_map(body, mesh=mesh, in_specs=in_specs, out_specs=out_specs, check_vma=False)
```

```python
import functools
import jax
import jax.numpy as jnp
from jax import lax
from jax.experimental import pallas as pl
from jax.experimental.pallas import tpu as pltpu
from jax.sharding import PartitionSpec as P

KSIZE = 7
HALF = 3
SPAN = KSIZE + HALF
epsilon = 1e-06
root_two_pi = 0.7978845608028654
cubic_coef = 0.044715
f32 = jnp.float32
bf16 = jnp.bfloat16
LANES = 128
CT = 16
GAIN = KSIZE * KSIZE
SHIFT = GAIN + 1
OFFSET = GAIN + 2


def vcall(kernel, out_shape, **kw):
    spec = pl.BlockSpec(memory_space=pltpu.VMEM)

    def call(*args):
        return pl.pallas_call(
            kernel,
            out_shape=out_shape,
            in_specs=[spec] * len(args),
            out_specs=jax.tree.map(lambda _: spec, out_shape),
            compiler_params=pltpu.CompilerParams(vmem_limit_bytes=8 << 20),
            **kw,
        )(*args)

    return call


def lane_ids(rows):
    return lax.broadcasted_iota(jnp.int32, (rows, LANES), 1)


def rolled(x, shift):
    shift = shift % LANES
    return x if shift == 0 else pltpu.roll(x, shift, 1)


def split3(x):
    hi = x.astype(bf16)
    rest = x - hi.astype(f32)
    mid = rest.astype(bf16)
    low = (rest - mid.astype(f32)).astype(bf16)
    return [hi.astype(f32), mid.astype(f32), low.astype(f32)]


def gelu_pair(hidden):
    inner = root_two_pi * (hidden + cubic_coef * hidden * hidden * hidden)
    tangent = jnp.tanh(inner)
    value = 0.5 * hidden * (1.0 + tangent)
    slope = 0.5 * (1.0 + tangent) + 0.5 * hidden * (1.0 - tangent * tangent) * root_two_pi * (
        1.0 + 3.0 * cubic_coef * hidden * hidden
    )
    return (value, slope)


def halo_rows(up, mid, down, left, right, at):
    lane = lane_ids(CT)
    l = left[at, :].astype(f32)
    r = right[at, :].astype(f32)
    rows = []
    for i in range(SPAN):
        if i < HALF:
            x = up[i, at, :]
        elif i < SPAN - HALF:
            x = mid[i - HALF, at, :]
        else:
            x = down[i - (SPAN - HALF), at, :]
        edge = jnp.where(
            lane >= 64, rolled(l, LANES - HALF - HALF * i), rolled(r, LANES - HALF * i)
        )
        rows.append((x.astype(f32), edge))
    return rows


def window(row, s):
    x, edge = row
    if s == 0:
        return x
    lane = lane_ids(CT)
    mask = (lane < -s) if s < 0 else (lane >= LANES - s)
    return jnp.where(mask, rolled(edge, -s), rolled(x, -s))


def edges_kernel(up, mid, down, first, last):
    channels = mid.shape[1]
    lane = lane_ids(CT)

    def step(t, carry):
        at = pl.ds(pl.multiple_of(t * CT, CT), CT)
        head = jnp.zeros((CT, LANES), f32)
        tail = jnp.zeros((CT, LANES), f32)
        for i in range(SPAN):
            if i < HALF:
                x = up[i, at, :]
            elif i < SPAN - HALF:
                x = mid[i - HALF, at, :]
            else:
                x = down[i - (SPAN - HALF), at, :]
            x = x.astype(f32)
            mask = (lane >= HALF * i) & (lane < HALF * i + HALF)
            head = jnp.where(mask, rolled(x, HALF * i), head)
            tail = jnp.where(mask, rolled(x, HALF * i + HALF), tail)
        first[at, :] = head.astype(bf16)
        last[at, :] = tail.astype(bf16)
        return carry

    lax.fori_loop(0, channels // CT, step, 0)


def edges(up, mid, down):
    shape = jax.ShapeDtypeStruct((mid.shape[1], LANES), bf16)
    return vcall(edges_kernel, out_shape=(shape, shape), name="edges")(up, mid, down)


def accumulate_taps(rows, kern, at, flip):
    accum = [jnp.zeros((CT, LANES), f32) for _ in range(SPAN - KSIZE + 1)]
    weights = kern[at, :]
    for b in range(KSIZE):
        shifted = [window(row, b - HALF) for row in rows]
        for a in range(KSIZE):
            tap = a * KSIZE + b
            if flip:
                tap = KSIZE * KSIZE - 1 - tap
            w = jnp.broadcast_to(weights[:, tap : tap + 1], (CT, LANES))
            for i in range(len(accum)):
                accum[i] = accum[i] + w * shifted[i + a]
    return accum


def forward_kernel(up, mid, down, left, right, kern, gain, shift, cot, mixed, payload):
    tile_rows, channels, _ = mid.shape

    def step(t, carry):
        at = pl.ds(pl.multiple_of(t * CT, CT), CT)
        rows = halo_rows(up, mid, down, left, right, at)
        accum = accumulate_taps(rows, kern, at, False)
        for i in range(tile_rows):
            mixed[at, i * LANES : (i + 1) * LANES] = accum[i]
        return carry

    lax.fori_loop(0, channels // CT, step, 0)
    for i in range(tile_rows):
        cols = slice(i * LANES, (i + 1) * LANES)
        x = mixed[:, cols]
        mean = jnp.sum(x, axis=0, keepdims=True) / channels
        dev = x - mean
        spread = jnp.sum(dev * dev, axis=0, keepdims=True)
        rows = split3(mean) + split3(spread)
        stats = jnp.concatenate(rows + [jnp.zeros((CT - 6, LANES), f32)], axis=0)
        if i == 0:
            row_id = lax.broadcasted_iota(jnp.int32, (CT, LANES), 0)
            both = jnp.concatenate([gain[...], shift[...]], axis=1)
            for k, part in enumerate(split3(both)):
                stats = jnp.where(row_id == 6 + k, jnp.broadcast_to(part, (CT, LANES)), stats)
        dev = dev.astype(bf16)
        stats = stats.astype(bf16)
        for d in range(payload.shape[0]):
            payload[d, 0:channels, cols] = dev
            payload[d, channels : 2 * channels, cols] = cot[i]
            payload[d, 2 * channels : 2 * channels + CT, cols] = stats


def forward(up, mid, down, left, right, kern, gain, shift, cot, parts):
    tile_rows, channels, _ = mid.shape
    pixels = tile_rows * LANES
    return vcall(
        forward_kernel,
        out_shape=(
            jax.ShapeDtypeStruct((channels, pixels), f32),
            jax.ShapeDtypeStruct((parts, 2 * channels + CT, pixels), bf16),
        ),
        name="forward",
    )(up, mid, down, left, right, kern, gain, shift, cot)


def column(row, n):
    i = lax.broadcasted_iota(jnp.int32, (n, n), 0)
    j = lax.broadcasted_iota(jnp.int32, (n, n), 1)
    return jnp.sum(jnp.where(i == j, jnp.broadcast_to(row, (n, n)), 0.0), axis=1, keepdims=True)


def dot(a, b, dims):
    return lax.dot_general(a, b, (dims, ((), ())), preferred_element_type=f32)


def row_masks(size):
    return {8: (1, 2, 6), 4: (1, 2), 2: (1,)}[size]


def row_bits(r, size):
    if size == 8:
        return (r % 2, (r // 2 + r // 4) % 2, r // 4)
    return (r % 2, r // 2)[: size.bit_length() - 1]


def row_chunk(r, size):
    chunk = 0
    for bit in row_bits(r, size):
        chunk = 2 * chunk + bit
    return chunk


def row_bit(step):
    return row_bits(lax.axis_index("row"), lax.axis_size("row"))[step]


def halves(ref, step, send, keep):
    n = send.shape[0]
    bit = row_bit(step)
    send[...] = ref[pl.ds(pl.multiple_of((1 - bit) * n, n), n), :]
    keep[...] = ref[pl.ds(pl.multiple_of(bit * n, n), n), :]


def halve_kernel(step, x, recv, send, keep, total):
    total[...] = x[...] + recv[...]
    halves(total, step, send, keep)


def halve(step, x, recv, name):
    shape = jax.ShapeDtypeStruct((x.shape[0] // 2, LANES), f32)
    return vcall(
        functools.partial(halve_kernel, step),
        out_shape=(shape, shape),
        scratch_shapes=[pltpu.VMEM(x.shape, f32)],
        name=name,
    )(x, recv)


def reduce_rows(send, keep):
    size = lax.axis_size("row")
    for step, mask in enumerate(row_masks(size)):
        recv = lax.ppermute(send, "row", [(i, i ^ mask) for i in range(size)])
        if step + 1 < len(row_masks(size)):
            send, keep = halve(step + 1, keep, recv, "halve")
    return keep, recv


def mlp_kernel(recv, w_exp, bias, w_red, payload, stats_out, send, keep, off, grads, s_norm, s_act, s_cot, s_gh):
    parts, height, pixels = recv.shape
    ch = (height - CT) // 2
    total = parts * ch
    width = 2 * LANES
    gains, shifts = [], []
    for k in range(parts):
        head = recv[k, 2 * ch : 2 * ch + CT, 0:LANES].astype(f32)
        both = head[6:7] + head[7:8] + head[8:9]
        gains.append(column(both[:, 0:ch], ch))
        shifts.append(column(both[:, ch : 2 * ch], ch))
    bias_col = column(bias[...], bias.shape[1])
    for blk in range(pixels // width):
        cols = slice(blk * width, (blk + 1) * width)
        means, spreads = [], []
        for k in range(parts):
            st = recv[k, 2 * ch : 2 * ch + CT, cols].astype(f32)
            means.append(st[0:1] + st[1:2] + st[2:3])
            spreads.append(st[3:4] + st[4:5] + st[5:6])
        centre = sum(means) / parts
        spread = sum(spreads)
        for k in range(parts):
            gap = means[k] - centre
            spread = spread + ch * gap * gap
        inverse = lax.rsqrt(spread / total + epsilon)
        stats_out[0:1, cols] = centre
        stats_out[1:2, cols] = inverse
        for k in range(parts):
            at = slice(k * ch, (k + 1) * ch)
            dev = recv[k, 0:ch, cols].astype(f32)
            normed = (dev + (means[k] - centre)) * inverse
            s_norm[at, cols] = (normed * gains[k] + shifts[k]).astype(bf16)
            s_cot[at, cols] = recv[k, ch : 2 * ch, cols]
        hidden = dot(w_exp[...], s_norm[:, cols], ((0,), (0,))) + bias_col
        value, slope = gelu_pair(hidden)
        active = value.astype(bf16)
        s_act[:, cols] = active
        gh = (dot(w_red[...], s_cot[:, cols], ((1,), (0,))) * slope).astype(bf16)
        s_gh[:, cols] = gh
        mlp = dot(w_red[...], active, ((0,), (0,)))
        part = dot(w_exp[...], gh, ((1,), (0,)))
        plain = jnp.zeros((1, width), f32)
        cross = jnp.zeros((1, width), f32)
        for k in range(parts):
            at = slice(k * ch, (k + 1) * ch)
            dev = recv[k, 0:ch, cols].astype(f32)
            normed = (dev + (means[k] - centre)) * inverse
            scaled = part[at] * gains[k]
            plain = plain + jnp.sum(scaled, axis=0, keepdims=True)
            cross = cross + jnp.sum(scaled * normed, axis=0, keepdims=True)
            payload[k, 0:ch, cols] = mlp[at].astype(bf16)
            payload[k, ch : 2 * ch, cols] = part[at].astype(bf16)
        sums = jnp.concatenate(
            split3(plain) + split3(cross) + [jnp.zeros((CT - 6, width), f32)], axis=0
        ).astype(bf16)
        for k in range(parts):
            payload[k, 2 * ch : 2 * ch + CT, cols] = sums
    last = ((1,), (1,))
    grad_exp = dot(s_norm[...], s_gh[...], last)
    grad_red = dot(s_act[...], s_cot[...], last)
    n = grad_exp.shape[0]
    grads[0:n, :] = grad_exp[:, 0:LANES]
    grads[n : 2 * n, :] = grad_exp[:, LANES:]
    grads[2 * n : 3 * n, :] = grad_red[:, 0:LANES]
    grads[3 * n : 4 * n, :] = grad_red[:, LANES:]
    halves(grads, 0, send, keep)
    sums = dot(s_gh[...], jnp.ones((pixels, LANES), bf16), ((1,), (0,)))
    table = jnp.zeros((ch, LANES), f32)
    lane = lane_ids(ch)
    for j in range(sums.shape[0] // ch):
        table = jnp.where(lane == OFFSET + j, sums[j * ch : (j + 1) * ch], table)
    off[...] = table


def mlp(recv, w_exp, bias, w_red):
    _, _, pixels = recv.shape
    hid = w_red.shape[0]
    total = w_exp.shape[0]
    return vcall(
        mlp_kernel,
        out_shape=(
            jax.ShapeDtypeStruct(recv.shape, bf16),
            jax.ShapeDtypeStruct((2, pixels), f32),
            jax.ShapeDtypeStruct((2 * total, LANES), f32),
            jax.ShapeDtypeStruct((2 * total, LANES), f32),
            jax.ShapeDtypeStruct(((recv.shape[1] - CT) // 2, LANES), f32),
        ),
        scratch_shapes=[
            pltpu.VMEM((4 * total, LANES), f32),
            pltpu.VMEM((total, pixels), bf16),
            pltpu.VMEM((hid, pixels), bf16),
            pltpu.VMEM((total, pixels), bf16),
            pltpu.VMEM((hid, pixels), bf16),
        ],
        name="mlp",
    )(recv, w_exp, bias, w_red)


def norm_back_kernel(recv, mixed, stats, gain, image, off, result, grad_mixed, rounded, small):
    parts, height, _ = recv.shape
    ch = (height - CT) // 2
    tile_rows = image.shape[0]
    total = parts * ch
    gain_col = column(gain[...], ch)
    acc_gain = jnp.zeros((ch, LANES), f32)
    acc_shift = jnp.zeros((ch, LANES), f32)
    for i in range(tile_rows):
        cols = slice(i * LANES, (i + 1) * LANES)
        mlp_out = jnp.zeros((ch, LANES), f32)
        grad = jnp.zeros((ch, LANES), f32)
        sums = jnp.zeros((CT, LANES), f32)
        for k in range(parts):
            mlp_out = mlp_out + recv[k, 0:ch, cols].astype(f32)
            grad = grad + recv[k, ch : 2 * ch, cols].astype(f32)
            sums = sums + recv[k, 2 * ch : 2 * ch + CT, cols].astype(f32)
        result[i] = (image[i].astype(f32) + mlp_out).astype(bf16)
        plain = (sums[0:1] + sums[1:2] + sums[2:3]) / total
        cross = (sums[3:4] + sums[4:5] + sums[5:6]) / total
        inverse = stats[1:2, cols]
        normed = (mixed[:, cols] - stats[0:1, cols]) * inverse
        acc_gain = acc_gain + grad * normed
        acc_shift = acc_shift + grad
        out = inverse * (grad * gain_col - plain - normed * cross)
        grad_mixed[i] = out
        rounded[i] = out.astype(bf16)
    g = jnp.sum(acc_gain, axis=1, keepdims=True)
    s = jnp.sum(acc_shift, axis=1, keepdims=True)
    lane = lane_ids(ch)
    small[...] = jnp.where(lane == GAIN, g, jnp.where(lane == SHIFT, s, off[...]))


def norm_back(recv, mixed, stats, gain, image, off):
    _, channels, _ = image.shape
    return vcall(
        norm_back_kernel,
        out_shape=(
            jax.ShapeDtypeStruct(image.shape, bf16),
            jax.ShapeDtypeStruct(image.shape, f32),
            jax.ShapeDtypeStruct(image.shape, bf16),
            jax.ShapeDtypeStruct((channels, LANES), f32),
        ),
        name="norm_back",
    )(recv, mixed, stats, gain, image, off)


def tap_grad_kernel(up, mid, down, left, right, grad_mixed, small, send, keep, table_ref, total):
    tile_rows, channels, _ = mid.shape
    lane = lane_ids(CT)

    def step(t, carry):
        at = pl.ds(pl.multiple_of(t * CT, CT), CT)
        rows = halo_rows(up, mid, down, left, right, at)
        grads = [grad_mixed[i, at, :] for i in range(tile_rows)]
        table = small[at, :]
        for b in range(KSIZE):
            shifted = [window(row, b - HALF) for row in rows]
            for a in range(KSIZE):
                accum = grads[0] * shifted[a]
                for i in range(1, tile_rows):
                    accum = accum + grads[i] * shifted[a + i]
                value = jnp.sum(accum, axis=1, keepdims=True)
                table = jnp.where(lane == a * KSIZE + b, value, table)
        table_ref[at, :] = table
        return carry

    lax.fori_loop(0, channels // CT, step, 0)
    half = channels // 2
    total[...] = table_ref[0:half, :] + rolled(table_ref[half:channels, :], LANES // 2)
    halves(total, 0, send, keep)


def tap_grad(up, mid, down, left, right, grad_mixed, small):
    channels = mid.shape[1]
    shape = jax.ShapeDtypeStruct((channels // 4, LANES), f32)
    return vcall(
        tap_grad_kernel,
        out_shape=(shape, shape),
        scratch_shapes=[pltpu.VMEM((channels, LANES), f32), pltpu.VMEM((channels // 2, LANES), f32)],
        name="tap_grad",
    )(up, mid, down, left, right, grad_mixed, small)


def backward_kernel(up, mid, down, left, right, kern, cot, out):
    tile_rows, channels, _ = mid.shape

    def step(t, carry):
        at = pl.ds(pl.multiple_of(t * CT, CT), CT)
        rows = halo_rows(up, mid, down, left, right, at)
        accum = accumulate_taps(rows, kern, at, True)
        for i in range(tile_rows):
            out[i, at, :] = (cot[i, at, :].astype(f32) + accum[i]).astype(bf16)
        return carry

    lax.fori_loop(0, channels // CT, step, 0)


def backward(up, mid, down, left, right, kern, cot):
    return vcall(
        backward_kernel,
        out_shape=jax.ShapeDtypeStruct(cot.shape, bf16),
        name="backward",
    )(up, mid, down, left, right, kern, cot)


def hi_lo(x):
    hi = x.astype(bf16).astype(f32)
    return jnp.concatenate([hi, x - hi], axis=0)


def col_pack_kernel(big, small, more, out):
    total = big[0]
    for c in range(1, big.shape[0]):
        total = total + big[c]
    tail = small[...] + more[...]
    tile = jnp.concatenate([total, hi_lo(tail)], axis=0).astype(bf16)
    for c in range(out.shape[0]):
        out[c] = tile


def col_pack(big, small, more):
    cols, part, _ = big.shape
    shape = (cols, part + 2 * small.shape[0], LANES)
    return vcall(col_pack_kernel, out_shape=jax.ShapeDtypeStruct(shape, bf16), name="col_pack")(
        big, small, more
    )


def row_pack_kernel(per, recv, out):
    cols, height, _ = recv.shape
    part = height - 2 * per
    x = recv[...].astype(f32)
    big = x[:, 0:part, :].reshape(cols * part, LANES)
    tail = x[0, part:, :]
    for c in range(1, cols):
        tail = tail + x[c, part:, :]
    extra = hi_lo(tail[0:per] + tail[per:])
    pad = jnp.zeros((CT - 2 * per % CT, LANES), f32) if 2 * per % CT else None
    pieces = [big, extra] if pad is None else [big, extra, pad]
    tile = jnp.concatenate(pieces, axis=0).astype(bf16)
    for r in range(out.shape[0]):
        out[r] = tile


def row_pack(recv, rows, per):
    cols, height, _ = recv.shape
    tall = cols * (height - 2 * per) + -(-2 * per // CT) * CT
    return vcall(
        functools.partial(row_pack_kernel, per),
        out_shape=jax.ShapeDtypeStruct((rows, tall, LANES), bf16),
        name="row_pack",
    )(recv)


def final_kernel(scale, flat, exp_ref, red_ref, taps_ref, gain_ref, shift_ref, off_ref, small):
    rows = flat.shape[0]
    n = exp_ref.shape[0]
    per = small.shape[0] // rows
    size_all = 4 * n // rows
    for r in range(rows):
        x = flat[r].astype(f32) * scale
        block = x[0:size_all]
        tail = x[size_all : size_all + per] + x[size_all + per : size_all + 2 * per]
        chunk = row_chunk(r, rows)
        small[chunk * per : (chunk + 1) * per, :] = tail
        start = chunk * size_all
        lo = 0
        while lo < size_all:
            which, at = divmod(start + lo, n)
            size = min(size_all - lo, n - at)
            ref = (exp_ref, red_ref)[which // 2]
            lane = (which % 2) * LANES
            ref[at : at + size, lane : lane + LANES] = block[lo : lo + size]
            lo += size
    x = small[...]
    both = jnp.concatenate([x, rolled(x, LANES // 2)], axis=0)
    wide = jnp.concatenate([both, jnp.zeros((LANES - both.shape[0], LANES), f32)], axis=0)
    flip = jnp.transpose(wide)[:, 0 : both.shape[0]]
    taps_ref[...] = flip[0 : taps_ref.shape[0], :]
    gain_ref[...] = flip[GAIN : GAIN + 1]
    shift_ref[...] = flip[SHIFT : SHIFT + 1]
    channels = flip.shape[1]
    for j in range(off_ref.shape[1] // channels):
        off_ref[:, j * channels : (j + 1) * channels] = flip[OFFSET + j : OFFSET + j + 1]


def final(flat, scale, total, hid, channels, taps):
    return vcall(
        functools.partial(final_kernel, scale),
        out_shape=(
            jax.ShapeDtypeStruct((total, hid), f32),
            jax.ShapeDtypeStruct((hid, total), f32),
            jax.ShapeDtypeStruct((taps, channels), f32),
            jax.ShapeDtypeStruct((1, channels), f32),
            jax.ShapeDtypeStruct((1, channels), f32),
            jax.ShapeDtypeStruct((1, hid), f32),
        ),
        scratch_shapes=[pltpu.VMEM((channels // 2, LANES), f32)],
        name="final",
    )(flat)


def neighbours(first, last, axis):
    size = lax.axis_size(axis)
    up = [(i, i + 1) for i in range(size - 1)]
    down = [(j, i) for i, j in up]
    return lax.ppermute(last, axis, up), lax.ppermute(first, axis, down)


def halo(x):
    rows = x.shape[0]
    up, down = neighbours(x[:HALF], x[rows - HALF :], "row")
    first, last = edges(up, x, down)
    left, right = neighbours(first, last, "col")
    return up, down, left, right


def exchange(x, axis):
    return lax.all_to_all(x, axis, 0, 0)


def reduce_big(send, keep):
    cols = lax.axis_size("col")
    keep, recv = reduce_rows(send, keep)
    part = keep + recv
    return exchange(part.reshape(cols, part.shape[0] // cols, LANES), "col")


def reduce_rest(big, send, keep):
    keep, recv = reduce_rows(send, keep)
    flat = exchange(col_pack(big, keep, recv), "col")
    return exchange(row_pack(flat, lax.axis_size("row"), keep.shape[0]), "row")


def body(
    image, depth_kernel, norm_gain, norm_shift, expand_weight, expand_bias, reduce_weight, cotangent
):
    channels, tile_rows, tile_cols = image.shape
    pixels = tile_rows * tile_cols
    parts = lax.axis_size("ch")
    hid = reduce_weight.shape[0]
    total = expand_weight.shape[0]
    img = jnp.transpose(image, (1, 0, 2))
    cot = jnp.transpose(cotangent, (1, 0, 2))
    gain = norm_gain.reshape(1, channels)
    shift = norm_shift.reshape(1, channels)
    bias = lax.dynamic_slice_in_dim(expand_bias, lax.axis_index("ch") * hid, hid).reshape(1, hid)
    up, down, left, right = halo(img)
    mixed, send = forward(up, img, down, left, right, depth_kernel, gain, shift, cot, parts)
    recv = exchange(send, "ch")
    send, stats, give, keep, off = mlp(recv, expand_weight, bias, reduce_weight)
    recv = exchange(send, "ch")
    big = reduce_big(give, keep)
    result, grad_mixed, rounded, small = norm_back(recv, mixed, stats, gain, img, off)
    g_up, g_down, g_left, g_right = halo(rounded)
    give, keep = tap_grad(up, img, down, left, right, grad_mixed, small)
    grad_image = backward(g_up, rounded, g_down, g_left, g_right, depth_kernel, cot)
    flat = reduce_rest(big, give, keep)
    pixels_all = pixels * lax.axis_size("row") * lax.axis_size("col")
    scale = float(pixels_all) ** (-0.5)
    grad_exp, grad_red, grad_taps, grad_gain, grad_shift, grad_off = final(
        flat, scale, total, hid, channels, depth_kernel.shape[1]
    )
    return (
        jnp.transpose(result, (1, 0, 2)),
        jnp.transpose(grad_image, (1, 0, 2)),
        jnp.transpose(grad_taps),
        grad_gain.reshape(channels),
        grad_shift.reshape(channels),
        grad_exp,
        grad_off.reshape(hid),
        grad_red,
    )


def solution(mesh):
    in_specs = (
        P("ch", "row", "col"),
        P("ch", None),
        P("ch"),
        P("ch"),
        P(None, "ch"),
        P(),
        P("ch", None),
        P("ch", "row", "col"),
    )
    out_specs = (
        P("ch", "row", "col"),
        P("ch", "row", "col"),
        P("ch", None),
        P("ch"),
        P("ch"),
        P(None, "ch"),
        P("ch"),
        P("ch", None),
    )

    return jax.shard_map(body, mesh=mesh, in_specs=in_specs, out_specs=out_specs, check_vma=False)
```

```python
import functools
import jax
import jax.numpy as jnp
from jax import lax
from jax.experimental import pallas as pl
from jax.experimental.pallas import tpu as pltpu
from jax.sharding import PartitionSpec as P

KSIZE = 7
HALF = 3
SPAN = KSIZE + HALF
epsilon = 1e-06
root_two_pi = 0.7978845608028654
cubic_coef = 0.044715
f32 = jnp.float32
bf16 = jnp.bfloat16
LANES = 128
CT = 16
GAIN = KSIZE * KSIZE
SHIFT = GAIN + 1
OFFSET = GAIN + 2


def vcall(kernel, out_shape, **kw):
    spec = pl.BlockSpec(memory_space=pltpu.VMEM)

    def call(*args):
        return pl.pallas_call(
            kernel,
            out_shape=out_shape,
            in_specs=[spec] * len(args),
            out_specs=jax.tree.map(lambda _: spec, out_shape),
            compiler_params=pltpu.CompilerParams(vmem_limit_bytes=8 << 20),
            **kw,
        )(*args)

    return call


def lane_ids(rows):
    return lax.broadcasted_iota(jnp.int32, (rows, LANES), 1)


def rolled(x, shift):
    shift = shift % LANES
    return x if shift == 0 else pltpu.roll(x, shift, 1)


def split3(x):
    hi = x.astype(bf16)
    rest = x - hi.astype(f32)
    mid = rest.astype(bf16)
    low = (rest - mid.astype(f32)).astype(bf16)
    return [hi.astype(f32), mid.astype(f32), low.astype(f32)]


def gelu_pair(hidden):
    inner = root_two_pi * (hidden + cubic_coef * hidden * hidden * hidden)
    tangent = jnp.tanh(inner)
    value = 0.5 * hidden * (1.0 + tangent)
    slope = 0.5 * (1.0 + tangent) + 0.5 * hidden * (1.0 - tangent * tangent) * root_two_pi * (
        1.0 + 3.0 * cubic_coef * hidden * hidden
    )
    return (value, slope)


def halo_rows(up, mid, down, left, right, at):
    lane = lane_ids(CT)
    l = left[at, :].astype(f32)
    r = right[at, :].astype(f32)
    rows = []
    for i in range(SPAN):
        if i < HALF:
            x = up[i, at, :]
        elif i < SPAN - HALF:
            x = mid[i - HALF, at, :]
        else:
            x = down[i - (SPAN - HALF), at, :]
        edge = jnp.where(
            lane >= 64, rolled(l, LANES - HALF - HALF * i), rolled(r, LANES - HALF * i)
        )
        rows.append((x.astype(f32), edge))
    return rows


def window(row, s):
    x, edge = row
    if s == 0:
        return x
    lane = lane_ids(CT)
    mask = (lane < -s) if s < 0 else (lane >= LANES - s)
    return jnp.where(mask, rolled(edge, -s), rolled(x, -s))


def edges_kernel(up, mid, down, first, last):
    channels = mid.shape[1]
    lane = lane_ids(CT)

    def step(t, carry):
        at = pl.ds(pl.multiple_of(t * CT, CT), CT)
        head = jnp.zeros((CT, LANES), f32)
        tail = jnp.zeros((CT, LANES), f32)
        for i in range(SPAN):
            if i < HALF:
                x = up[i, at, :]
            elif i < SPAN - HALF:
                x = mid[i - HALF, at, :]
            else:
                x = down[i - (SPAN - HALF), at, :]
            x = x.astype(f32)
            mask = (lane >= HALF * i) & (lane < HALF * i + HALF)
            head = jnp.where(mask, rolled(x, HALF * i), head)
            tail = jnp.where(mask, rolled(x, HALF * i + HALF), tail)
        first[at, :] = head.astype(bf16)
        last[at, :] = tail.astype(bf16)
        return carry

    lax.fori_loop(0, channels // CT, step, 0)


def edges(up, mid, down):
    shape = jax.ShapeDtypeStruct((mid.shape[1], LANES), bf16)
    return vcall(edges_kernel, out_shape=(shape, shape), name="edges")(up, mid, down)


def accumulate_taps(rows, kern, at, flip):
    accum = [jnp.zeros((CT, LANES), f32) for _ in range(SPAN - KSIZE + 1)]
    weights = kern[at, :]
    for b in range(KSIZE):
        shifted = [window(row, b - HALF) for row in rows]
        for a in range(KSIZE):
            tap = a * KSIZE + b
            if flip:
                tap = KSIZE * KSIZE - 1 - tap
            w = jnp.broadcast_to(weights[:, tap : tap + 1], (CT, LANES))
            for i in range(len(accum)):
                accum[i] = accum[i] + w * shifted[i + a]
    return accum


def forward_kernel(up, mid, down, left, right, kern, gain, shift, cot, mixed, payload):
    tile_rows, channels, _ = mid.shape

    def step(t, carry):
        at = pl.ds(pl.multiple_of(t * CT, CT), CT)
        rows = halo_rows(up, mid, down, left, right, at)
        accum = accumulate_taps(rows, kern, at, False)
        for i in range(tile_rows):
            mixed[at, i * LANES : (i + 1) * LANES] = accum[i]
        return carry

    lax.fori_loop(0, channels // CT, step, 0)
    for i in range(tile_rows):
        cols = slice(i * LANES, (i + 1) * LANES)
        x = mixed[:, cols]
        mean = jnp.sum(x, axis=0, keepdims=True) / channels
        dev = x - mean
        spread = jnp.sum(dev * dev, axis=0, keepdims=True)
        rows = split3(mean) + split3(spread)
        stats = jnp.concatenate(rows + [jnp.zeros((CT - 6, LANES), f32)], axis=0)
        if i == 0:
            row_id = lax.broadcasted_iota(jnp.int32, (CT, LANES), 0)
            both = jnp.concatenate([gain[...], shift[...]], axis=1)
            for k, part in enumerate(split3(both)):
                stats = jnp.where(row_id == 6 + k, jnp.broadcast_to(part, (CT, LANES)), stats)
        dev = dev.astype(bf16)
        stats = stats.astype(bf16)
        for d in range(payload.shape[0]):
            payload[d, 0:channels, cols] = dev
            payload[d, channels : 2 * channels, cols] = cot[i]
            payload[d, 2 * channels : 2 * channels + CT, cols] = stats


def forward(up, mid, down, left, right, kern, gain, shift, cot, parts):
    tile_rows, channels, _ = mid.shape
    pixels = tile_rows * LANES
    return vcall(
        forward_kernel,
        out_shape=(
            jax.ShapeDtypeStruct((channels, pixels), f32),
            jax.ShapeDtypeStruct((parts, 2 * channels + CT, pixels), bf16),
        ),
        name="forward",
    )(up, mid, down, left, right, kern, gain, shift, cot)


def column(row, n):
    i = lax.broadcasted_iota(jnp.int32, (n, n), 0)
    j = lax.broadcasted_iota(jnp.int32, (n, n), 1)
    return jnp.sum(jnp.where(i == j, jnp.broadcast_to(row, (n, n)), 0.0), axis=1, keepdims=True)


def dot(a, b, dims):
    return lax.dot_general(a, b, (dims, ((), ())), preferred_element_type=f32)


def row_masks(size):
    return {8: (1, 2, 6), 4: (1, 2), 2: (1,)}[size]


def row_bits(r, size):
    if size == 8:
        return (r % 2, (r // 2 + r // 4) % 2, r // 4)
    return (r % 2, r // 2)[: size.bit_length() - 1]


def row_chunk(r, size):
    chunk = 0
    for bit in row_bits(r, size):
        chunk = 2 * chunk + bit
    return chunk


def row_bit(step):
    return row_bits(lax.axis_index("row"), lax.axis_size("row"))[step]


def halves(ref, step, send, keep):
    n = send.shape[0]
    bit = row_bit(step)
    send[...] = ref[pl.ds(pl.multiple_of((1 - bit) * n, n), n), :]
    keep[...] = ref[pl.ds(pl.multiple_of(bit * n, n), n), :]


def halve_kernel(step, x, recv, send, keep, total):
    total[...] = x[...] + recv[...]
    halves(total, step, send, keep)


def halve(step, x, recv, name):
    shape = jax.ShapeDtypeStruct((x.shape[0] // 2, LANES), f32)
    return vcall(
        functools.partial(halve_kernel, step),
        out_shape=(shape, shape),
        scratch_shapes=[pltpu.VMEM(x.shape, f32)],
        name=name,
    )(x, recv)


def reduce_rows(send, keep):
    size = lax.axis_size("row")
    for step, mask in enumerate(row_masks(size)):
        recv = lax.ppermute(send, "row", [(i, i ^ mask) for i in range(size)])
        if step + 1 < len(row_masks(size)):
            send, keep = halve(step + 1, keep, recv, "halve")
    return keep, recv


def mlp_kernel(recv, w_exp, bias, w_red, payload, stats_out, send, keep, off, grads, s_norm, s_act, s_cot, s_gh):
    parts, height, pixels = recv.shape
    ch = (height - CT) // 2
    total = parts * ch
    width = 2 * LANES
    gains, shifts = [], []
    for k in range(parts):
        head = recv[k, 2 * ch : 2 * ch + CT, 0:LANES].astype(f32)
        both = head[6:7] + head[7:8] + head[8:9]
        gains.append(column(both[:, 0:ch], ch))
        shifts.append(column(both[:, ch : 2 * ch], ch))
    bias_col = column(bias[...], bias.shape[1])
    for blk in range(pixels // width):
        cols = slice(blk * width, (blk + 1) * width)
        means, spreads = [], []
        for k in range(parts):
            st = recv[k, 2 * ch : 2 * ch + CT, cols].astype(f32)
            means.append(st[0:1] + st[1:2] + st[2:3])
            spreads.append(st[3:4] + st[4:5] + st[5:6])
        centre = sum(means) / parts
        spread = sum(spreads)
        for k in range(parts):
            gap = means[k] - centre
            spread = spread + ch * gap * gap
        inverse = lax.rsqrt(spread / total + epsilon)
        stats_out[0:1, cols] = centre
        stats_out[1:2, cols] = inverse
        for k in range(parts):
            at = slice(k * ch, (k + 1) * ch)
            dev = recv[k, 0:ch, cols].astype(f32)
            normed = (dev + (means[k] - centre)) * inverse
            s_norm[at, cols] = (normed * gains[k] + shifts[k]).astype(bf16)
            s_cot[at, cols] = recv[k, ch : 2 * ch, cols]
        hidden = dot(w_exp[...], s_norm[:, cols], ((0,), (0,))) + bias_col
        value, slope = gelu_pair(hidden)
        active = value.astype(bf16)
        s_act[:, cols] = active
        gh = (dot(w_red[...], s_cot[:, cols], ((1,), (0,))) * slope).astype(bf16)
        s_gh[:, cols] = gh
        mlp = dot(w_red[...], active, ((0,), (0,)))
        part = dot(w_exp[...], gh, ((1,), (0,)))
        plain = jnp.zeros((1, width), f32)
        cross = jnp.zeros((1, width), f32)
        for k in range(parts):
            at = slice(k * ch, (k + 1) * ch)
            dev = recv[k, 0:ch, cols].astype(f32)
            normed = (dev + (means[k] - centre)) * inverse
            scaled = part[at] * gains[k]
            plain = plain + jnp.sum(scaled, axis=0, keepdims=True)
            cross = cross + jnp.sum(scaled * normed, axis=0, keepdims=True)
            payload[k, 0:ch, cols] = mlp[at].astype(bf16)
            payload[k, ch : 2 * ch, cols] = part[at].astype(bf16)
        sums = jnp.concatenate(
            split3(plain) + split3(cross) + [jnp.zeros((CT - 6, width), f32)], axis=0
        ).astype(bf16)
        for k in range(parts):
            payload[k, 2 * ch : 2 * ch + CT, cols] = sums
    last = ((1,), (1,))
    grad_exp = dot(s_norm[...], s_gh[...], last)
    grad_red = dot(s_act[...], s_cot[...], last)
    n = grad_exp.shape[0]
    grads[0:n, :] = grad_exp[:, 0:LANES]
    grads[n : 2 * n, :] = grad_exp[:, LANES:]
    grads[2 * n : 3 * n, :] = grad_red[:, 0:LANES]
    grads[3 * n : 4 * n, :] = grad_red[:, LANES:]
    halves(grads, 0, send, keep)
    sums = dot(s_gh[...], jnp.ones((pixels, LANES), bf16), ((1,), (0,)))
    table = jnp.zeros((ch, LANES), f32)
    lane = lane_ids(ch)
    for j in range(sums.shape[0] // ch):
        table = jnp.where(lane == OFFSET + j, sums[j * ch : (j + 1) * ch], table)
    off[...] = table


def mlp(recv, w_exp, bias, w_red):
    _, _, pixels = recv.shape
    hid = w_red.shape[0]
    total = w_exp.shape[0]
    return vcall(
        mlp_kernel,
        out_shape=(
            jax.ShapeDtypeStruct(recv.shape, bf16),
            jax.ShapeDtypeStruct((2, pixels), f32),
            jax.ShapeDtypeStruct((2 * total, LANES), f32),
            jax.ShapeDtypeStruct((2 * total, LANES), f32),
            jax.ShapeDtypeStruct(((recv.shape[1] - CT) // 2, LANES), f32),
        ),
        scratch_shapes=[
            pltpu.VMEM((4 * total, LANES), f32),
            pltpu.VMEM((total, pixels), bf16),
            pltpu.VMEM((hid, pixels), bf16),
            pltpu.VMEM((total, pixels), bf16),
            pltpu.VMEM((hid, pixels), bf16),
        ],
        name="mlp",
    )(recv, w_exp, bias, w_red)


def norm_back_kernel(recv, mixed, stats, gain, image, off, result, grad_mixed, rounded, small):
    parts, height, _ = recv.shape
    ch = (height - CT) // 2
    tile_rows = image.shape[0]
    total = parts * ch
    gain_col = column(gain[...], ch)
    acc_gain = jnp.zeros((ch, LANES), f32)
    acc_shift = jnp.zeros((ch, LANES), f32)
    for i in range(tile_rows):
        cols = slice(i * LANES, (i + 1) * LANES)
        mlp_out = jnp.zeros((ch, LANES), f32)
        grad = jnp.zeros((ch, LANES), f32)
        sums = jnp.zeros((CT, LANES), f32)
        for k in range(parts):
            mlp_out = mlp_out + recv[k, 0:ch, cols].astype(f32)
            grad = grad + recv[k, ch : 2 * ch, cols].astype(f32)
            sums = sums + recv[k, 2 * ch : 2 * ch + CT, cols].astype(f32)
        result[i] = (image[i].astype(f32) + mlp_out).astype(bf16)
        plain = (sums[0:1] + sums[1:2] + sums[2:3]) / total
        cross = (sums[3:4] + sums[4:5] + sums[5:6]) / total
        inverse = stats[1:2, cols]
        normed = (mixed[:, cols] - stats[0:1, cols]) * inverse
        acc_gain = acc_gain + grad * normed
        acc_shift = acc_shift + grad
        out = inverse * (grad * gain_col - plain - normed * cross)
        grad_mixed[i] = out
        rounded[i] = out.astype(bf16)
    g = jnp.sum(acc_gain, axis=1, keepdims=True)
    s = jnp.sum(acc_shift, axis=1, keepdims=True)
    lane = lane_ids(ch)
    small[...] = jnp.where(lane == GAIN, g, jnp.where(lane == SHIFT, s, off[...]))


def norm_back(recv, mixed, stats, gain, image, off):
    _, channels, _ = image.shape
    return vcall(
        norm_back_kernel,
        out_shape=(
            jax.ShapeDtypeStruct(image.shape, bf16),
            jax.ShapeDtypeStruct(image.shape, f32),
            jax.ShapeDtypeStruct(image.shape, bf16),
            jax.ShapeDtypeStruct((channels, LANES), f32),
        ),
        name="norm_back",
    )(recv, mixed, stats, gain, image, off)


def tap_grad_kernel(up, mid, down, left, right, grad_mixed, small, keep, recv, out, table_ref, total):
    tile_rows, channels, _ = mid.shape
    lane = lane_ids(CT)

    def step(t, carry):
        at = pl.ds(pl.multiple_of(t * CT, CT), CT)
        rows = halo_rows(up, mid, down, left, right, at)
        grads = [grad_mixed[i, at, :] for i in range(tile_rows)]
        table = small[at, :]
        for b in range(KSIZE):
            shifted = [window(row, b - HALF) for row in rows]
            for a in range(KSIZE):
                accum = grads[0] * shifted[a]
                for i in range(1, tile_rows):
                    accum = accum + grads[i] * shifted[a + i]
                value = jnp.sum(accum, axis=1, keepdims=True)
                table = jnp.where(lane == a * KSIZE + b, value, table)
        table_ref[at, :] = table
        return carry

    lax.fori_loop(0, channels // CT, step, 0)
    half = channels // 2
    total[...] = table_ref[0:half, :] + rolled(table_ref[half:channels, :], LANES // 2)
    cols, height, _ = out.shape
    part = keep.shape[0] // cols
    per = total.shape[0] // cols
    for c in range(cols):
        at = slice(c * part, (c + 1) * part)
        out[c, 0:part, :] = keep[at, :] + recv[at, :]
        out[c, part : part + per, :] = total[c * per : (c + 1) * per, :]
        out[c, part + per :, :] = jnp.zeros((height - part - per, LANES), f32)


def tap_grad(up, mid, down, left, right, grad_mixed, small, keep, recv, cols):
    channels = mid.shape[1]
    part, per = keep.shape[0] // cols, channels // 2 // cols
    height = part + -(-2 * per // 8) * 8
    return vcall(
        tap_grad_kernel,
        out_shape=jax.ShapeDtypeStruct((cols, height, LANES), f32),
        scratch_shapes=[pltpu.VMEM((channels, LANES), f32), pltpu.VMEM((channels // 2, LANES), f32)],
        name="tap_grad",
    )(up, mid, down, left, right, grad_mixed, small, keep, recv)


def backward_kernel(up, mid, down, left, right, kern, cot, out):
    tile_rows, channels, _ = mid.shape

    def step(t, carry):
        at = pl.ds(pl.multiple_of(t * CT, CT), CT)
        rows = halo_rows(up, mid, down, left, right, at)
        accum = accumulate_taps(rows, kern, at, True)
        for i in range(tile_rows):
            out[i, at, :] = (cot[i, at, :].astype(f32) + accum[i]).astype(bf16)
        return carry

    lax.fori_loop(0, channels // CT, step, 0)


def backward(up, mid, down, left, right, kern, cot):
    return vcall(
        backward_kernel,
        out_shape=jax.ShapeDtypeStruct(cot.shape, bf16),
        name="backward",
    )(up, mid, down, left, right, kern, cot)


def hi_lo(x):
    hi = x.astype(bf16).astype(f32)
    return jnp.concatenate([hi, x - hi], axis=0)


def col_pack_kernel(per, recv, out):
    total = recv[0]
    for c in range(1, recv.shape[0]):
        total = total + recv[c]
    part = total.shape[0] - -(-2 * per // 8) * 8
    tail = hi_lo(total[part : part + per])
    pad = total.shape[0] - part - 2 * per
    pieces = [total[0:part], tail] + ([jnp.zeros((pad, LANES), f32)] if pad else [])
    tile = jnp.concatenate(pieces, axis=0).astype(bf16)
    for c in range(out.shape[0]):
        out[c] = tile


def col_pack(recv, per):
    return vcall(
        functools.partial(col_pack_kernel, per),
        out_shape=jax.ShapeDtypeStruct(recv.shape, bf16),
        name="col_pack",
    )(recv)


def row_pack_kernel(per, recv, out, tile):
    cols, height, _ = recv.shape
    part = height - -(-2 * per // 8) * 8
    base, size = cols * part, cols * per
    for c in range(cols):
        x = recv[c].astype(f32)
        tile[c * part : (c + 1) * part, :] = x[0:part]
        tile[base + c * per : base + (c + 1) * per, :] = x[part : part + per]
        low = base + size + c * per
        tile[low : low + per, :] = x[part + per : part + 2 * per]
    x = tile[...].astype(bf16)
    for r in range(out.shape[0]):
        out[r] = x


def row_pack(recv, rows, per):
    cols, height, _ = recv.shape
    tall = cols * (height - -(-2 * per // 8) * 8 + 2 * per)
    return vcall(
        functools.partial(row_pack_kernel, per),
        out_shape=jax.ShapeDtypeStruct((rows, tall, LANES), bf16),
        scratch_shapes=[pltpu.VMEM((tall, LANES), f32)],
        name="row_pack",
    )(recv)


def final_kernel(scale, flat, exp_ref, red_ref, taps_ref, gain_ref, shift_ref, off_ref):
    rows = flat.shape[0]
    n = exp_ref.shape[0]
    per = taps_ref.shape[1] // 2
    size_all = 4 * n // rows
    for r in range(rows):
        x = flat[r].astype(f32) * scale
        block = x[0:size_all]
        tail = x[size_all : size_all + per] + x[size_all + per : size_all + 2 * per]
        total = tail if r == 0 else total + tail
        start = row_chunk(r, rows) * size_all
        lo = 0
        while lo < size_all:
            which, at = divmod(start + lo, n)
            size = min(size_all - lo, n - at)
            ref = (exp_ref, red_ref)[which // 2]
            lane = (which % 2) * LANES
            ref[at : at + size, lane : lane + LANES] = block[lo : lo + size]
            lo += size
    x = total
    both = jnp.concatenate([x, rolled(x, LANES // 2)], axis=0)
    wide = jnp.concatenate([both, jnp.zeros((LANES - both.shape[0], LANES), f32)], axis=0)
    flip = jnp.transpose(wide)[:, 0 : both.shape[0]]
    taps_ref[...] = flip[0 : taps_ref.shape[0], :]
    gain_ref[...] = flip[GAIN : GAIN + 1]
    shift_ref[...] = flip[SHIFT : SHIFT + 1]
    channels = flip.shape[1]
    for j in range(off_ref.shape[1] // channels):
        off_ref[:, j * channels : (j + 1) * channels] = flip[OFFSET + j : OFFSET + j + 1]


def final(flat, scale, total, hid, channels, taps):
    return vcall(
        functools.partial(final_kernel, scale),
        out_shape=(
            jax.ShapeDtypeStruct((total, hid), f32),
            jax.ShapeDtypeStruct((hid, total), f32),
            jax.ShapeDtypeStruct((taps, channels), f32),
            jax.ShapeDtypeStruct((1, channels), f32),
            jax.ShapeDtypeStruct((1, channels), f32),
            jax.ShapeDtypeStruct((1, hid), f32),
        ),
        name="final",
    )(flat)


def neighbours(first, last, axis):
    size = lax.axis_size(axis)
    up = [(i, i + 1) for i in range(size - 1)]
    down = [(j, i) for i, j in up]
    return lax.ppermute(last, axis, up), lax.ppermute(first, axis, down)


def halo(x):
    rows = x.shape[0]
    up, down = neighbours(x[:HALF], x[rows - HALF :], "row")
    first, last = edges(up, x, down)
    left, right = neighbours(first, last, "col")
    return up, down, left, right


def exchange(x, axis):
    return lax.all_to_all(x, axis, 0, 0)


def reduce_cols(part, per):
    part = exchange(part, "col")
    flat = exchange(col_pack(part, per), "col")
    return exchange(row_pack(flat, lax.axis_size("row"), per), "row")


def body(
    image, depth_kernel, norm_gain, norm_shift, expand_weight, expand_bias, reduce_weight, cotangent
):
    channels, tile_rows, tile_cols = image.shape
    pixels = tile_rows * tile_cols
    parts = lax.axis_size("ch")
    hid = reduce_weight.shape[0]
    total = expand_weight.shape[0]
    img = jnp.transpose(image, (1, 0, 2))
    cot = jnp.transpose(cotangent, (1, 0, 2))
    gain = norm_gain.reshape(1, channels)
    shift = norm_shift.reshape(1, channels)
    bias = lax.dynamic_slice_in_dim(expand_bias, lax.axis_index("ch") * hid, hid).reshape(1, hid)
    up, down, left, right = halo(img)
    mixed, send = forward(up, img, down, left, right, depth_kernel, gain, shift, cot, parts)
    recv = exchange(send, "ch")
    send, stats, give, keep, off = mlp(recv, expand_weight, bias, reduce_weight)
    recv = exchange(send, "ch")
    keep, part = reduce_rows(give, keep)
    result, grad_mixed, rounded, small = norm_back(recv, mixed, stats, gain, img, off)
    g_up, g_down, g_left, g_right = halo(rounded)
    cols = lax.axis_size("col")
    part = tap_grad(up, img, down, left, right, grad_mixed, small, keep, part, cols)
    grad_image = backward(g_up, rounded, g_down, g_left, g_right, depth_kernel, cot)
    flat = reduce_cols(part, channels // 2 // cols)
    pixels_all = pixels * lax.axis_size("row") * lax.axis_size("col")
    scale = float(pixels_all) ** (-0.5)
    grad_exp, grad_red, grad_taps, grad_gain, grad_shift, grad_off = final(
        flat, scale, total, hid, channels, depth_kernel.shape[1]
    )
    return (
        jnp.transpose(result, (1, 0, 2)),
        jnp.transpose(grad_image, (1, 0, 2)),
        jnp.transpose(grad_taps),
        grad_gain.reshape(channels),
        grad_shift.reshape(channels),
        grad_exp,
        grad_off.reshape(hid),
        grad_red,
    )


def solution(mesh):
    in_specs = (
        P("ch", "row", "col"),
        P("ch", None),
        P("ch"),
        P("ch"),
        P(None, "ch"),
        P(),
        P("ch", None),
        P("ch", "row", "col"),
    )
    out_specs = (
        P("ch", "row", "col"),
        P("ch", "row", "col"),
        P("ch", None),
        P("ch"),
        P("ch"),
        P(None, "ch"),
        P("ch"),
        P("ch", None),
    )

    return jax.shard_map(body, mesh=mesh, in_specs=in_specs, out_specs=out_specs, check_vma=False)
```

```python
import functools
import jax
import jax.numpy as jnp
from jax import lax
from jax.experimental import pallas as pl
from jax.experimental.pallas import tpu as pltpu
from jax.sharding import PartitionSpec as P

KSIZE = 7
HALF = 3
SPAN = KSIZE + HALF
epsilon = 1e-06
root_two_pi = 0.7978845608028654
cubic_coef = 0.044715
f32 = jnp.float32
bf16 = jnp.bfloat16
LANES = 128
CT = 16
GAIN = KSIZE * KSIZE
SHIFT = GAIN + 1
OFFSET = GAIN + 2


def vcall(kernel, out_shape, **kw):
    spec = pl.BlockSpec(memory_space=pltpu.VMEM)

    def call(*args):
        return pl.pallas_call(
            kernel,
            out_shape=out_shape,
            in_specs=[spec] * len(args),
            out_specs=jax.tree.map(lambda _: spec, out_shape),
            compiler_params=pltpu.CompilerParams(vmem_limit_bytes=8 << 20),
            **kw,
        )(*args)

    return call


def lane_ids(rows):
    return lax.broadcasted_iota(jnp.int32, (rows, LANES), 1)


def rolled(x, shift):
    shift = shift % LANES
    return x if shift == 0 else pltpu.roll(x, shift, 1)


def split3(x):
    hi = x.astype(bf16)
    rest = x - hi.astype(f32)
    mid = rest.astype(bf16)
    low = (rest - mid.astype(f32)).astype(bf16)
    return [hi.astype(f32), mid.astype(f32), low.astype(f32)]


def gelu_pair(hidden):
    inner = root_two_pi * (hidden + cubic_coef * hidden * hidden * hidden)
    tangent = jnp.tanh(inner)
    value = 0.5 * hidden * (1.0 + tangent)
    slope = 0.5 * (1.0 + tangent) + 0.5 * hidden * (1.0 - tangent * tangent) * root_two_pi * (
        1.0 + 3.0 * cubic_coef * hidden * hidden
    )
    return (value, slope)


def halo_rows(up, mid, down, left, right, at):
    lane = lane_ids(CT)
    l = left[at, :].astype(f32)
    r = right[at, :].astype(f32)
    rows = []
    for i in range(SPAN):
        if i < HALF:
            x = up[i, at, :]
        elif i < SPAN - HALF:
            x = mid[i - HALF, at, :]
        else:
            x = down[i - (SPAN - HALF), at, :]
        edge = jnp.where(
            lane >= 64, rolled(l, LANES - HALF - HALF * i), rolled(r, LANES - HALF * i)
        )
        rows.append((x.astype(f32), edge))
    return rows


def window(row, s):
    x, edge = row
    if s == 0:
        return x
    lane = lane_ids(CT)
    mask = (lane < -s) if s < 0 else (lane >= LANES - s)
    return jnp.where(mask, rolled(edge, -s), rolled(x, -s))


def edges_kernel(up, mid, down, gain, shift, first, last, both):
    both[...] = jnp.concatenate([gain[...], shift[...]], axis=1)
    channels = mid.shape[1]
    lane = lane_ids(CT)

    def step(t, carry):
        at = pl.ds(pl.multiple_of(t * CT, CT), CT)
        head = jnp.zeros((CT, LANES), f32)
        tail = jnp.zeros((CT, LANES), f32)
        for i in range(SPAN):
            if i < HALF:
                x = up[i, at, :]
            elif i < SPAN - HALF:
                x = mid[i - HALF, at, :]
            else:
                x = down[i - (SPAN - HALF), at, :]
            x = x.astype(f32)
            mask = (lane >= HALF * i) & (lane < HALF * i + HALF)
            head = jnp.where(mask, rolled(x, HALF * i), head)
            tail = jnp.where(mask, rolled(x, HALF * i + HALF), tail)
        first[at, :] = head.astype(bf16)
        last[at, :] = tail.astype(bf16)
        return carry

    lax.fori_loop(0, channels // CT, step, 0)


def edges(up, mid, down, gain, shift):
    channels = mid.shape[1]
    shape = jax.ShapeDtypeStruct((channels, LANES), bf16)
    return vcall(
        edges_kernel,
        out_shape=(shape, shape, jax.ShapeDtypeStruct((1, 2 * channels), f32)),
        name="edges",
    )(up, mid, down, gain, shift)


def accumulate_taps(rows, kern, at, flip):
    accum = [jnp.zeros((CT, LANES), f32) for _ in range(SPAN - KSIZE + 1)]
    weights = kern[at, :]
    for b in range(KSIZE):
        shifted = [window(row, b - HALF) for row in rows]
        for a in range(KSIZE):
            tap = a * KSIZE + b
            if flip:
                tap = KSIZE * KSIZE - 1 - tap
            w = jnp.broadcast_to(weights[:, tap : tap + 1], (CT, LANES))
            for i in range(len(accum)):
                accum[i] = accum[i] + w * shifted[i + a]
    return accum


def forward_kernel(up, mid, down, left, right, kern, affine, cot, mixed, payload):
    tile_rows, channels, _ = mid.shape

    def step(t, carry):
        at = pl.ds(pl.multiple_of(t * CT, CT), CT)
        rows = halo_rows(up, mid, down, left, right, at)
        accum = accumulate_taps(rows, kern, at, False)
        for i in range(tile_rows):
            mixed[at, i * LANES : (i + 1) * LANES] = accum[i]
        return carry

    lax.fori_loop(0, channels // CT, step, 0)
    for i in range(tile_rows):
        cols = slice(i * LANES, (i + 1) * LANES)
        x = mixed[:, cols]
        mean = jnp.sum(x, axis=0, keepdims=True) / channels
        dev = x - mean
        spread = jnp.sum(dev * dev, axis=0, keepdims=True)
        rows = split3(mean) + split3(spread)
        stats = jnp.concatenate(rows + [jnp.zeros((CT - 6, LANES), f32)], axis=0)
        if i == 0:
            row_id = lax.broadcasted_iota(jnp.int32, (CT, LANES), 0)
            for k, part in enumerate(split3(affine[...])):
                stats = jnp.where(row_id == 6 + k, jnp.broadcast_to(part, (CT, LANES)), stats)
        dev = dev.astype(bf16)
        stats = stats.astype(bf16)
        for d in range(payload.shape[0]):
            payload[d, 0:channels, cols] = dev
            payload[d, channels : 2 * channels, cols] = cot[i]
            payload[d, 2 * channels : 2 * channels + CT, cols] = stats


def forward(up, mid, down, left, right, kern, affine, cot, parts):
    tile_rows, channels, _ = mid.shape
    pixels = tile_rows * LANES
    return vcall(
        forward_kernel,
        out_shape=(
            jax.ShapeDtypeStruct((channels, pixels), f32),
            jax.ShapeDtypeStruct((parts, 2 * channels + CT, pixels), bf16),
        ),
        name="forward",
    )(up, mid, down, left, right, kern, affine, cot)


def column(row, n):
    i = lax.broadcasted_iota(jnp.int32, (n, n), 0)
    j = lax.broadcasted_iota(jnp.int32, (n, n), 1)
    return jnp.sum(jnp.where(i == j, jnp.broadcast_to(row, (n, n)), 0.0), axis=1, keepdims=True)


def dot(a, b, dims):
    return lax.dot_general(a, b, (dims, ((), ())), preferred_element_type=f32)


def row_chunk(r, size):
    return (r % 2) * (size // 2) + r // 2


def halves(ref, send, keep):
    n = send.shape[0]
    bit = lax.axis_index("row") % 2
    send[...] = ref[pl.ds(pl.multiple_of((1 - bit) * n, n), n), :]
    keep[...] = ref[pl.ds(pl.multiple_of(bit * n, n), n), :]


def spread_kernel(x, recv, *rest):
    outs, total = rest[:-1], rest[-1]
    total[...] = x[...] + recv[...]
    n = outs[0].shape[0]
    y = lax.axis_index("row") // 2
    for m, out in enumerate(outs):
        low, high = y % 2, y // 2
        low = 1 - low if m % 2 else low
        high = 1 - high if m // 2 else high
        out[...] = total[pl.ds(pl.multiple_of((2 * high + low) * n, n), n), :]


def spread(x, recv, parts):
    shape = jax.ShapeDtypeStruct((x.shape[0] // parts, LANES), f32)
    return vcall(
        spread_kernel,
        out_shape=(shape,) * parts,
        scratch_shapes=[pltpu.VMEM(x.shape, f32)],
        name="spread",
    )(x, recv)


def reduce_rows(send, keep):
    size = lax.axis_size("row")
    recv = lax.ppermute(send, "row", [(i, i ^ 1) for i in range(size)])
    if size == 2:
        return [keep, recv]
    chunks = spread(keep, recv, size // 2)
    return [chunks[0]] + [
        lax.ppermute(chunks[m], "row", [(i, i ^ (2 * m)) for i in range(size)])
        for m in range(1, size // 2)
    ]


def mlp_kernel(recv, w_exp, bias, w_red, payload, stats_out, send, keep, off, grads, s_norm, s_act, s_cot, s_gh):
    parts, height, pixels = recv.shape
    ch = (height - CT) // 2
    total = parts * ch
    width = 2 * LANES
    gains, shifts = [], []
    for k in range(parts):
        head = recv[k, 2 * ch : 2 * ch + CT, 0:LANES].astype(f32)
        both = head[6:7] + head[7:8] + head[8:9]
        gains.append(column(both[:, 0:ch], ch))
        shifts.append(column(both[:, ch : 2 * ch], ch))
    bias_col = column(bias[...], bias.shape[1])
    for blk in range(pixels // width):
        cols = slice(blk * width, (blk + 1) * width)
        means, spreads = [], []
        for k in range(parts):
            st = recv[k, 2 * ch : 2 * ch + CT, cols].astype(f32)
            means.append(st[0:1] + st[1:2] + st[2:3])
            spreads.append(st[3:4] + st[4:5] + st[5:6])
        centre = sum(means) / parts
        spread = sum(spreads)
        for k in range(parts):
            gap = means[k] - centre
            spread = spread + ch * gap * gap
        inverse = lax.rsqrt(spread / total + epsilon)
        stats_out[0:1, cols] = centre
        stats_out[1:2, cols] = inverse
        for k in range(parts):
            at = slice(k * ch, (k + 1) * ch)
            dev = recv[k, 0:ch, cols].astype(f32)
            normed = (dev + (means[k] - centre)) * inverse
            s_norm[at, cols] = (normed * gains[k] + shifts[k]).astype(bf16)
            s_cot[at, cols] = recv[k, ch : 2 * ch, cols]
        hidden = dot(w_exp[...], s_norm[:, cols], ((0,), (0,))) + bias_col
        value, slope = gelu_pair(hidden)
        active = value.astype(bf16)
        s_act[:, cols] = active
        gh = (dot(w_red[...], s_cot[:, cols], ((1,), (0,))) * slope).astype(bf16)
        s_gh[:, cols] = gh
        mlp = dot(w_red[...], active, ((0,), (0,)))
        part = dot(w_exp[...], gh, ((1,), (0,)))
        plain = jnp.zeros((1, width), f32)
        cross = jnp.zeros((1, width), f32)
        for k in range(parts):
            at = slice(k * ch, (k + 1) * ch)
            dev = recv[k, 0:ch, cols].astype(f32)
            normed = (dev + (means[k] - centre)) * inverse
            scaled = part[at] * gains[k]
            plain = plain + jnp.sum(scaled, axis=0, keepdims=True)
            cross = cross + jnp.sum(scaled * normed, axis=0, keepdims=True)
            payload[k, 0:ch, cols] = mlp[at].astype(bf16)
            payload[k, ch : 2 * ch, cols] = part[at].astype(bf16)
        sums = jnp.concatenate(
            split3(plain) + split3(cross) + [jnp.zeros((CT - 6, width), f32)], axis=0
        ).astype(bf16)
        for k in range(parts):
            payload[k, 2 * ch : 2 * ch + CT, cols] = sums
    last = ((1,), (1,))
    grad_exp = dot(s_norm[...], s_gh[...], last)
    grad_red = dot(s_act[...], s_cot[...], last)
    n = grad_exp.shape[0]
    grads[0:n, :] = grad_exp[:, 0:LANES]
    grads[n : 2 * n, :] = grad_exp[:, LANES:]
    grads[2 * n : 3 * n, :] = grad_red[:, 0:LANES]
    grads[3 * n : 4 * n, :] = grad_red[:, LANES:]
    halves(grads, send, keep)
    sums = dot(s_gh[...], jnp.ones((pixels, LANES), bf16), ((1,), (0,)))
    table = jnp.zeros((ch, LANES), f32)
    lane = lane_ids(ch)
    for j in range(sums.shape[0] // ch):
        table = jnp.where(lane == OFFSET + j, sums[j * ch : (j + 1) * ch], table)
    off[...] = table


def mlp(recv, w_exp, bias, w_red):
    _, _, pixels = recv.shape
    hid = w_red.shape[0]
    total = w_exp.shape[0]
    return vcall(
        mlp_kernel,
        out_shape=(
            jax.ShapeDtypeStruct(recv.shape, bf16),
            jax.ShapeDtypeStruct((2, pixels), f32),
            jax.ShapeDtypeStruct((2 * total, LANES), f32),
            jax.ShapeDtypeStruct((2 * total, LANES), f32),
            jax.ShapeDtypeStruct(((recv.shape[1] - CT) // 2, LANES), f32),
        ),
        scratch_shapes=[
            pltpu.VMEM((4 * total, LANES), f32),
            pltpu.VMEM((total, pixels), bf16),
            pltpu.VMEM((hid, pixels), bf16),
            pltpu.VMEM((total, pixels), bf16),
            pltpu.VMEM((hid, pixels), bf16),
        ],
        name="mlp",
    )(recv, w_exp, bias, w_red)


def norm_back_kernel(recv, mixed, stats, gain, image, off, result, grad_mixed, rounded, small):
    parts, height, _ = recv.shape
    ch = (height - CT) // 2
    tile_rows = image.shape[0]
    total = parts * ch
    gain_col = column(gain[...], ch)
    acc_gain = jnp.zeros((ch, LANES), f32)
    acc_shift = jnp.zeros((ch, LANES), f32)
    for i in range(tile_rows):
        cols = slice(i * LANES, (i + 1) * LANES)
        mlp_out = jnp.zeros((ch, LANES), f32)
        grad = jnp.zeros((ch, LANES), f32)
        sums = jnp.zeros((CT, LANES), f32)
        for k in range(parts):
            mlp_out = mlp_out + recv[k, 0:ch, cols].astype(f32)
            grad = grad + recv[k, ch : 2 * ch, cols].astype(f32)
            sums = sums + recv[k, 2 * ch : 2 * ch + CT, cols].astype(f32)
        result[i] = (image[i].astype(f32) + mlp_out).astype(bf16)
        plain = (sums[0:1] + sums[1:2] + sums[2:3]) / total
        cross = (sums[3:4] + sums[4:5] + sums[5:6]) / total
        inverse = stats[1:2, cols]
        normed = (mixed[:, cols] - stats[0:1, cols]) * inverse
        acc_gain = acc_gain + grad * normed
        acc_shift = acc_shift + grad
        out = inverse * (grad * gain_col - plain - normed * cross)
        grad_mixed[i] = out
        rounded[i] = out.astype(bf16)
    g = jnp.sum(acc_gain, axis=1, keepdims=True)
    s = jnp.sum(acc_shift, axis=1, keepdims=True)
    lane = lane_ids(ch)
    small[...] = jnp.where(lane == GAIN, g, jnp.where(lane == SHIFT, s, off[...]))


def norm_back(recv, mixed, stats, gain, image, off):
    _, channels, _ = image.shape
    return vcall(
        norm_back_kernel,
        out_shape=(
            jax.ShapeDtypeStruct(image.shape, bf16),
            jax.ShapeDtypeStruct(image.shape, f32),
            jax.ShapeDtypeStruct(image.shape, bf16),
            jax.ShapeDtypeStruct((channels, LANES), f32),
        ),
        name="norm_back",
    )(recv, mixed, stats, gain, image, off)


def tap_grad_kernel(up, mid, down, left, right, grad_mixed, small, *rest):
    pieces, (out, table_ref, total) = rest[:-3], rest[-3:]
    tile_rows, channels, _ = mid.shape
    lane = lane_ids(CT)

    def step(t, carry):
        at = pl.ds(pl.multiple_of(t * CT, CT), CT)
        rows = halo_rows(up, mid, down, left, right, at)
        grads = [grad_mixed[i, at, :] for i in range(tile_rows)]
        table = small[at, :]
        for b in range(KSIZE):
            shifted = [window(row, b - HALF) for row in rows]
            for a in range(KSIZE):
                accum = grads[0] * shifted[a]
                for i in range(1, tile_rows):
                    accum = accum + grads[i] * shifted[a + i]
                value = jnp.sum(accum, axis=1, keepdims=True)
                table = jnp.where(lane == a * KSIZE + b, value, table)
        table_ref[at, :] = table
        return carry

    lax.fori_loop(0, channels // CT, step, 0)
    half = channels // 2
    total[...] = table_ref[0:half, :] + rolled(table_ref[half:channels, :], LANES // 2)
    cols, height, _ = out.shape
    part = pieces[0].shape[0] // cols
    per = total.shape[0] // cols
    for c in range(cols):
        at = slice(c * part, (c + 1) * part)
        out[c, 0:part, :] = sum(x[at, :] for x in pieces)
        out[c, part : part + per, :] = total[c * per : (c + 1) * per, :]
        out[c, part + per :, :] = jnp.zeros((height - part - per, LANES), f32)


def tap_grad(up, mid, down, left, right, grad_mixed, small, pieces, cols):
    channels = mid.shape[1]
    part, per = pieces[0].shape[0] // cols, channels // 2 // cols
    height = part + -(-2 * per // 8) * 8
    return vcall(
        tap_grad_kernel,
        out_shape=jax.ShapeDtypeStruct((cols, height, LANES), f32),
        scratch_shapes=[pltpu.VMEM((channels, LANES), f32), pltpu.VMEM((channels // 2, LANES), f32)],
        name="tap_grad",
    )(up, mid, down, left, right, grad_mixed, small, *pieces)


def backward_kernel(up, mid, down, left, right, kern, cot, out):
    tile_rows, channels, _ = mid.shape

    def step(t, carry):
        at = pl.ds(pl.multiple_of(t * CT, CT), CT)
        rows = halo_rows(up, mid, down, left, right, at)
        accum = accumulate_taps(rows, kern, at, True)
        for i in range(tile_rows):
            out[i, at, :] = (cot[i, at, :].astype(f32) + accum[i]).astype(bf16)
        return carry

    lax.fori_loop(0, channels // CT, step, 0)


def backward(up, mid, down, left, right, kern, cot):
    return vcall(
        backward_kernel,
        out_shape=jax.ShapeDtypeStruct(cot.shape, bf16),
        name="backward",
    )(up, mid, down, left, right, kern, cot)


def hi_lo(x):
    hi = x.astype(bf16).astype(f32)
    return jnp.concatenate([hi, x - hi], axis=0)


def col_pack_kernel(per, recv, out):
    total = recv[0]
    for c in range(1, recv.shape[0]):
        total = total + recv[c]
    part = total.shape[0] - -(-2 * per // 8) * 8
    tail = hi_lo(total[part : part + per])
    pad = total.shape[0] - part - 2 * per
    pieces = [total[0:part], tail] + ([jnp.zeros((pad, LANES), f32)] if pad else [])
    tile = jnp.concatenate(pieces, axis=0).astype(bf16)
    for c in range(out.shape[0]):
        out[c] = tile


def col_pack(recv, per):
    return vcall(
        functools.partial(col_pack_kernel, per),
        out_shape=jax.ShapeDtypeStruct(recv.shape, bf16),
        name="col_pack",
    )(recv)


def row_pack_kernel(per, recv, out, tile):
    cols, height, _ = recv.shape
    part = height - -(-2 * per // 8) * 8
    base, size = cols * part, cols * per
    for c in range(cols):
        x = recv[c].astype(f32)
        tile[c * part : (c + 1) * part, :] = x[0:part]
        tile[base + c * per : base + (c + 1) * per, :] = x[part : part + per]
        low = base + size + c * per
        tile[low : low + per, :] = x[part + per : part + 2 * per]
    x = tile[...].astype(bf16)
    for r in range(out.shape[0]):
        out[r] = x


def row_pack(recv, rows, per):
    cols, height, _ = recv.shape
    tall = cols * (height - -(-2 * per // 8) * 8 + 2 * per)
    return vcall(
        functools.partial(row_pack_kernel, per),
        out_shape=jax.ShapeDtypeStruct((rows, tall, LANES), bf16),
        scratch_shapes=[pltpu.VMEM((tall, LANES), f32)],
        name="row_pack",
    )(recv)


def final_kernel(scale, flat, exp_ref, red_ref, taps_ref, gain_ref, shift_ref, off_ref):
    rows = flat.shape[0]
    n = exp_ref.shape[0]
    per = taps_ref.shape[1] // 2
    size_all = 4 * n // rows
    for r in range(rows):
        x = flat[r].astype(f32) * scale
        block = x[0:size_all]
        tail = x[size_all : size_all + per] + x[size_all + per : size_all + 2 * per]
        total = tail if r == 0 else total + tail
        start = row_chunk(r, rows) * size_all
        lo = 0
        while lo < size_all:
            which, at = divmod(start + lo, n)
            size = min(size_all - lo, n - at)
            ref = (exp_ref, red_ref)[which // 2]
            lane = (which % 2) * LANES
            ref[at : at + size, lane : lane + LANES] = block[lo : lo + size]
            lo += size
    x = total
    both = jnp.concatenate([x, rolled(x, LANES // 2)], axis=0)
    wide = jnp.concatenate([both, jnp.zeros((LANES - both.shape[0], LANES), f32)], axis=0)
    flip = jnp.transpose(wide)[:, 0 : both.shape[0]]
    taps_ref[...] = flip[0 : taps_ref.shape[0], :]
    gain_ref[...] = flip[GAIN : GAIN + 1]
    shift_ref[...] = flip[SHIFT : SHIFT + 1]
    channels = flip.shape[1]
    for j in range(off_ref.shape[1] // channels):
        off_ref[:, j * channels : (j + 1) * channels] = flip[OFFSET + j : OFFSET + j + 1]


def final(flat, scale, total, hid, channels, taps):
    return vcall(
        functools.partial(final_kernel, scale),
        out_shape=(
            jax.ShapeDtypeStruct((total, hid), f32),
            jax.ShapeDtypeStruct((hid, total), f32),
            jax.ShapeDtypeStruct((taps, channels), f32),
            jax.ShapeDtypeStruct((1, channels), f32),
            jax.ShapeDtypeStruct((1, channels), f32),
            jax.ShapeDtypeStruct((1, hid), f32),
        ),
        name="final",
    )(flat)


def neighbours(first, last, axis):
    size = lax.axis_size(axis)
    up = [(i, i + 1) for i in range(size - 1)]
    down = [(j, i) for i, j in up]
    return lax.ppermute(last, axis, up), lax.ppermute(first, axis, down)


def halo(x, gain, shift):
    rows = x.shape[0]
    up, down = neighbours(x[:HALF], x[rows - HALF :], "row")
    first, last, both = edges(up, x, down, gain, shift)
    left, right = neighbours(first, last, "col")
    return up, down, left, right, both


def exchange(x, axis):
    return lax.all_to_all(x, axis, 0, 0)


def reduce_cols(part, per):
    part = exchange(part, "col")
    flat = exchange(col_pack(part, per), "col")
    return exchange(row_pack(flat, lax.axis_size("row"), per), "row")


def body(
    image, depth_kernel, norm_gain, norm_shift, expand_weight, expand_bias, reduce_weight, cotangent
):
    channels, tile_rows, tile_cols = image.shape
    pixels = tile_rows * tile_cols
    parts = lax.axis_size("ch")
    hid = reduce_weight.shape[0]
    total = expand_weight.shape[0]
    img = jnp.transpose(image, (1, 0, 2))
    cot = jnp.transpose(cotangent, (1, 0, 2))
    gain = norm_gain.reshape(1, channels)
    shift = norm_shift.reshape(1, channels)
    bias = lax.dynamic_slice_in_dim(expand_bias, lax.axis_index("ch") * hid, hid).reshape(1, hid)
    up, down, left, right, affine = halo(img, gain, shift)
    mixed, send = forward(up, img, down, left, right, depth_kernel, affine, cot, parts)
    recv = exchange(send, "ch")
    send, stats, give, keep, off = mlp(recv, expand_weight, bias, reduce_weight)
    recv = exchange(send, "ch")
    pieces = reduce_rows(give, keep)
    result, grad_mixed, rounded, small = norm_back(recv, mixed, stats, gain, img, off)
    g_up, g_down, g_left, g_right, _ = halo(rounded, gain, shift)
    cols = lax.axis_size("col")
    part = tap_grad(up, img, down, left, right, grad_mixed, small, pieces, cols)
    grad_image = backward(g_up, rounded, g_down, g_left, g_right, depth_kernel, cot)
    flat = reduce_cols(part, channels // 2 // cols)
    pixels_all = pixels * lax.axis_size("row") * lax.axis_size("col")
    scale = float(pixels_all) ** (-0.5)
    grad_exp, grad_red, grad_taps, grad_gain, grad_shift, grad_off = final(
        flat, scale, total, hid, channels, depth_kernel.shape[1]
    )
    return (
        jnp.transpose(result, (1, 0, 2)),
        jnp.transpose(grad_image, (1, 0, 2)),
        jnp.transpose(grad_taps),
        grad_gain.reshape(channels),
        grad_shift.reshape(channels),
        grad_exp,
        grad_off.reshape(hid),
        grad_red,
    )


def solution(mesh):
    in_specs = (
        P("ch", "row", "col"),
        P("ch", None),
        P("ch"),
        P("ch"),
        P(None, "ch"),
        P(),
        P("ch", None),
        P("ch", "row", "col"),
    )
    out_specs = (
        P("ch", "row", "col"),
        P("ch", "row", "col"),
        P("ch", None),
        P("ch"),
        P("ch"),
        P(None, "ch"),
        P("ch"),
        P("ch", None),
    )

    return jax.shard_map(body, mesh=mesh, in_specs=in_specs, out_specs=out_specs, check_vma=False)
```

```python
import functools
import jax
import jax.numpy as jnp
from jax import lax
from jax.experimental import pallas as pl
from jax.experimental.pallas import tpu as pltpu
from jax.sharding import PartitionSpec as P

KSIZE = 7
HALF = 3
SPAN = KSIZE + HALF
epsilon = 1e-06
root_two_pi = 0.7978845608028654
cubic_coef = 0.044715
f32 = jnp.float32
bf16 = jnp.bfloat16
LANES = 128
CT = 16
GAIN = KSIZE * KSIZE
SHIFT = GAIN + 1
OFFSET = GAIN + 2


def vcall(kernel, out_shape, hbm=(), **kw):
    spec = pl.BlockSpec(memory_space=pltpu.VMEM)
    outside = pl.BlockSpec(memory_space=pltpu.MemorySpace.HBM)

    def call(*args):
        return pl.pallas_call(
            kernel,
            out_shape=out_shape,
            in_specs=[outside if k in hbm else spec for k in range(len(args))],
            out_specs=jax.tree.map(lambda _: spec, out_shape),
            compiler_params=pltpu.CompilerParams(vmem_limit_bytes=8 << 20),
            **kw,
        )(*args)

    return call


def lane_ids(rows):
    return lax.broadcasted_iota(jnp.int32, (rows, LANES), 1)


def rolled(x, shift):
    shift = shift % LANES
    return x if shift == 0 else pltpu.roll(x, shift, 1)


def split3(x):
    hi = x.astype(bf16)
    rest = x - hi.astype(f32)
    mid = rest.astype(bf16)
    low = (rest - mid.astype(f32)).astype(bf16)
    return [hi.astype(f32), mid.astype(f32), low.astype(f32)]


def gelu_pair(hidden):
    inner = root_two_pi * (hidden + cubic_coef * hidden * hidden * hidden)
    tangent = jnp.tanh(inner)
    value = 0.5 * hidden * (1.0 + tangent)
    slope = 0.5 * (1.0 + tangent) + 0.5 * hidden * (1.0 - tangent * tangent) * root_two_pi * (
        1.0 + 3.0 * cubic_coef * hidden * hidden
    )
    return (value, slope)


def halo_rows(up, mid, down, left, right, at):
    lane = lane_ids(CT)
    l = left[at, :].astype(f32)
    r = right[at, :].astype(f32)
    rows = []
    for i in range(SPAN):
        if i < HALF:
            x = up[i, at, :]
        elif i < SPAN - HALF:
            x = mid[i - HALF, at, :]
        else:
            x = down[i - (SPAN - HALF), at, :]
        edge = jnp.where(
            lane >= 64, rolled(l, LANES - HALF - HALF * i), rolled(r, LANES - HALF * i)
        )
        rows.append((x.astype(f32), edge))
    return rows


def window(row, s):
    x, edge = row
    if s == 0:
        return x
    lane = lane_ids(CT)
    mask = (lane < -s) if s < 0 else (lane >= LANES - s)
    return jnp.where(mask, rolled(edge, -s), rolled(x, -s))


def edges_kernel(up, mid, down, first, last):
    channels = mid.shape[1]
    lane = lane_ids(CT)

    def step(t, carry):
        at = pl.ds(pl.multiple_of(t * CT, CT), CT)
        head = jnp.zeros((CT, LANES), f32)
        tail = jnp.zeros((CT, LANES), f32)
        for i in range(SPAN):
            if i < HALF:
                x = up[i, at, :]
            elif i < SPAN - HALF:
                x = mid[i - HALF, at, :]
            else:
                x = down[i - (SPAN - HALF), at, :]
            x = x.astype(f32)
            mask = (lane >= HALF * i) & (lane < HALF * i + HALF)
            head = jnp.where(mask, rolled(x, HALF * i), head)
            tail = jnp.where(mask, rolled(x, HALF * i + HALF), tail)
        first[at, :] = head.astype(bf16)
        last[at, :] = tail.astype(bf16)
        return carry

    lax.fori_loop(0, channels // CT, step, 0)


def edges(up, mid, down):
    shape = jax.ShapeDtypeStruct((mid.shape[1], LANES), bf16)
    return vcall(edges_kernel, out_shape=(shape, shape), name="edges")(up, mid, down)


def accumulate_taps(rows, kern, at, flip):
    accum = [jnp.zeros((CT, LANES), f32) for _ in range(SPAN - KSIZE + 1)]
    weights = kern[at, :]
    for b in range(KSIZE):
        shifted = [window(row, b - HALF) for row in rows]
        for a in range(KSIZE):
            tap = a * KSIZE + b
            if flip:
                tap = KSIZE * KSIZE - 1 - tap
            w = jnp.broadcast_to(weights[:, tap : tap + 1], (CT, LANES))
            for i in range(len(accum)):
                accum[i] = accum[i] + w * shifted[i + a]
    return accum


def forward_kernel(up, mid, down, left, right, kern, gain, shift, cot, mixed, payload, affine, sem):
    tile_rows, channels, _ = mid.shape
    copies = [
        pltpu.make_async_copy(x, affine.at[pl.ds(k, 1)], sem.at[k]) for k, x in enumerate((gain, shift))
    ]
    for copy in copies:
        copy.start()

    def step(t, carry):
        at = pl.ds(pl.multiple_of(t * CT, CT), CT)
        rows = halo_rows(up, mid, down, left, right, at)
        accum = accumulate_taps(rows, kern, at, False)
        for i in range(tile_rows):
            mixed[at, i * LANES : (i + 1) * LANES] = accum[i]
        return carry

    lax.fori_loop(0, channels // CT, step, 0)
    for i in range(tile_rows):
        cols = slice(i * LANES, (i + 1) * LANES)
        x = mixed[:, cols]
        mean = jnp.sum(x, axis=0, keepdims=True) / channels
        dev = x - mean
        spread = jnp.sum(dev * dev, axis=0, keepdims=True)
        rows = split3(mean) + split3(spread)
        stats = jnp.concatenate(rows + [jnp.zeros((CT - 6, LANES), f32)], axis=0)
        if i == 0:
            row_id = lax.broadcasted_iota(jnp.int32, (CT, LANES), 0)
            for copy in copies:
                copy.wait()
            both = jnp.concatenate([affine[0:1], affine[1:2]], axis=1)
            for k, part in enumerate(split3(both)):
                stats = jnp.where(row_id == 6 + k, jnp.broadcast_to(part, (CT, LANES)), stats)
        dev = dev.astype(bf16)
        stats = stats.astype(bf16)
        for d in range(payload.shape[0]):
            payload[d, 0:channels, cols] = dev
            payload[d, channels : 2 * channels, cols] = cot[i]
            payload[d, 2 * channels : 2 * channels + CT, cols] = stats


def forward(up, mid, down, left, right, kern, gain, shift, cot, parts):
    tile_rows, channels, _ = mid.shape
    pixels = tile_rows * LANES
    return vcall(
        forward_kernel,
        out_shape=(
            jax.ShapeDtypeStruct((channels, pixels), f32),
            jax.ShapeDtypeStruct((parts, 2 * channels + CT, pixels), bf16),
        ),
        hbm=(6, 7),
        scratch_shapes=[pltpu.VMEM((2, channels), f32), pltpu.SemaphoreType.DMA((2,))],
        name="forward",
    )(up, mid, down, left, right, kern, gain, shift, cot)


def column(row, n):
    i = lax.broadcasted_iota(jnp.int32, (n, n), 0)
    j = lax.broadcasted_iota(jnp.int32, (n, n), 1)
    return jnp.sum(jnp.where(i == j, jnp.broadcast_to(row, (n, n)), 0.0), axis=1, keepdims=True)


def dot(a, b, dims):
    return lax.dot_general(a, b, (dims, ((), ())), preferred_element_type=f32)


def row_chunk(r, size):
    return (r % 2) * (size // 2) + r // 2


def halves(ref, send, keep):
    n = send.shape[0]
    bit = lax.axis_index("row") % 2
    send[...] = ref[pl.ds(pl.multiple_of((1 - bit) * n, n), n), :]
    keep[...] = ref[pl.ds(pl.multiple_of(bit * n, n), n), :]


def spread_kernel(x, recv, *rest):
    outs, total = rest[:-1], rest[-1]
    total[...] = x[...] + recv[...]
    n = outs[0].shape[0]
    y = lax.axis_index("row") // 2
    for m, out in enumerate(outs):
        low, high = y % 2, y // 2
        low = 1 - low if m % 2 else low
        high = 1 - high if m // 2 else high
        out[...] = total[pl.ds(pl.multiple_of((2 * high + low) * n, n), n), :]


def spread(x, recv, parts):
    shape = jax.ShapeDtypeStruct((x.shape[0] // parts, LANES), f32)
    return vcall(
        spread_kernel,
        out_shape=(shape,) * parts,
        scratch_shapes=[pltpu.VMEM(x.shape, f32)],
        name="spread",
    )(x, recv)


def reduce_rows(send, keep):
    size = lax.axis_size("row")
    recv = lax.ppermute(send, "row", [(i, i ^ 1) for i in range(size)])
    if size == 2:
        return [keep, recv]
    chunks = spread(keep, recv, size // 2)
    return [chunks[0]] + [
        lax.ppermute(chunks[m], "row", [(i, i ^ (2 * m)) for i in range(size)])
        for m in range(1, size // 2)
    ]


def mlp_kernel(recv, w_exp, bias, w_red, payload, stats_out, send, keep, off, grads, s_norm, s_act, s_cot, s_gh):
    parts, height, pixels = recv.shape
    ch = (height - CT) // 2
    total = parts * ch
    width = 2 * LANES
    gains, shifts = [], []
    for k in range(parts):
        head = recv[k, 2 * ch : 2 * ch + CT, 0:LANES].astype(f32)
        both = head[6:7] + head[7:8] + head[8:9]
        gains.append(column(both[:, 0:ch], ch))
        shifts.append(column(both[:, ch : 2 * ch], ch))
    bias_col = column(bias[...], bias.shape[1])
    for blk in range(pixels // width):
        cols = slice(blk * width, (blk + 1) * width)
        means, spreads = [], []
        for k in range(parts):
            st = recv[k, 2 * ch : 2 * ch + CT, cols].astype(f32)
            means.append(st[0:1] + st[1:2] + st[2:3])
            spreads.append(st[3:4] + st[4:5] + st[5:6])
        centre = sum(means) / parts
        spread = sum(spreads)
        for k in range(parts):
            gap = means[k] - centre
            spread = spread + ch * gap * gap
        inverse = lax.rsqrt(spread / total + epsilon)
        stats_out[0:1, cols] = centre
        stats_out[1:2, cols] = inverse
        for k in range(parts):
            at = slice(k * ch, (k + 1) * ch)
            dev = recv[k, 0:ch, cols].astype(f32)
            normed = (dev + (means[k] - centre)) * inverse
            s_norm[at, cols] = (normed * gains[k] + shifts[k]).astype(bf16)
            s_cot[at, cols] = recv[k, ch : 2 * ch, cols]
        hidden = dot(w_exp[...], s_norm[:, cols], ((0,), (0,))) + bias_col
        value, slope = gelu_pair(hidden)
        active = value.astype(bf16)
        s_act[:, cols] = active
        gh = (dot(w_red[...], s_cot[:, cols], ((1,), (0,))) * slope).astype(bf16)
        s_gh[:, cols] = gh
        mlp = dot(w_red[...], active, ((0,), (0,)))
        part = dot(w_exp[...], gh, ((1,), (0,)))
        plain = jnp.zeros((1, width), f32)
        cross = jnp.zeros((1, width), f32)
        for k in range(parts):
            at = slice(k * ch, (k + 1) * ch)
            dev = recv[k, 0:ch, cols].astype(f32)
            normed = (dev + (means[k] - centre)) * inverse
            scaled = part[at] * gains[k]
            plain = plain + jnp.sum(scaled, axis=0, keepdims=True)
            cross = cross + jnp.sum(scaled * normed, axis=0, keepdims=True)
            payload[k, 0:ch, cols] = mlp[at].astype(bf16)
            payload[k, ch : 2 * ch, cols] = part[at].astype(bf16)
        sums = jnp.concatenate(
            split3(plain) + split3(cross) + [jnp.zeros((CT - 6, width), f32)], axis=0
        ).astype(bf16)
        for k in range(parts):
            payload[k, 2 * ch : 2 * ch + CT, cols] = sums
    last = ((1,), (1,))
    grad_exp = dot(s_norm[...], s_gh[...], last)
    grad_red = dot(s_act[...], s_cot[...], last)
    n = grad_exp.shape[0]
    grads[0:n, :] = grad_exp[:, 0:LANES]
    grads[n : 2 * n, :] = grad_exp[:, LANES:]
    grads[2 * n : 3 * n, :] = grad_red[:, 0:LANES]
    grads[3 * n : 4 * n, :] = grad_red[:, LANES:]
    halves(grads, send, keep)
    sums = dot(s_gh[...], jnp.ones((pixels, LANES), bf16), ((1,), (0,)))
    table = jnp.zeros((ch, LANES), f32)
    lane = lane_ids(ch)
    for j in range(sums.shape[0] // ch):
        table = jnp.where(lane == OFFSET + j, sums[j * ch : (j + 1) * ch], table)
    off[...] = table


def mlp(recv, w_exp, bias, w_red):
    _, _, pixels = recv.shape
    hid = w_red.shape[0]
    total = w_exp.shape[0]
    return vcall(
        mlp_kernel,
        out_shape=(
            jax.ShapeDtypeStruct(recv.shape, bf16),
            jax.ShapeDtypeStruct((2, pixels), f32),
            jax.ShapeDtypeStruct((2 * total, LANES), f32),
            jax.ShapeDtypeStruct((2 * total, LANES), f32),
            jax.ShapeDtypeStruct(((recv.shape[1] - CT) // 2, LANES), f32),
        ),
        scratch_shapes=[
            pltpu.VMEM((4 * total, LANES), f32),
            pltpu.VMEM((total, pixels), bf16),
            pltpu.VMEM((hid, pixels), bf16),
            pltpu.VMEM((total, pixels), bf16),
            pltpu.VMEM((hid, pixels), bf16),
        ],
        name="mlp",
    )(recv, w_exp, bias, w_red)


def norm_back_kernel(recv, mixed, stats, gain, image, off, result, grad_mixed, rounded, small):
    parts, height, _ = recv.shape
    ch = (height - CT) // 2
    tile_rows = image.shape[0]
    total = parts * ch
    gain_col = column(gain[...], ch)
    acc_gain = jnp.zeros((ch, LANES), f32)
    acc_shift = jnp.zeros((ch, LANES), f32)
    for i in range(tile_rows):
        cols = slice(i * LANES, (i + 1) * LANES)
        mlp_out = jnp.zeros((ch, LANES), f32)
        grad = jnp.zeros((ch, LANES), f32)
        sums = jnp.zeros((CT, LANES), f32)
        for k in range(parts):
            mlp_out = mlp_out + recv[k, 0:ch, cols].astype(f32)
            grad = grad + recv[k, ch : 2 * ch, cols].astype(f32)
            sums = sums + recv[k, 2 * ch : 2 * ch + CT, cols].astype(f32)
        result[i] = (image[i].astype(f32) + mlp_out).astype(bf16)
        plain = (sums[0:1] + sums[1:2] + sums[2:3]) / total
        cross = (sums[3:4] + sums[4:5] + sums[5:6]) / total
        inverse = stats[1:2, cols]
        normed = (mixed[:, cols] - stats[0:1, cols]) * inverse
        acc_gain = acc_gain + grad * normed
        acc_shift = acc_shift + grad
        out = inverse * (grad * gain_col - plain - normed * cross)
        grad_mixed[i] = out
        rounded[i] = out.astype(bf16)
    g = jnp.sum(acc_gain, axis=1, keepdims=True)
    s = jnp.sum(acc_shift, axis=1, keepdims=True)
    lane = lane_ids(ch)
    small[...] = jnp.where(lane == GAIN, g, jnp.where(lane == SHIFT, s, off[...]))


def norm_back(recv, mixed, stats, gain, image, off):
    _, channels, _ = image.shape
    return vcall(
        norm_back_kernel,
        out_shape=(
            jax.ShapeDtypeStruct(image.shape, bf16),
            jax.ShapeDtypeStruct(image.shape, f32),
            jax.ShapeDtypeStruct(image.shape, bf16),
            jax.ShapeDtypeStruct((channels, LANES), f32),
        ),
        name="norm_back",
    )(recv, mixed, stats, gain, image, off)


def tap_grad_kernel(up, mid, down, left, right, grad_mixed, small, *rest):
    pieces, (out, table_ref, total) = rest[:-3], rest[-3:]
    tile_rows, channels, _ = mid.shape
    lane = lane_ids(CT)

    def step(t, carry):
        at = pl.ds(pl.multiple_of(t * CT, CT), CT)
        rows = halo_rows(up, mid, down, left, right, at)
        grads = [grad_mixed[i, at, :] for i in range(tile_rows)]
        table = small[at, :]
        for b in range(KSIZE):
            shifted = [window(row, b - HALF) for row in rows]
            for a in range(KSIZE):
                accum = grads[0] * shifted[a]
                for i in range(1, tile_rows):
                    accum = accum + grads[i] * shifted[a + i]
                value = jnp.sum(accum, axis=1, keepdims=True)
                table = jnp.where(lane == a * KSIZE + b, value, table)
        table_ref[at, :] = table
        return carry

    lax.fori_loop(0, channels // CT, step, 0)
    half = channels // 2
    total[...] = table_ref[0:half, :] + rolled(table_ref[half:channels, :], LANES // 2)
    cols, height, _ = out.shape
    part = pieces[0].shape[0] // cols
    per = total.shape[0] // cols
    for c in range(cols):
        at = slice(c * part, (c + 1) * part)
        out[c, 0:part, :] = sum(x[at, :] for x in pieces)
        out[c, part : part + per, :] = total[c * per : (c + 1) * per, :]
        out[c, part + per :, :] = jnp.zeros((height - part - per, LANES), f32)


def tap_grad(up, mid, down, left, right, grad_mixed, small, pieces, cols):
    channels = mid.shape[1]
    part, per = pieces[0].shape[0] // cols, channels // 2 // cols
    height = part + -(-2 * per // 8) * 8
    return vcall(
        tap_grad_kernel,
        out_shape=jax.ShapeDtypeStruct((cols, height, LANES), f32),
        scratch_shapes=[pltpu.VMEM((channels, LANES), f32), pltpu.VMEM((channels // 2, LANES), f32)],
        name="tap_grad",
    )(up, mid, down, left, right, grad_mixed, small, *pieces)


def backward_kernel(up, mid, down, left, right, kern, cot, out):
    tile_rows, channels, _ = mid.shape

    def step(t, carry):
        at = pl.ds(pl.multiple_of(t * CT, CT), CT)
        rows = halo_rows(up, mid, down, left, right, at)
        accum = accumulate_taps(rows, kern, at, True)
        for i in range(tile_rows):
            out[i, at, :] = (cot[i, at, :].astype(f32) + accum[i]).astype(bf16)
        return carry

    lax.fori_loop(0, channels // CT, step, 0)


def backward(up, mid, down, left, right, kern, cot):
    return vcall(
        backward_kernel,
        out_shape=jax.ShapeDtypeStruct(cot.shape, bf16),
        name="backward",
    )(up, mid, down, left, right, kern, cot)


def hi_lo(x):
    hi = x.astype(bf16).astype(f32)
    return jnp.concatenate([hi, x - hi], axis=0)


def col_pack_kernel(per, recv, out):
    total = recv[0]
    for c in range(1, recv.shape[0]):
        total = total + recv[c]
    part = total.shape[0] - -(-2 * per // 8) * 8
    tail = hi_lo(total[part : part + per])
    pad = total.shape[0] - part - 2 * per
    pieces = [total[0:part], tail] + ([jnp.zeros((pad, LANES), f32)] if pad else [])
    tile = jnp.concatenate(pieces, axis=0).astype(bf16)
    for c in range(out.shape[0]):
        out[c] = tile


def col_pack(recv, per):
    return vcall(
        functools.partial(col_pack_kernel, per),
        out_shape=jax.ShapeDtypeStruct(recv.shape, bf16),
        name="col_pack",
    )(recv)


def row_pack_kernel(per, recv, out, tile):
    cols, height, _ = recv.shape
    part = height - -(-2 * per // 8) * 8
    base, size = cols * part, cols * per
    for c in range(cols):
        x = recv[c].astype(f32)
        tile[c * part : (c + 1) * part, :] = x[0:part]
        tile[base + c * per : base + (c + 1) * per, :] = x[part : part + per]
        low = base + size + c * per
        tile[low : low + per, :] = x[part + per : part + 2 * per]
    x = tile[...].astype(bf16)
    for r in range(out.shape[0]):
        out[r] = x


def row_pack(recv, rows, per):
    cols, height, _ = recv.shape
    tall = cols * (height - -(-2 * per // 8) * 8 + 2 * per)
    return vcall(
        functools.partial(row_pack_kernel, per),
        out_shape=jax.ShapeDtypeStruct((rows, tall, LANES), bf16),
        scratch_shapes=[pltpu.VMEM((tall, LANES), f32)],
        name="row_pack",
    )(recv)


def final_kernel(scale, flat, exp_ref, red_ref, taps_ref, gain_ref, shift_ref, off_ref):
    rows = flat.shape[0]
    n = exp_ref.shape[0]
    per = taps_ref.shape[1] // 2
    size_all = 4 * n // rows
    for r in range(rows):
        x = flat[r].astype(f32) * scale
        block = x[0:size_all]
        tail = x[size_all : size_all + per] + x[size_all + per : size_all + 2 * per]
        total = tail if r == 0 else total + tail
        start = row_chunk(r, rows) * size_all
        lo = 0
        while lo < size_all:
            which, at = divmod(start + lo, n)
            size = min(size_all - lo, n - at)
            ref = (exp_ref, red_ref)[which // 2]
            lane = (which % 2) * LANES
            ref[at : at + size, lane : lane + LANES] = block[lo : lo + size]
            lo += size
    x = total
    both = jnp.concatenate([x, rolled(x, LANES // 2)], axis=0)
    wide = jnp.concatenate([both, jnp.zeros((LANES - both.shape[0], LANES), f32)], axis=0)
    flip = jnp.transpose(wide)[:, 0 : both.shape[0]]
    taps_ref[...] = flip[0 : taps_ref.shape[0], :]
    gain_ref[...] = flip[GAIN : GAIN + 1]
    shift_ref[...] = flip[SHIFT : SHIFT + 1]
    channels = flip.shape[1]
    for j in range(off_ref.shape[1] // channels):
        off_ref[:, j * channels : (j + 1) * channels] = flip[OFFSET + j : OFFSET + j + 1]


def final(flat, scale, total, hid, channels, taps):
    return vcall(
        functools.partial(final_kernel, scale),
        out_shape=(
            jax.ShapeDtypeStruct((total, hid), f32),
            jax.ShapeDtypeStruct((hid, total), f32),
            jax.ShapeDtypeStruct((taps, channels), f32),
            jax.ShapeDtypeStruct((1, channels), f32),
            jax.ShapeDtypeStruct((1, channels), f32),
            jax.ShapeDtypeStruct((1, hid), f32),
        ),
        name="final",
    )(flat)


def neighbours(first, last, axis):
    size = lax.axis_size(axis)
    up = [(i, i + 1) for i in range(size - 1)]
    down = [(j, i) for i, j in up]
    return lax.ppermute(last, axis, up), lax.ppermute(first, axis, down)


def halo(x):
    rows = x.shape[0]
    up, down = neighbours(x[:HALF], x[rows - HALF :], "row")
    first, last = edges(up, x, down)
    left, right = neighbours(first, last, "col")
    return up, down, left, right


def exchange(x, axis):
    return lax.all_to_all(x, axis, 0, 0)


def reduce_cols(part, per):
    part = exchange(part, "col")
    flat = exchange(col_pack(part, per), "col")
    return exchange(row_pack(flat, lax.axis_size("row"), per), "row")


def body(
    image, depth_kernel, norm_gain, norm_shift, expand_weight, expand_bias, reduce_weight, cotangent
):
    channels, tile_rows, tile_cols = image.shape
    pixels = tile_rows * tile_cols
    parts = lax.axis_size("ch")
    hid = reduce_weight.shape[0]
    total = expand_weight.shape[0]
    img = jnp.transpose(image, (1, 0, 2))
    cot = jnp.transpose(cotangent, (1, 0, 2))
    gain = norm_gain.reshape(1, channels)
    shift = norm_shift.reshape(1, channels)
    bias = lax.dynamic_slice_in_dim(expand_bias, lax.axis_index("ch") * hid, hid).reshape(1, hid)
    up, down, left, right = halo(img)
    mixed, send = forward(up, img, down, left, right, depth_kernel, gain, shift, cot, parts)
    recv = exchange(send, "ch")
    send, stats, give, keep, off = mlp(recv, expand_weight, bias, reduce_weight)
    recv = exchange(send, "ch")
    pieces = reduce_rows(give, keep)
    result, grad_mixed, rounded, small = norm_back(recv, mixed, stats, gain, img, off)
    g_up, g_down, g_left, g_right = halo(rounded)
    cols = lax.axis_size("col")
    part = tap_grad(up, img, down, left, right, grad_mixed, small, pieces, cols)
    grad_image = backward(g_up, rounded, g_down, g_left, g_right, depth_kernel, cot)
    flat = reduce_cols(part, channels // 2 // cols)
    pixels_all = pixels * lax.axis_size("row") * lax.axis_size("col")
    scale = float(pixels_all) ** (-0.5)
    grad_exp, grad_red, grad_taps, grad_gain, grad_shift, grad_off = final(
        flat, scale, total, hid, channels, depth_kernel.shape[1]
    )
    return (
        jnp.transpose(result, (1, 0, 2)),
        jnp.transpose(grad_image, (1, 0, 2)),
        jnp.transpose(grad_taps),
        grad_gain.reshape(channels),
        grad_shift.reshape(channels),
        grad_exp,
        grad_off.reshape(hid),
        grad_red,
    )


def solution(mesh):
    in_specs = (
        P("ch", "row", "col"),
        P("ch", None),
        P("ch"),
        P("ch"),
        P(None, "ch"),
        P(),
        P("ch", None),
        P("ch", "row", "col"),
    )
    out_specs = (
        P("ch", "row", "col"),
        P("ch", "row", "col"),
        P("ch", None),
        P("ch"),
        P("ch"),
        P(None, "ch"),
        P("ch"),
        P("ch", None),
    )

    return jax.shard_map(body, mesh=mesh, in_specs=in_specs, out_specs=out_specs, check_vma=False)
```

```python
import functools
import jax
import jax.numpy as jnp
from jax import lax
from jax.experimental import pallas as pl
from jax.experimental.pallas import tpu as pltpu
from jax.sharding import PartitionSpec as P

KSIZE = 7
HALF = 3
SPAN = KSIZE + HALF
epsilon = 1e-06
root_two_pi = 0.7978845608028654
cubic_coef = 0.044715
f32 = jnp.float32
bf16 = jnp.bfloat16
LANES = 128
CT = 16
GAIN = KSIZE * KSIZE
SHIFT = GAIN + 1
OFFSET = GAIN + 2


def vcall(kernel, out_shape, **kw):
    spec = pl.BlockSpec(memory_space=pltpu.VMEM)

    def call(*args):
        return pl.pallas_call(
            kernel,
            out_shape=out_shape,
            in_specs=[spec] * len(args),
            out_specs=jax.tree.map(lambda _: spec, out_shape),
            compiler_params=pltpu.CompilerParams(vmem_limit_bytes=8 << 20),
            **kw,
        )(*args)

    return call


def lane_ids(rows):
    return lax.broadcasted_iota(jnp.int32, (rows, LANES), 1)


def rolled(x, shift):
    shift = shift % LANES
    return x if shift == 0 else pltpu.roll(x, shift, 1)


def split3(x):
    hi = x.astype(bf16)
    rest = x - hi.astype(f32)
    mid = rest.astype(bf16)
    low = (rest - mid.astype(f32)).astype(bf16)
    return [hi.astype(f32), mid.astype(f32), low.astype(f32)]


def gelu_pair(hidden):
    inner = root_two_pi * (hidden + cubic_coef * hidden * hidden * hidden)
    tangent = jnp.tanh(inner)
    value = 0.5 * hidden * (1.0 + tangent)
    slope = 0.5 * (1.0 + tangent) + 0.5 * hidden * (1.0 - tangent * tangent) * root_two_pi * (
        1.0 + 3.0 * cubic_coef * hidden * hidden
    )
    return (value, slope)


def halo_rows(up, mid, down, left, right, at):
    lane = lane_ids(CT)
    l = left[at, :].astype(f32)
    r = right[at, :].astype(f32)
    rows = []
    for i in range(SPAN):
        if i < HALF:
            x = up[i, at, :]
        elif i < SPAN - HALF:
            x = mid[i - HALF, at, :]
        else:
            x = down[i - (SPAN - HALF), at, :]
        edge = jnp.where(
            lane >= 64, rolled(l, LANES - HALF - HALF * i), rolled(r, LANES - HALF * i)
        )
        rows.append((x.astype(f32), edge))
    return rows


def window(row, s):
    x, edge = row
    if s == 0:
        return x
    lane = lane_ids(CT)
    mask = (lane < -s) if s < 0 else (lane >= LANES - s)
    return jnp.where(mask, rolled(edge, -s), rolled(x, -s))


def edges_kernel(up, mid, down, gain, shift, first, last, both):
    both[...] = jnp.concatenate([gain[...], shift[...]], axis=1)
    channels = mid.shape[1]
    lane = lane_ids(CT)

    def step(t, carry):
        at = pl.ds(pl.multiple_of(t * CT, CT), CT)
        head = jnp.zeros((CT, LANES), f32)
        tail = jnp.zeros((CT, LANES), f32)
        for i in range(SPAN):
            if i < HALF:
                x = up[i, at, :]
            elif i < SPAN - HALF:
                x = mid[i - HALF, at, :]
            else:
                x = down[i - (SPAN - HALF), at, :]
            x = x.astype(f32)
            mask = (lane >= HALF * i) & (lane < HALF * i + HALF)
            head = jnp.where(mask, rolled(x, HALF * i), head)
            tail = jnp.where(mask, rolled(x, HALF * i + HALF), tail)
        first[at, :] = head.astype(bf16)
        last[at, :] = tail.astype(bf16)
        return carry

    lax.fori_loop(0, channels // CT, step, 0)


def edges(up, mid, down, gain, shift):
    channels = mid.shape[1]
    shape = jax.ShapeDtypeStruct((channels, LANES), bf16)
    return vcall(
        edges_kernel,
        out_shape=(shape, shape, jax.ShapeDtypeStruct((1, 2 * channels), f32)),
        name="edges",
    )(up, mid, down, gain, shift)


def accumulate_taps(rows, kern, at, flip):
    accum = [jnp.zeros((CT, LANES), f32) for _ in range(SPAN - KSIZE + 1)]
    weights = kern[at, :]
    for b in range(KSIZE):
        shifted = [window(row, b - HALF) for row in rows]
        for a in range(KSIZE):
            tap = a * KSIZE + b
            if flip:
                tap = KSIZE * KSIZE - 1 - tap
            w = jnp.broadcast_to(weights[:, tap : tap + 1], (CT, LANES))
            for i in range(len(accum)):
                accum[i] = accum[i] + w * shifted[i + a]
    return accum


def forward_kernel(up, mid, down, left, right, kern, affine, cot, mixed, payload):
    tile_rows, channels, _ = mid.shape

    def step(t, carry):
        at = pl.ds(pl.multiple_of(t * CT, CT), CT)
        rows = halo_rows(up, mid, down, left, right, at)
        accum = accumulate_taps(rows, kern, at, False)
        for i in range(tile_rows):
            mixed[at, i * LANES : (i + 1) * LANES] = accum[i]
        return carry

    lax.fori_loop(0, channels // CT, step, 0)
    for i in range(tile_rows):
        cols = slice(i * LANES, (i + 1) * LANES)
        x = mixed[:, cols]
        mean = jnp.sum(x, axis=0, keepdims=True) / channels
        dev = x - mean
        spread = jnp.sum(dev * dev, axis=0, keepdims=True)
        rows = split3(mean) + split3(spread)
        stats = jnp.concatenate(rows + [jnp.zeros((CT - 6, LANES), f32)], axis=0)
        if i == 0:
            row_id = lax.broadcasted_iota(jnp.int32, (CT, LANES), 0)
            for k, part in enumerate(split3(affine[...])):
                stats = jnp.where(row_id == 6 + k, jnp.broadcast_to(part, (CT, LANES)), stats)
        dev = dev.astype(bf16)
        stats = stats.astype(bf16)
        for d in range(payload.shape[0]):
            payload[d, 0:channels, cols] = dev
            payload[d, channels : 2 * channels, cols] = cot[i]
            payload[d, 2 * channels : 2 * channels + CT, cols] = stats


def forward(up, mid, down, left, right, kern, affine, cot, parts):
    tile_rows, channels, _ = mid.shape
    pixels = tile_rows * LANES
    return vcall(
        forward_kernel,
        out_shape=(
            jax.ShapeDtypeStruct((channels, pixels), f32),
            jax.ShapeDtypeStruct((parts, 2 * channels + CT, pixels), bf16),
        ),
        name="forward",
    )(up, mid, down, left, right, kern, affine, cot)


def column(row, n):
    i = lax.broadcasted_iota(jnp.int32, (n, n), 0)
    j = lax.broadcasted_iota(jnp.int32, (n, n), 1)
    return jnp.sum(jnp.where(i == j, jnp.broadcast_to(row, (n, n)), 0.0), axis=1, keepdims=True)


def dot(a, b, dims):
    return lax.dot_general(a, b, (dims, ((), ())), preferred_element_type=f32)


def row_chunk(r, size):
    return (r % 2) * (size // 2) + r // 2


def halves(ref, send, keep):
    n = send.shape[0]
    bit = lax.axis_index("row") % 2
    send[...] = ref[pl.ds(pl.multiple_of((1 - bit) * n, n), n), :]
    keep[...] = ref[pl.ds(pl.multiple_of(bit * n, n), n), :]


def spread_kernel(x, recv, *rest):
    outs, total = rest[:-1], rest[-1]
    total[...] = x[...] + recv[...]
    n = outs[0].shape[0]
    y = lax.axis_index("row") // 2
    for m, out in enumerate(outs):
        low, high = y % 2, y // 2
        low = 1 - low if m % 2 else low
        high = 1 - high if m // 2 else high
        out[...] = total[pl.ds(pl.multiple_of((2 * high + low) * n, n), n), :].astype(out.dtype)


def spread(x, recv, parts):
    shape = (x.shape[0] // parts, LANES)
    return vcall(
        spread_kernel,
        out_shape=tuple(jax.ShapeDtypeStruct(shape, bf16 if m else f32) for m in range(parts)),
        scratch_shapes=[pltpu.VMEM(x.shape, f32)],
        name="spread",
    )(x, recv)


def reduce_rows(send, keep):
    size = lax.axis_size("row")
    recv = lax.ppermute(send, "row", [(i, i ^ 1) for i in range(size)])
    if size == 2:
        return [keep, recv]
    chunks = spread(keep, recv, size // 2)
    return [chunks[0]] + [
        lax.ppermute(chunks[m], "row", [(i, i ^ (2 * m)) for i in range(size)])
        for m in range(1, size // 2)
    ]


def mlp_kernel(recv, w_exp, bias, w_red, payload, stats_out, send, keep, off, grads, s_norm, s_act, s_cot, s_gh):
    parts, height, pixels = recv.shape
    ch = (height - CT) // 2
    total = parts * ch
    width = 2 * LANES
    gains, shifts = [], []
    for k in range(parts):
        head = recv[k, 2 * ch : 2 * ch + CT, 0:LANES].astype(f32)
        both = head[6:7] + head[7:8] + head[8:9]
        gains.append(column(both[:, 0:ch], ch))
        shifts.append(column(both[:, ch : 2 * ch], ch))
    bias_col = column(bias[...], bias.shape[1])
    for blk in range(pixels // width):
        cols = slice(blk * width, (blk + 1) * width)
        means, spreads = [], []
        for k in range(parts):
            st = recv[k, 2 * ch : 2 * ch + CT, cols].astype(f32)
            means.append(st[0:1] + st[1:2] + st[2:3])
            spreads.append(st[3:4] + st[4:5] + st[5:6])
        centre = sum(means) / parts
        spread = sum(spreads)
        for k in range(parts):
            gap = means[k] - centre
            spread = spread + ch * gap * gap
        inverse = lax.rsqrt(spread / total + epsilon)
        stats_out[0:1, cols] = centre
        stats_out[1:2, cols] = inverse
        for k in range(parts):
            at = slice(k * ch, (k + 1) * ch)
            dev = recv[k, 0:ch, cols].astype(f32)
            normed = (dev + (means[k] - centre)) * inverse
            s_norm[at, cols] = (normed * gains[k] + shifts[k]).astype(bf16)
            s_cot[at, cols] = recv[k, ch : 2 * ch, cols]
        hidden = dot(w_exp[...], s_norm[:, cols], ((0,), (0,))) + bias_col
        value, slope = gelu_pair(hidden)
        active = value.astype(bf16)
        s_act[:, cols] = active
        gh = (dot(w_red[...], s_cot[:, cols], ((1,), (0,))) * slope).astype(bf16)
        s_gh[:, cols] = gh
        mlp = dot(w_red[...], active, ((0,), (0,)))
        part = dot(w_exp[...], gh, ((1,), (0,)))
        plain = jnp.zeros((1, width), f32)
        cross = jnp.zeros((1, width), f32)
        for k in range(parts):
            at = slice(k * ch, (k + 1) * ch)
            dev = recv[k, 0:ch, cols].astype(f32)
            normed = (dev + (means[k] - centre)) * inverse
            scaled = part[at] * gains[k]
            plain = plain + jnp.sum(scaled, axis=0, keepdims=True)
            cross = cross + jnp.sum(scaled * normed, axis=0, keepdims=True)
            payload[k, 0:ch, cols] = mlp[at].astype(bf16)
            payload[k, ch : 2 * ch, cols] = part[at].astype(bf16)
        sums = jnp.concatenate(
            split3(plain) + split3(cross) + [jnp.zeros((CT - 6, width), f32)], axis=0
        ).astype(bf16)
        for k in range(parts):
            payload[k, 2 * ch : 2 * ch + CT, cols] = sums
    last = ((1,), (1,))
    grad_exp = dot(s_norm[...], s_gh[...], last)
    grad_red = dot(s_act[...], s_cot[...], last)
    n = grad_exp.shape[0]
    grads[0:n, :] = grad_exp[:, 0:LANES]
    grads[n : 2 * n, :] = grad_exp[:, LANES:]
    grads[2 * n : 3 * n, :] = grad_red[:, 0:LANES]
    grads[3 * n : 4 * n, :] = grad_red[:, LANES:]
    halves(grads, send, keep)
    sums = dot(s_gh[...], jnp.ones((pixels, LANES), bf16), ((1,), (0,)))
    table = jnp.zeros((ch, LANES), f32)
    lane = lane_ids(ch)
    for j in range(sums.shape[0] // ch):
        table = jnp.where(lane == OFFSET + j, sums[j * ch : (j + 1) * ch], table)
    off[...] = table


def mlp(recv, w_exp, bias, w_red):
    _, _, pixels = recv.shape
    hid = w_red.shape[0]
    total = w_exp.shape[0]
    return vcall(
        mlp_kernel,
        out_shape=(
            jax.ShapeDtypeStruct(recv.shape, bf16),
            jax.ShapeDtypeStruct((2, pixels), f32),
            jax.ShapeDtypeStruct((2 * total, LANES), f32),
            jax.ShapeDtypeStruct((2 * total, LANES), f32),
            jax.ShapeDtypeStruct(((recv.shape[1] - CT) // 2, LANES), f32),
        ),
        scratch_shapes=[
            pltpu.VMEM((4 * total, LANES), f32),
            pltpu.VMEM((total, pixels), bf16),
            pltpu.VMEM((hid, pixels), bf16),
            pltpu.VMEM((total, pixels), bf16),
            pltpu.VMEM((hid, pixels), bf16),
        ],
        name="mlp",
    )(recv, w_exp, bias, w_red)


def norm_back_kernel(recv, mixed, stats, gain, image, off, result, grad_mixed, rounded, small):
    parts, height, _ = recv.shape
    ch = (height - CT) // 2
    tile_rows = image.shape[0]
    total = parts * ch
    gain_col = column(gain[...], ch)
    acc_gain = jnp.zeros((ch, LANES), f32)
    acc_shift = jnp.zeros((ch, LANES), f32)
    for i in range(tile_rows):
        cols = slice(i * LANES, (i + 1) * LANES)
        mlp_out = jnp.zeros((ch, LANES), f32)
        grad = jnp.zeros((ch, LANES), f32)
        sums = jnp.zeros((CT, LANES), f32)
        for k in range(parts):
            mlp_out = mlp_out + recv[k, 0:ch, cols].astype(f32)
            grad = grad + recv[k, ch : 2 * ch, cols].astype(f32)
            sums = sums + recv[k, 2 * ch : 2 * ch + CT, cols].astype(f32)
        result[i] = (image[i].astype(f32) + mlp_out).astype(bf16)
        plain = (sums[0:1] + sums[1:2] + sums[2:3]) / total
        cross = (sums[3:4] + sums[4:5] + sums[5:6]) / total
        inverse = stats[1:2, cols]
        normed = (mixed[:, cols] - stats[0:1, cols]) * inverse
        acc_gain = acc_gain + grad * normed
        acc_shift = acc_shift + grad
        out = inverse * (grad * gain_col - plain - normed * cross)
        grad_mixed[i] = out
        rounded[i] = out.astype(bf16)
    g = jnp.sum(acc_gain, axis=1, keepdims=True)
    s = jnp.sum(acc_shift, axis=1, keepdims=True)
    lane = lane_ids(ch)
    small[...] = jnp.where(lane == GAIN, g, jnp.where(lane == SHIFT, s, off[...]))


def norm_back(recv, mixed, stats, gain, image, off):
    _, channels, _ = image.shape
    return vcall(
        norm_back_kernel,
        out_shape=(
            jax.ShapeDtypeStruct(image.shape, bf16),
            jax.ShapeDtypeStruct(image.shape, f32),
            jax.ShapeDtypeStruct(image.shape, bf16),
            jax.ShapeDtypeStruct((channels, LANES), f32),
        ),
        name="norm_back",
    )(recv, mixed, stats, gain, image, off)


def tap_grad_kernel(up, mid, down, left, right, grad_mixed, small, *rest):
    pieces, (out, table_ref, total) = rest[:-3], rest[-3:]
    tile_rows, channels, _ = mid.shape
    lane = lane_ids(CT)

    def step(t, carry):
        at = pl.ds(pl.multiple_of(t * CT, CT), CT)
        rows = halo_rows(up, mid, down, left, right, at)
        grads = [grad_mixed[i, at, :] for i in range(tile_rows)]
        table = small[at, :]
        for b in range(KSIZE):
            shifted = [window(row, b - HALF) for row in rows]
            for a in range(KSIZE):
                accum = grads[0] * shifted[a]
                for i in range(1, tile_rows):
                    accum = accum + grads[i] * shifted[a + i]
                value = jnp.sum(accum, axis=1, keepdims=True)
                table = jnp.where(lane == a * KSIZE + b, value, table)
        table_ref[at, :] = table
        return carry

    lax.fori_loop(0, channels // CT, step, 0)
    half = channels // 2
    total[...] = table_ref[0:half, :] + rolled(table_ref[half:channels, :], LANES // 2)
    cols, height, _ = out.shape
    part = pieces[0].shape[0] // cols
    per = total.shape[0] // cols
    for c in range(cols):
        at = slice(c * part, (c + 1) * part)
        out[c, 0:part, :] = sum(x[at, :].astype(f32) for x in pieces)
        out[c, part : part + per, :] = total[c * per : (c + 1) * per, :]
        out[c, part + per :, :] = jnp.zeros((height - part - per, LANES), f32)


def tap_grad(up, mid, down, left, right, grad_mixed, small, pieces, cols):
    channels = mid.shape[1]
    part, per = pieces[0].shape[0] // cols, channels // 2 // cols
    height = part + -(-2 * per // 8) * 8
    return vcall(
        tap_grad_kernel,
        out_shape=jax.ShapeDtypeStruct((cols, height, LANES), f32),
        scratch_shapes=[pltpu.VMEM((channels, LANES), f32), pltpu.VMEM((channels // 2, LANES), f32)],
        name="tap_grad",
    )(up, mid, down, left, right, grad_mixed, small, *pieces)


def backward_kernel(up, mid, down, left, right, kern, cot, out):
    tile_rows, channels, _ = mid.shape

    def step(t, carry):
        at = pl.ds(pl.multiple_of(t * CT, CT), CT)
        rows = halo_rows(up, mid, down, left, right, at)
        accum = accumulate_taps(rows, kern, at, True)
        for i in range(tile_rows):
            out[i, at, :] = (cot[i, at, :].astype(f32) + accum[i]).astype(bf16)
        return carry

    lax.fori_loop(0, channels // CT, step, 0)


def backward(up, mid, down, left, right, kern, cot):
    return vcall(
        backward_kernel,
        out_shape=jax.ShapeDtypeStruct(cot.shape, bf16),
        name="backward",
    )(up, mid, down, left, right, kern, cot)


def hi_lo(x):
    hi = x.astype(bf16).astype(f32)
    return jnp.concatenate([hi, x - hi], axis=0)


def col_pack_kernel(per, recv, out):
    total = recv[0]
    for c in range(1, recv.shape[0]):
        total = total + recv[c]
    part = total.shape[0] - -(-2 * per // 8) * 8
    tail = hi_lo(total[part : part + per])
    pad = total.shape[0] - part - 2 * per
    pieces = [total[0:part], tail] + ([jnp.zeros((pad, LANES), f32)] if pad else [])
    tile = jnp.concatenate(pieces, axis=0).astype(bf16)
    for c in range(out.shape[0]):
        out[c] = tile


def col_pack(recv, per):
    return vcall(
        functools.partial(col_pack_kernel, per),
        out_shape=jax.ShapeDtypeStruct(recv.shape, bf16),
        name="col_pack",
    )(recv)


def row_pack_kernel(per, recv, out, tile):
    cols, height, _ = recv.shape
    part = height - -(-2 * per // 8) * 8
    base, size = cols * part, cols * per
    for c in range(cols):
        x = recv[c].astype(f32)
        tile[c * part : (c + 1) * part, :] = x[0:part]
        tile[base + c * per : base + (c + 1) * per, :] = x[part : part + per]
        low = base + size + c * per
        tile[low : low + per, :] = x[part + per : part + 2 * per]
    x = tile[...].astype(bf16)
    for r in range(out.shape[0]):
        out[r] = x


def row_pack(recv, rows, per):
    cols, height, _ = recv.shape
    tall = cols * (height - -(-2 * per // 8) * 8 + 2 * per)
    return vcall(
        functools.partial(row_pack_kernel, per),
        out_shape=jax.ShapeDtypeStruct((rows, tall, LANES), bf16),
        scratch_shapes=[pltpu.VMEM((tall, LANES), f32)],
        name="row_pack",
    )(recv)


def final_kernel(scale, flat, exp_ref, red_ref, taps_ref, gain_ref, shift_ref, off_ref):
    rows = flat.shape[0]
    n = exp_ref.shape[0]
    per = taps_ref.shape[1] // 2
    size_all = 4 * n // rows
    for r in range(rows):
        x = flat[r].astype(f32) * scale
        block = x[0:size_all]
        tail = x[size_all : size_all + per] + x[size_all + per : size_all + 2 * per]
        total = tail if r == 0 else total + tail
        start = row_chunk(r, rows) * size_all
        lo = 0
        while lo < size_all:
            which, at = divmod(start + lo, n)
            size = min(size_all - lo, n - at)
            ref = (exp_ref, red_ref)[which // 2]
            lane = (which % 2) * LANES
            ref[at : at + size, lane : lane + LANES] = block[lo : lo + size]
            lo += size
    x = total
    both = jnp.concatenate([x, rolled(x, LANES // 2)], axis=0)
    wide = jnp.concatenate([both, jnp.zeros((LANES - both.shape[0], LANES), f32)], axis=0)
    flip = jnp.transpose(wide)[:, 0 : both.shape[0]]
    taps_ref[...] = flip[0 : taps_ref.shape[0], :]
    gain_ref[...] = flip[GAIN : GAIN + 1]
    shift_ref[...] = flip[SHIFT : SHIFT + 1]
    channels = flip.shape[1]
    for j in range(off_ref.shape[1] // channels):
        off_ref[:, j * channels : (j + 1) * channels] = flip[OFFSET + j : OFFSET + j + 1]


def final(flat, scale, total, hid, channels, taps):
    return vcall(
        functools.partial(final_kernel, scale),
        out_shape=(
            jax.ShapeDtypeStruct((total, hid), f32),
            jax.ShapeDtypeStruct((hid, total), f32),
            jax.ShapeDtypeStruct((taps, channels), f32),
            jax.ShapeDtypeStruct((1, channels), f32),
            jax.ShapeDtypeStruct((1, channels), f32),
            jax.ShapeDtypeStruct((1, hid), f32),
        ),
        name="final",
    )(flat)


def neighbours(first, last, axis):
    size = lax.axis_size(axis)
    up = [(i, i + 1) for i in range(size - 1)]
    down = [(j, i) for i, j in up]
    return lax.ppermute(last, axis, up), lax.ppermute(first, axis, down)


def halo(x, gain, shift):
    rows = x.shape[0]
    up, down = neighbours(x[:HALF], x[rows - HALF :], "row")
    first, last, both = edges(up, x, down, gain, shift)
    left, right = neighbours(first, last, "col")
    return up, down, left, right, both


def exchange(x, axis):
    return lax.all_to_all(x, axis, 0, 0)


def reduce_cols(part, per):
    part = exchange(part, "col")
    flat = exchange(col_pack(part, per), "col")
    return exchange(row_pack(flat, lax.axis_size("row"), per), "row")


def body(
    image, depth_kernel, norm_gain, norm_shift, expand_weight, expand_bias, reduce_weight, cotangent
):
    channels, tile_rows, tile_cols = image.shape
    pixels = tile_rows * tile_cols
    parts = lax.axis_size("ch")
    hid = reduce_weight.shape[0]
    total = expand_weight.shape[0]
    img = jnp.transpose(image, (1, 0, 2))
    cot = jnp.transpose(cotangent, (1, 0, 2))
    gain = norm_gain.reshape(1, channels)
    shift = norm_shift.reshape(1, channels)
    bias = lax.dynamic_slice_in_dim(expand_bias, lax.axis_index("ch") * hid, hid).reshape(1, hid)
    up, down, left, right, affine = halo(img, gain, shift)
    mixed, send = forward(up, img, down, left, right, depth_kernel, affine, cot, parts)
    recv = exchange(send, "ch")
    send, stats, give, keep, off = mlp(recv, expand_weight, bias, reduce_weight)
    recv = exchange(send, "ch")
    pieces = reduce_rows(give, keep)
    result, grad_mixed, rounded, small = norm_back(recv, mixed, stats, gain, img, off)
    g_up, g_down, g_left, g_right, _ = halo(rounded, gain, shift)
    cols = lax.axis_size("col")
    part = tap_grad(up, img, down, left, right, grad_mixed, small, pieces, cols)
    grad_image = backward(g_up, rounded, g_down, g_left, g_right, depth_kernel, cot)
    flat = reduce_cols(part, channels // 2 // cols)
    pixels_all = pixels * lax.axis_size("row") * lax.axis_size("col")
    scale = float(pixels_all) ** (-0.5)
    grad_exp, grad_red, grad_taps, grad_gain, grad_shift, grad_off = final(
        flat, scale, total, hid, channels, depth_kernel.shape[1]
    )
    return (
        jnp.transpose(result, (1, 0, 2)),
        jnp.transpose(grad_image, (1, 0, 2)),
        jnp.transpose(grad_taps),
        grad_gain.reshape(channels),
        grad_shift.reshape(channels),
        grad_exp,
        grad_off.reshape(hid),
        grad_red,
    )


def solution(mesh):
    in_specs = (
        P("ch", "row", "col"),
        P("ch", None),
        P("ch"),
        P("ch"),
        P(None, "ch"),
        P(),
        P("ch", None),
        P("ch", "row", "col"),
    )
    out_specs = (
        P("ch", "row", "col"),
        P("ch", "row", "col"),
        P("ch", None),
        P("ch"),
        P("ch"),
        P(None, "ch"),
        P("ch"),
        P("ch", None),
    )

    return jax.shard_map(body, mesh=mesh, in_specs=in_specs, out_specs=out_specs, check_vma=False)
```

```python
import functools
import jax
import jax.numpy as jnp
from jax import lax
from jax.experimental import pallas as pl
from jax.experimental.pallas import tpu as pltpu
from jax.sharding import PartitionSpec as P

KSIZE = 7
HALF = 3
SPAN = KSIZE + HALF
epsilon = 1e-06
root_two_pi = 0.7978845608028654
cubic_coef = 0.044715
f32 = jnp.float32
bf16 = jnp.bfloat16
LANES = 128
CT = 16
GAIN = KSIZE * KSIZE
SHIFT = GAIN + 1
OFFSET = GAIN + 2


def vcall(kernel, out_shape, **kw):
    spec = pl.BlockSpec(memory_space=pltpu.VMEM)

    def call(*args):
        return pl.pallas_call(
            kernel,
            out_shape=out_shape,
            in_specs=[spec] * len(args),
            out_specs=jax.tree.map(lambda _: spec, out_shape),
            compiler_params=pltpu.CompilerParams(vmem_limit_bytes=8 << 20),
            **kw,
        )(*args)

    return call


def lane_ids(rows):
    return lax.broadcasted_iota(jnp.int32, (rows, LANES), 1)


def rolled(x, shift):
    shift = shift % LANES
    return x if shift == 0 else pltpu.roll(x, shift, 1)


def split3(x):
    hi = x.astype(bf16)
    rest = x - hi.astype(f32)
    mid = rest.astype(bf16)
    low = (rest - mid.astype(f32)).astype(bf16)
    return [hi.astype(f32), mid.astype(f32), low.astype(f32)]


def gelu_pair(hidden):
    inner = root_two_pi * (hidden + cubic_coef * hidden * hidden * hidden)
    tangent = jnp.tanh(inner)
    value = 0.5 * hidden * (1.0 + tangent)
    slope = 0.5 * (1.0 + tangent) + 0.5 * hidden * (1.0 - tangent * tangent) * root_two_pi * (
        1.0 + 3.0 * cubic_coef * hidden * hidden
    )
    return (value, slope)


def halo_rows(up, mid, down, left, right, at):
    lane = lane_ids(CT)
    l = left[at, :].astype(f32)
    r = right[at, :].astype(f32)
    rows = []
    for i in range(SPAN):
        if i < HALF:
            x = up[i, at, :]
        elif i < SPAN - HALF:
            x = mid[i - HALF, at, :]
        else:
            x = down[i - (SPAN - HALF), at, :]
        edge = jnp.where(
            lane >= 64, rolled(l, LANES - HALF - HALF * i), rolled(r, LANES - HALF * i)
        )
        rows.append((x.astype(f32), edge))
    return rows


def window(row, s):
    x, edge = row
    if s == 0:
        return x
    lane = lane_ids(CT)
    mask = (lane < -s) if s < 0 else (lane >= LANES - s)
    return jnp.where(mask, rolled(edge, -s), rolled(x, -s))


def edges_kernel(up, mid, down, gain, shift, first, last, both):
    both[...] = jnp.concatenate([gain[...], shift[...]], axis=1)
    channels = mid.shape[1]
    lane = lane_ids(CT)

    def step(t, carry):
        at = pl.ds(pl.multiple_of(t * CT, CT), CT)
        head = jnp.zeros((CT, LANES), f32)
        tail = jnp.zeros((CT, LANES), f32)
        for i in range(SPAN):
            if i < HALF:
                x = up[i, at, :]
            elif i < SPAN - HALF:
                x = mid[i - HALF, at, :]
            else:
                x = down[i - (SPAN - HALF), at, :]
            x = x.astype(f32)
            mask = (lane >= HALF * i) & (lane < HALF * i + HALF)
            head = jnp.where(mask, rolled(x, HALF * i), head)
            tail = jnp.where(mask, rolled(x, HALF * i + HALF), tail)
        first[at, :] = head.astype(bf16)
        last[at, :] = tail.astype(bf16)
        return carry

    lax.fori_loop(0, channels // CT, step, 0)


def edges(up, mid, down, gain, shift):
    channels = mid.shape[1]
    shape = jax.ShapeDtypeStruct((channels, LANES), bf16)
    return vcall(
        edges_kernel,
        out_shape=(shape, shape, jax.ShapeDtypeStruct((1, 2 * channels), f32)),
        name="edges",
    )(up, mid, down, gain, shift)


def accumulate_taps(rows, kern, at, flip):
    accum = [jnp.zeros((CT, LANES), f32) for _ in range(SPAN - KSIZE + 1)]
    weights = kern[at, :]
    for b in range(KSIZE):
        shifted = [window(row, b - HALF) for row in rows]
        for a in range(KSIZE):
            tap = a * KSIZE + b
            if flip:
                tap = KSIZE * KSIZE - 1 - tap
            w = jnp.broadcast_to(weights[:, tap : tap + 1], (CT, LANES))
            for i in range(len(accum)):
                accum[i] = accum[i] + w * shifted[i + a]
    return accum


def forward_kernel(up, mid, down, left, right, kern, affine, cot, mixed, payload):
    tile_rows, channels, _ = mid.shape

    def step(t, carry):
        at = pl.ds(pl.multiple_of(t * CT, CT), CT)
        rows = halo_rows(up, mid, down, left, right, at)
        accum = accumulate_taps(rows, kern, at, False)
        for i in range(tile_rows):
            mixed[at, i * LANES : (i + 1) * LANES] = accum[i]
        return carry

    lax.fori_loop(0, channels // CT, step, 0)
    for i in range(tile_rows):
        cols = slice(i * LANES, (i + 1) * LANES)
        x = mixed[:, cols]
        mean = jnp.sum(x, axis=0, keepdims=True) / channels
        dev = x - mean
        spread = jnp.sum(dev * dev, axis=0, keepdims=True)
        rows = split3(mean) + split3(spread)
        stats = jnp.concatenate(rows + [jnp.zeros((CT - 6, LANES), f32)], axis=0)
        if i == 0:
            row_id = lax.broadcasted_iota(jnp.int32, (CT, LANES), 0)
            for k, part in enumerate(split3(affine[...])):
                stats = jnp.where(row_id == 6 + k, jnp.broadcast_to(part, (CT, LANES)), stats)
        dev = dev.astype(bf16)
        stats = stats.astype(bf16)
        for d in range(payload.shape[0]):
            payload[d, 0:channels, cols] = dev
            payload[d, channels : 2 * channels, cols] = cot[i]
            payload[d, 2 * channels : 2 * channels + CT, cols] = stats


def forward(up, mid, down, left, right, kern, affine, cot, parts):
    tile_rows, channels, _ = mid.shape
    pixels = tile_rows * LANES
    return vcall(
        forward_kernel,
        out_shape=(
            jax.ShapeDtypeStruct((channels, pixels), f32),
            jax.ShapeDtypeStruct((parts, 2 * channels + CT, pixels), bf16),
        ),
        name="forward",
    )(up, mid, down, left, right, kern, affine, cot)


def column(row, n):
    i = lax.broadcasted_iota(jnp.int32, (n, n), 0)
    j = lax.broadcasted_iota(jnp.int32, (n, n), 1)
    return jnp.sum(jnp.where(i == j, jnp.broadcast_to(row, (n, n)), 0.0), axis=1, keepdims=True)


def dot(a, b, dims):
    return lax.dot_general(a, b, (dims, ((), ())), preferred_element_type=f32)


def row_chunk(r, size):
    return (r % 2) * (size // 2) + r // 2


def halves(ref, send, keep):
    n = send.shape[0]
    bit = lax.axis_index("row") % 2
    send[...] = ref[pl.ds(pl.multiple_of((1 - bit) * n, n), n), :]
    keep[...] = ref[pl.ds(pl.multiple_of(bit * n, n), n), :]


def spread_kernel(x, recv, *rest):
    outs, total = rest[:-1], rest[-1]
    total[...] = x[...] + recv[...]
    n = outs[0].shape[0]
    y = lax.axis_index("row") // 2
    for m, out in enumerate(outs):
        low, high = y % 2, y // 2
        low = 1 - low if m % 2 else low
        high = 1 - high if m // 2 else high
        out[...] = total[pl.ds(pl.multiple_of((2 * high + low) * n, n), n), :].astype(out.dtype)


def spread(x, recv, parts):
    shape = (x.shape[0] // parts, LANES)
    return vcall(
        spread_kernel,
        out_shape=tuple(jax.ShapeDtypeStruct(shape, bf16 if m else f32) for m in range(parts)),
        scratch_shapes=[pltpu.VMEM(x.shape, f32)],
        name="spread",
    )(x, recv)


def reduce_rows(send, keep):
    size = lax.axis_size("row")
    recv = lax.ppermute(send, "row", [(i, i ^ 1) for i in range(size)])
    if size == 2:
        return [keep, recv]
    chunks = spread(keep, recv, size // 2)
    return [chunks[0]] + [
        lax.ppermute(chunks[m], "row", [(i, i ^ (2 * m)) for i in range(size)])
        for m in range(1, size // 2)
    ]


def mlp_kernel(recv, w_exp, bias, w_red, payload, stats_out, send, keep, off, grads, s_norm, s_act, s_cot, s_gh):
    parts, height, pixels = recv.shape
    ch = (height - CT) // 2
    total = parts * ch
    width = 2 * LANES
    gains, shifts = [], []
    for k in range(parts):
        head = recv[k, 2 * ch : 2 * ch + CT, 0:LANES].astype(f32)
        both = head[6:7] + head[7:8] + head[8:9]
        gains.append(column(both[:, 0:ch], ch))
        shifts.append(column(both[:, ch : 2 * ch], ch))
    bias_col = column(bias[...], bias.shape[1])
    for blk in range(pixels // width):
        cols = slice(blk * width, (blk + 1) * width)
        means, spreads = [], []
        for k in range(parts):
            st = recv[k, 2 * ch : 2 * ch + CT, cols].astype(f32)
            means.append(st[0:1] + st[1:2] + st[2:3])
            spreads.append(st[3:4] + st[4:5] + st[5:6])
        centre = sum(means) / parts
        spread = sum(spreads)
        for k in range(parts):
            gap = means[k] - centre
            spread = spread + ch * gap * gap
        inverse = lax.rsqrt(spread / total + epsilon)
        stats_out[0:1, cols] = centre
        stats_out[1:2, cols] = inverse
        for k in range(parts):
            at = slice(k * ch, (k + 1) * ch)
            dev = recv[k, 0:ch, cols].astype(f32)
            normed = (dev + (means[k] - centre)) * inverse
            s_norm[at, cols] = (normed * gains[k] + shifts[k]).astype(bf16)
            s_cot[at, cols] = recv[k, ch : 2 * ch, cols]
        hidden = dot(w_exp[...], s_norm[:, cols], ((0,), (0,))) + bias_col
        value, slope = gelu_pair(hidden)
        active = value.astype(bf16)
        s_act[:, cols] = active
        gh = (dot(w_red[...], s_cot[:, cols], ((1,), (0,))) * slope).astype(bf16)
        s_gh[:, cols] = gh
        mlp = dot(w_red[...], active, ((0,), (0,)))
        part = dot(w_exp[...], gh, ((1,), (0,)))
        plain = jnp.zeros((1, width), f32)
        cross = jnp.zeros((1, width), f32)
        for k in range(parts):
            at = slice(k * ch, (k + 1) * ch)
            dev = recv[k, 0:ch, cols].astype(f32)
            normed = (dev + (means[k] - centre)) * inverse
            scaled = part[at] * gains[k]
            plain = plain + jnp.sum(scaled, axis=0, keepdims=True)
            cross = cross + jnp.sum(scaled * normed, axis=0, keepdims=True)
            payload[k, 0:ch, cols] = mlp[at].astype(bf16)
            payload[k, ch : 2 * ch, cols] = part[at].astype(bf16)
        sums = jnp.concatenate(
            split3(plain) + split3(cross) + [jnp.zeros((CT - 6, width), f32)], axis=0
        ).astype(bf16)
        for k in range(parts):
            payload[k, 2 * ch : 2 * ch + CT, cols] = sums
    last = ((1,), (1,))
    grad_exp = dot(s_norm[...], s_gh[...], last)
    grad_red = dot(s_act[...], s_cot[...], last)
    n = grad_exp.shape[0]
    grads[0:n, :] = grad_exp[:, 0:LANES]
    grads[n : 2 * n, :] = grad_exp[:, LANES:]
    grads[2 * n : 3 * n, :] = grad_red[:, 0:LANES]
    grads[3 * n : 4 * n, :] = grad_red[:, LANES:]
    halves(grads, send, keep)
    sums = dot(s_gh[...], jnp.ones((pixels, LANES), bf16), ((1,), (0,)))
    table = jnp.zeros((ch, LANES), f32)
    lane = lane_ids(ch)
    for j in range(sums.shape[0] // ch):
        table = jnp.where(lane == OFFSET + j, sums[j * ch : (j + 1) * ch], table)
    off[...] = table


def mlp(recv, w_exp, bias, w_red):
    _, _, pixels = recv.shape
    hid = w_red.shape[0]
    total = w_exp.shape[0]
    return vcall(
        mlp_kernel,
        out_shape=(
            jax.ShapeDtypeStruct(recv.shape, bf16),
            jax.ShapeDtypeStruct((2, pixels), f32),
            jax.ShapeDtypeStruct((2 * total, LANES), f32),
            jax.ShapeDtypeStruct((2 * total, LANES), f32),
            jax.ShapeDtypeStruct(((recv.shape[1] - CT) // 2, LANES), f32),
        ),
        scratch_shapes=[
            pltpu.VMEM((4 * total, LANES), f32),
            pltpu.VMEM((total, pixels), bf16),
            pltpu.VMEM((hid, pixels), bf16),
            pltpu.VMEM((total, pixels), bf16),
            pltpu.VMEM((hid, pixels), bf16),
        ],
        name="mlp",
    )(recv, w_exp, bias, w_red)


def norm_back_kernel(recv, mixed, stats, gain, image, off, result, grad_mixed, rounded, small):
    parts, height, _ = recv.shape
    ch = (height - CT) // 2
    tile_rows = image.shape[0]
    total = parts * ch
    gain_col = column(gain[...], ch)
    acc_gain = jnp.zeros((ch, LANES), f32)
    acc_shift = jnp.zeros((ch, LANES), f32)
    for i in range(tile_rows):
        cols = slice(i * LANES, (i + 1) * LANES)
        mlp_out = jnp.zeros((ch, LANES), f32)
        grad = jnp.zeros((ch, LANES), f32)
        sums = jnp.zeros((CT, LANES), f32)
        for k in range(parts):
            mlp_out = mlp_out + recv[k, 0:ch, cols].astype(f32)
            grad = grad + recv[k, ch : 2 * ch, cols].astype(f32)
            sums = sums + recv[k, 2 * ch : 2 * ch + CT, cols].astype(f32)
        result[i] = (image[i].astype(f32) + mlp_out).astype(bf16)
        plain = (sums[0:1] + sums[1:2] + sums[2:3]) / total
        cross = (sums[3:4] + sums[4:5] + sums[5:6]) / total
        inverse = stats[1:2, cols]
        normed = (mixed[:, cols] - stats[0:1, cols]) * inverse
        acc_gain = acc_gain + grad * normed
        acc_shift = acc_shift + grad
        out = inverse * (grad * gain_col - plain - normed * cross)
        grad_mixed[i] = out
        rounded[i] = out.astype(bf16)
    g = jnp.sum(acc_gain, axis=1, keepdims=True)
    s = jnp.sum(acc_shift, axis=1, keepdims=True)
    lane = lane_ids(ch)
    small[...] = jnp.where(lane == GAIN, g, jnp.where(lane == SHIFT, s, off[...]))


def norm_back(recv, mixed, stats, gain, image, off):
    _, channels, _ = image.shape
    return vcall(
        norm_back_kernel,
        out_shape=(
            jax.ShapeDtypeStruct(image.shape, bf16),
            jax.ShapeDtypeStruct(image.shape, f32),
            jax.ShapeDtypeStruct(image.shape, bf16),
            jax.ShapeDtypeStruct((channels, LANES), f32),
        ),
        name="norm_back",
    )(recv, mixed, stats, gain, image, off)


def tap_grad_kernel(up, mid, down, left, right, grad_mixed, small, *rest):
    pieces, (out, table_ref, total) = rest[:-3], rest[-3:]
    tile_rows, channels, _ = mid.shape
    lane = lane_ids(CT)

    def step(t, carry):
        at = pl.ds(pl.multiple_of(t * CT, CT), CT)
        rows = halo_rows(up, mid, down, left, right, at)
        grads = [grad_mixed[i, at, :] for i in range(tile_rows)]
        table = small[at, :]
        for b in range(KSIZE):
            shifted = [window(row, b - HALF) for row in rows]
            for a in range(KSIZE):
                accum = grads[0] * shifted[a]
                for i in range(1, tile_rows):
                    accum = accum + grads[i] * shifted[a + i]
                value = jnp.sum(accum, axis=1, keepdims=True)
                table = jnp.where(lane == a * KSIZE + b, value, table)
        table_ref[at, :] = table
        return carry

    lax.fori_loop(0, channels // CT, step, 0)
    half = channels // 2
    total[...] = table_ref[0:half, :] + rolled(table_ref[half:channels, :], LANES // 2)
    cols, height, _ = out.shape
    part = pieces[0].shape[0] // cols
    per = total.shape[0] // cols
    pad = height - part - 2 * per
    for c in range(cols):
        at = slice(c * part, (c + 1) * part)
        big = sum(x[at, :].astype(f32) for x in pieces)
        tile = [big, hi_lo(total[c * per : (c + 1) * per, :])]
        if pad:
            tile.append(jnp.zeros((pad, LANES), f32))
        out[c] = jnp.concatenate(tile, axis=0).astype(bf16)


def tap_grad(up, mid, down, left, right, grad_mixed, small, pieces, cols):
    channels = mid.shape[1]
    part, per = pieces[0].shape[0] // cols, channels // 2 // cols
    height = part + -(-2 * per // 8) * 8
    return vcall(
        tap_grad_kernel,
        out_shape=jax.ShapeDtypeStruct((cols, height, LANES), bf16),
        scratch_shapes=[pltpu.VMEM((channels, LANES), f32), pltpu.VMEM((channels // 2, LANES), f32)],
        name="tap_grad",
    )(up, mid, down, left, right, grad_mixed, small, *pieces)


def backward_kernel(up, mid, down, left, right, kern, cot, out):
    tile_rows, channels, _ = mid.shape

    def step(t, carry):
        at = pl.ds(pl.multiple_of(t * CT, CT), CT)
        rows = halo_rows(up, mid, down, left, right, at)
        accum = accumulate_taps(rows, kern, at, True)
        for i in range(tile_rows):
            out[i, at, :] = (cot[i, at, :].astype(f32) + accum[i]).astype(bf16)
        return carry

    lax.fori_loop(0, channels // CT, step, 0)


def backward(up, mid, down, left, right, kern, cot):
    return vcall(
        backward_kernel,
        out_shape=jax.ShapeDtypeStruct(cot.shape, bf16),
        name="backward",
    )(up, mid, down, left, right, kern, cot)


def hi_lo(x):
    hi = x.astype(bf16).astype(f32)
    return jnp.concatenate([hi, x - hi], axis=0)


def col_pack_kernel(per, recv, out):
    total = recv[0].astype(f32)
    for c in range(1, recv.shape[0]):
        total = total + recv[c].astype(f32)
    part = total.shape[0] - -(-2 * per // 8) * 8
    tail = hi_lo(total[part : part + per] + total[part + per : part + 2 * per])
    pad = total.shape[0] - part - 2 * per
    pieces = [total[0:part], tail] + ([jnp.zeros((pad, LANES), f32)] if pad else [])
    tile = jnp.concatenate(pieces, axis=0).astype(bf16)
    for c in range(out.shape[0]):
        out[c] = tile


def col_pack(recv, per):
    return vcall(
        functools.partial(col_pack_kernel, per),
        out_shape=jax.ShapeDtypeStruct(recv.shape, bf16),
        name="col_pack",
    )(recv)


def row_pack_kernel(per, recv, out, tile):
    cols, height, _ = recv.shape
    part = height - -(-2 * per // 8) * 8
    base, size = cols * part, cols * per
    for c in range(cols):
        x = recv[c].astype(f32)
        tile[c * part : (c + 1) * part, :] = x[0:part]
        tile[base + c * per : base + (c + 1) * per, :] = x[part : part + per]
        low = base + size + c * per
        tile[low : low + per, :] = x[part + per : part + 2 * per]
    x = tile[...].astype(bf16)
    for r in range(out.shape[0]):
        out[r] = x


def row_pack(recv, rows, per):
    cols, height, _ = recv.shape
    tall = cols * (height - -(-2 * per // 8) * 8 + 2 * per)
    return vcall(
        functools.partial(row_pack_kernel, per),
        out_shape=jax.ShapeDtypeStruct((rows, tall, LANES), bf16),
        scratch_shapes=[pltpu.VMEM((tall, LANES), f32)],
        name="row_pack",
    )(recv)


def final_kernel(scale, flat, exp_ref, red_ref, taps_ref, gain_ref, shift_ref, off_ref):
    rows = flat.shape[0]
    n = exp_ref.shape[0]
    per = taps_ref.shape[1] // 2
    size_all = 4 * n // rows
    for r in range(rows):
        x = flat[r].astype(f32) * scale
        block = x[0:size_all]
        tail = x[size_all : size_all + per] + x[size_all + per : size_all + 2 * per]
        total = tail if r == 0 else total + tail
        start = row_chunk(r, rows) * size_all
        lo = 0
        while lo < size_all:
            which, at = divmod(start + lo, n)
            size = min(size_all - lo, n - at)
            ref = (exp_ref, red_ref)[which // 2]
            lane = (which % 2) * LANES
            ref[at : at + size, lane : lane + LANES] = block[lo : lo + size]
            lo += size
    x = total
    both = jnp.concatenate([x, rolled(x, LANES // 2)], axis=0)
    wide = jnp.concatenate([both, jnp.zeros((LANES - both.shape[0], LANES), f32)], axis=0)
    flip = jnp.transpose(wide)[:, 0 : both.shape[0]]
    taps_ref[...] = flip[0 : taps_ref.shape[0], :]
    gain_ref[...] = flip[GAIN : GAIN + 1]
    shift_ref[...] = flip[SHIFT : SHIFT + 1]
    channels = flip.shape[1]
    for j in range(off_ref.shape[1] // channels):
        off_ref[:, j * channels : (j + 1) * channels] = flip[OFFSET + j : OFFSET + j + 1]


def final(flat, scale, total, hid, channels, taps):
    return vcall(
        functools.partial(final_kernel, scale),
        out_shape=(
            jax.ShapeDtypeStruct((total, hid), f32),
            jax.ShapeDtypeStruct((hid, total), f32),
            jax.ShapeDtypeStruct((taps, channels), f32),
            jax.ShapeDtypeStruct((1, channels), f32),
            jax.ShapeDtypeStruct((1, channels), f32),
            jax.ShapeDtypeStruct((1, hid), f32),
        ),
        name="final",
    )(flat)


def neighbours(first, last, axis):
    size = lax.axis_size(axis)
    up = [(i, i + 1) for i in range(size - 1)]
    down = [(j, i) for i, j in up]
    return lax.ppermute(last, axis, up), lax.ppermute(first, axis, down)


def halo(x, gain, shift):
    rows = x.shape[0]
    up, down = neighbours(x[:HALF], x[rows - HALF :], "row")
    first, last, both = edges(up, x, down, gain, shift)
    left, right = neighbours(first, last, "col")
    return up, down, left, right, both


def exchange(x, axis):
    return lax.all_to_all(x, axis, 0, 0)


def reduce_cols(part, per):
    part = exchange(part, "col")
    flat = exchange(col_pack(part, per), "col")
    return exchange(row_pack(flat, lax.axis_size("row"), per), "row")


def body(
    image, depth_kernel, norm_gain, norm_shift, expand_weight, expand_bias, reduce_weight, cotangent
):
    channels, tile_rows, tile_cols = image.shape
    pixels = tile_rows * tile_cols
    parts = lax.axis_size("ch")
    hid = reduce_weight.shape[0]
    total = expand_weight.shape[0]
    img = jnp.transpose(image, (1, 0, 2))
    cot = jnp.transpose(cotangent, (1, 0, 2))
    gain = norm_gain.reshape(1, channels)
    shift = norm_shift.reshape(1, channels)
    bias = lax.dynamic_slice_in_dim(expand_bias, lax.axis_index("ch") * hid, hid).reshape(1, hid)
    up, down, left, right, affine = halo(img, gain, shift)
    mixed, send = forward(up, img, down, left, right, depth_kernel, affine, cot, parts)
    recv = exchange(send, "ch")
    send, stats, give, keep, off = mlp(recv, expand_weight, bias, reduce_weight)
    recv = exchange(send, "ch")
    pieces = reduce_rows(give, keep)
    result, grad_mixed, rounded, small = norm_back(recv, mixed, stats, gain, img, off)
    g_up, g_down, g_left, g_right, _ = halo(rounded, gain, shift)
    cols = lax.axis_size("col")
    part = tap_grad(up, img, down, left, right, grad_mixed, small, pieces, cols)
    grad_image = backward(g_up, rounded, g_down, g_left, g_right, depth_kernel, cot)
    flat = reduce_cols(part, channels // 2 // cols)
    pixels_all = pixels * lax.axis_size("row") * lax.axis_size("col")
    scale = float(pixels_all) ** (-0.5)
    grad_exp, grad_red, grad_taps, grad_gain, grad_shift, grad_off = final(
        flat, scale, total, hid, channels, depth_kernel.shape[1]
    )
    return (
        jnp.transpose(result, (1, 0, 2)),
        jnp.transpose(grad_image, (1, 0, 2)),
        jnp.transpose(grad_taps),
        grad_gain.reshape(channels),
        grad_shift.reshape(channels),
        grad_exp,
        grad_off.reshape(hid),
        grad_red,
    )


def solution(mesh):
    in_specs = (
        P("ch", "row", "col"),
        P("ch", None),
        P("ch"),
        P("ch"),
        P(None, "ch"),
        P(),
        P("ch", None),
        P("ch", "row", "col"),
    )
    out_specs = (
        P("ch", "row", "col"),
        P("ch", "row", "col"),
        P("ch", None),
        P("ch"),
        P("ch"),
        P(None, "ch"),
        P("ch"),
        P("ch", None),
    )

    return jax.shard_map(body, mesh=mesh, in_specs=in_specs, out_specs=out_specs, check_vma=False)
```

```python
import functools
import jax
import jax.numpy as jnp
from jax import lax
from jax.experimental import pallas as pl
from jax.experimental.pallas import tpu as pltpu
from jax.sharding import PartitionSpec as P

KSIZE = 7
HALF = 3
SPAN = KSIZE + HALF
epsilon = 1e-06
root_two_pi = 0.7978845608028654
cubic_coef = 0.044715
f32 = jnp.float32
bf16 = jnp.bfloat16
LANES = 128
CT = 16
GAIN = KSIZE * KSIZE
SHIFT = GAIN + 1
OFFSET = GAIN + 2


def vcall(kernel, out_shape, **kw):
    spec = pl.BlockSpec(memory_space=pltpu.VMEM)

    def call(*args):
        return pl.pallas_call(
            kernel,
            out_shape=out_shape,
            in_specs=[spec] * len(args),
            out_specs=jax.tree.map(lambda _: spec, out_shape),
            compiler_params=pltpu.CompilerParams(vmem_limit_bytes=8 << 20),
            **kw,
        )(*args)

    return call


def lane_ids(rows):
    return lax.broadcasted_iota(jnp.int32, (rows, LANES), 1)


def rolled(x, shift):
    shift = shift % LANES
    return x if shift == 0 else pltpu.roll(x, shift, 1)


def split3(x):
    hi = x.astype(bf16)
    rest = x - hi.astype(f32)
    mid = rest.astype(bf16)
    low = (rest - mid.astype(f32)).astype(bf16)
    return [hi.astype(f32), mid.astype(f32), low.astype(f32)]


def gelu_pair(hidden):
    inner = root_two_pi * (hidden + cubic_coef * hidden * hidden * hidden)
    tangent = jnp.tanh(inner)
    value = 0.5 * hidden * (1.0 + tangent)
    slope = 0.5 * (1.0 + tangent) + 0.5 * hidden * (1.0 - tangent * tangent) * root_two_pi * (
        1.0 + 3.0 * cubic_coef * hidden * hidden
    )
    return (value, slope)


def halo_rows(up, mid, down, left, right, at):
    lane = lane_ids(CT)
    l = left[at, :].astype(f32)
    r = right[at, :].astype(f32)
    rows = []
    for i in range(SPAN):
        if i < HALF:
            x = up[i, at, :]
        elif i < SPAN - HALF:
            x = mid[i - HALF, at, :]
        else:
            x = down[i - (SPAN - HALF), at, :]
        edge = jnp.where(
            lane >= 64, rolled(l, LANES - HALF - HALF * i), rolled(r, LANES - HALF * i)
        )
        rows.append((x.astype(f32), edge))
    return rows


def window(row, s):
    x, edge = row
    if s == 0:
        return x
    lane = lane_ids(CT)
    mask = (lane < s) if s > 0 else (lane >= LANES + s)
    return rolled(jnp.where(mask, edge, x), -s)


def edges_kernel(up, mid, down, gain, shift, first, last, both):
    both[...] = jnp.concatenate([gain[...], shift[...]], axis=1)
    channels = mid.shape[1]
    lane = lane_ids(CT)

    def step(t, carry):
        at = pl.ds(pl.multiple_of(t * CT, CT), CT)
        head = jnp.zeros((CT, LANES), f32)
        tail = jnp.zeros((CT, LANES), f32)
        for i in range(SPAN):
            if i < HALF:
                x = up[i, at, :]
            elif i < SPAN - HALF:
                x = mid[i - HALF, at, :]
            else:
                x = down[i - (SPAN - HALF), at, :]
            x = x.astype(f32)
            mask = (lane >= HALF * i) & (lane < HALF * i + HALF)
            head = jnp.where(mask, rolled(x, HALF * i), head)
            tail = jnp.where(mask, rolled(x, HALF * i + HALF), tail)
        first[at, :] = head.astype(bf16)
        last[at, :] = tail.astype(bf16)
        return carry

    lax.fori_loop(0, channels // CT, step, 0)


def edges(up, mid, down, gain, shift):
    channels = mid.shape[1]
    shape = jax.ShapeDtypeStruct((channels, LANES), bf16)
    return vcall(
        edges_kernel,
        out_shape=(shape, shape, jax.ShapeDtypeStruct((1, 2 * channels), f32)),
        name="edges",
    )(up, mid, down, gain, shift)


def accumulate_taps(rows, kern, at, flip):
    accum = [jnp.zeros((CT, LANES), f32) for _ in range(SPAN - KSIZE + 1)]
    weights = kern[at, :]
    for b in range(KSIZE):
        shifted = [window(row, b - HALF) for row in rows]
        for a in range(KSIZE):
            tap = a * KSIZE + b
            if flip:
                tap = KSIZE * KSIZE - 1 - tap
            w = jnp.broadcast_to(weights[:, tap : tap + 1], (CT, LANES))
            for i in range(len(accum)):
                accum[i] = accum[i] + w * shifted[i + a]
    return accum


def forward_kernel(up, mid, down, left, right, kern, affine, cot, mixed, payload):
    tile_rows, channels, _ = mid.shape

    def step(t, carry):
        at = pl.ds(pl.multiple_of(t * CT, CT), CT)
        rows = halo_rows(up, mid, down, left, right, at)
        accum = accumulate_taps(rows, kern, at, False)
        for i in range(tile_rows):
            mixed[at, i * LANES : (i + 1) * LANES] = accum[i]
        return carry

    lax.fori_loop(0, channels // CT, step, 0)
    for i in range(tile_rows):
        cols = slice(i * LANES, (i + 1) * LANES)
        x = mixed[:, cols]
        mean = jnp.sum(x, axis=0, keepdims=True) / channels
        dev = x - mean
        spread = jnp.sum(dev * dev, axis=0, keepdims=True)
        rows = split3(mean) + split3(spread)
        stats = jnp.concatenate(rows + [jnp.zeros((CT - 6, LANES), f32)], axis=0)
        if i == 0:
            row_id = lax.broadcasted_iota(jnp.int32, (CT, LANES), 0)
            for k, part in enumerate(split3(affine[...])):
                stats = jnp.where(row_id == 6 + k, jnp.broadcast_to(part, (CT, LANES)), stats)
        dev = dev.astype(bf16)
        stats = stats.astype(bf16)
        for d in range(payload.shape[0]):
            payload[d, 0:channels, cols] = dev
            payload[d, channels : 2 * channels, cols] = cot[i]
            payload[d, 2 * channels : 2 * channels + CT, cols] = stats


def forward(up, mid, down, left, right, kern, affine, cot, parts):
    tile_rows, channels, _ = mid.shape
    pixels = tile_rows * LANES
    return vcall(
        forward_kernel,
        out_shape=(
            jax.ShapeDtypeStruct((channels, pixels), f32),
            jax.ShapeDtypeStruct((parts, 2 * channels + CT, pixels), bf16),
        ),
        name="forward",
    )(up, mid, down, left, right, kern, affine, cot)


def column(row, n):
    i = lax.broadcasted_iota(jnp.int32, (n, n), 0)
    j = lax.broadcasted_iota(jnp.int32, (n, n), 1)
    return jnp.sum(jnp.where(i == j, jnp.broadcast_to(row, (n, n)), 0.0), axis=1, keepdims=True)


def dot(a, b, dims):
    return lax.dot_general(a, b, (dims, ((), ())), preferred_element_type=f32)


def row_chunk(r, size):
    return (r % 2) * (size // 2) + r // 2


def halves(ref, send, keep):
    n = send.shape[0]
    bit = lax.axis_index("row") % 2
    send[...] = ref[pl.ds(pl.multiple_of((1 - bit) * n, n), n), :]
    keep[...] = ref[pl.ds(pl.multiple_of(bit * n, n), n), :]


def spread_kernel(x, recv, *rest):
    outs, total = rest[:-1], rest[-1]
    total[...] = x[...] + recv[...]
    n = outs[0].shape[0]
    y = lax.axis_index("row") // 2
    for m, out in enumerate(outs):
        low, high = y % 2, y // 2
        low = 1 - low if m % 2 else low
        high = 1 - high if m // 2 else high
        out[...] = total[pl.ds(pl.multiple_of((2 * high + low) * n, n), n), :].astype(out.dtype)


def spread(x, recv, parts):
    shape = (x.shape[0] // parts, LANES)
    return vcall(
        spread_kernel,
        out_shape=tuple(jax.ShapeDtypeStruct(shape, bf16 if m else f32) for m in range(parts)),
        scratch_shapes=[pltpu.VMEM(x.shape, f32)],
        name="spread",
    )(x, recv)


def reduce_rows(send, keep):
    size = lax.axis_size("row")
    recv = lax.ppermute(send, "row", [(i, i ^ 1) for i in range(size)])
    if size == 2:
        return [keep, recv]
    chunks = spread(keep, recv, size // 2)
    return [chunks[0]] + [
        lax.ppermute(chunks[m], "row", [(i, i ^ (2 * m)) for i in range(size)])
        for m in range(1, size // 2)
    ]


def mlp_kernel(recv, w_exp, bias, w_red, payload, stats_out, send, keep, off, grads, s_norm, s_act, s_cot, s_gh):
    parts, height, pixels = recv.shape
    ch = (height - CT) // 2
    total = parts * ch
    width = 2 * LANES
    gains, shifts = [], []
    for k in range(parts):
        head = recv[k, 2 * ch : 2 * ch + CT, 0:LANES].astype(f32)
        both = head[6:7] + head[7:8] + head[8:9]
        gains.append(column(both[:, 0:ch], ch))
        shifts.append(column(both[:, ch : 2 * ch], ch))
    bias_col = column(bias[...], bias.shape[1])
    for blk in range(pixels // width):
        cols = slice(blk * width, (blk + 1) * width)
        means, spreads = [], []
        for k in range(parts):
            st = recv[k, 2 * ch : 2 * ch + CT, cols].astype(f32)
            means.append(st[0:1] + st[1:2] + st[2:3])
            spreads.append(st[3:4] + st[4:5] + st[5:6])
        centre = sum(means) / parts
        spread = sum(spreads)
        for k in range(parts):
            gap = means[k] - centre
            spread = spread + ch * gap * gap
        inverse = lax.rsqrt(spread / total + epsilon)
        stats_out[0:1, cols] = centre
        stats_out[1:2, cols] = inverse
        for k in range(parts):
            at = slice(k * ch, (k + 1) * ch)
            dev = recv[k, 0:ch, cols].astype(f32)
            normed = (dev + (means[k] - centre)) * inverse
            s_norm[at, cols] = (normed * gains[k] + shifts[k]).astype(bf16)
            s_cot[at, cols] = recv[k, ch : 2 * ch, cols]
        hidden = dot(w_exp[...], s_norm[:, cols], ((0,), (0,))) + bias_col
        value, slope = gelu_pair(hidden)
        active = value.astype(bf16)
        s_act[:, cols] = active
        gh = (dot(w_red[...], s_cot[:, cols], ((1,), (0,))) * slope).astype(bf16)
        s_gh[:, cols] = gh
        mlp = dot(w_red[...], active, ((0,), (0,)))
        part = dot(w_exp[...], gh, ((1,), (0,)))
        plain = jnp.zeros((1, width), f32)
        cross = jnp.zeros((1, width), f32)
        for k in range(parts):
            at = slice(k * ch, (k + 1) * ch)
            dev = recv[k, 0:ch, cols].astype(f32)
            normed = (dev + (means[k] - centre)) * inverse
            scaled = part[at] * gains[k]
            plain = plain + jnp.sum(scaled, axis=0, keepdims=True)
            cross = cross + jnp.sum(scaled * normed, axis=0, keepdims=True)
            payload[k, 0:ch, cols] = mlp[at].astype(bf16)
            payload[k, ch : 2 * ch, cols] = part[at].astype(bf16)
        sums = jnp.concatenate(
            split3(plain) + split3(cross) + [jnp.zeros((CT - 6, width), f32)], axis=0
        ).astype(bf16)
        for k in range(parts):
            payload[k, 2 * ch : 2 * ch + CT, cols] = sums
    last = ((1,), (1,))
    grad_exp = dot(s_norm[...], s_gh[...], last)
    grad_red = dot(s_act[...], s_cot[...], last)
    n = grad_exp.shape[0]
    grads[0:n, :] = grad_exp[:, 0:LANES]
    grads[n : 2 * n, :] = grad_exp[:, LANES:]
    grads[2 * n : 3 * n, :] = grad_red[:, 0:LANES]
    grads[3 * n : 4 * n, :] = grad_red[:, LANES:]
    halves(grads, send, keep)
    sums = dot(s_gh[...], jnp.ones((pixels, LANES), bf16), ((1,), (0,)))
    table = jnp.zeros((ch, LANES), f32)
    lane = lane_ids(ch)
    for j in range(sums.shape[0] // ch):
        table = jnp.where(lane == OFFSET + j, sums[j * ch : (j + 1) * ch], table)
    off[...] = table


def mlp(recv, w_exp, bias, w_red):
    _, _, pixels = recv.shape
    hid = w_red.shape[0]
    total = w_exp.shape[0]
    return vcall(
        mlp_kernel,
        out_shape=(
            jax.ShapeDtypeStruct(recv.shape, bf16),
            jax.ShapeDtypeStruct((2, pixels), f32),
            jax.ShapeDtypeStruct((2 * total, LANES), f32),
            jax.ShapeDtypeStruct((2 * total, LANES), f32),
            jax.ShapeDtypeStruct(((recv.shape[1] - CT) // 2, LANES), f32),
        ),
        scratch_shapes=[
            pltpu.VMEM((4 * total, LANES), f32),
            pltpu.VMEM((total, pixels), bf16),
            pltpu.VMEM((hid, pixels), bf16),
            pltpu.VMEM((total, pixels), bf16),
            pltpu.VMEM((hid, pixels), bf16),
        ],
        name="mlp",
    )(recv, w_exp, bias, w_red)


def norm_back_kernel(recv, mixed, stats, gain, image, off, result, grad_mixed, rounded, small):
    parts, height, _ = recv.shape
    ch = (height - CT) // 2
    tile_rows = image.shape[0]
    total = parts * ch
    gain_col = column(gain[...], ch)
    acc_gain = jnp.zeros((ch, LANES), f32)
    acc_shift = jnp.zeros((ch, LANES), f32)
    for i in range(tile_rows):
        cols = slice(i * LANES, (i + 1) * LANES)
        mlp_out = jnp.zeros((ch, LANES), f32)
        grad = jnp.zeros((ch, LANES), f32)
        sums = jnp.zeros((CT, LANES), f32)
        for k in range(parts):
            mlp_out = mlp_out + recv[k, 0:ch, cols].astype(f32)
            grad = grad + recv[k, ch : 2 * ch, cols].astype(f32)
            sums = sums + recv[k, 2 * ch : 2 * ch + CT, cols].astype(f32)
        result[i] = (image[i].astype(f32) + mlp_out).astype(bf16)
        plain = (sums[0:1] + sums[1:2] + sums[2:3]) / total
        cross = (sums[3:4] + sums[4:5] + sums[5:6]) / total
        inverse = stats[1:2, cols]
        normed = (mixed[:, cols] - stats[0:1, cols]) * inverse
        acc_gain = acc_gain + grad * normed
        acc_shift = acc_shift + grad
        out = inverse * (grad * gain_col - plain - normed * cross)
        grad_mixed[i] = out
        rounded[i] = out.astype(bf16)
    g = jnp.sum(acc_gain, axis=1, keepdims=True)
    s = jnp.sum(acc_shift, axis=1, keepdims=True)
    lane = lane_ids(ch)
    small[...] = jnp.where(lane == GAIN, g, jnp.where(lane == SHIFT, s, off[...]))


def norm_back(recv, mixed, stats, gain, image, off):
    _, channels, _ = image.shape
    return vcall(
        norm_back_kernel,
        out_shape=(
            jax.ShapeDtypeStruct(image.shape, bf16),
            jax.ShapeDtypeStruct(image.shape, f32),
            jax.ShapeDtypeStruct(image.shape, bf16),
            jax.ShapeDtypeStruct((channels, LANES), f32),
        ),
        name="norm_back",
    )(recv, mixed, stats, gain, image, off)


def tap_grad_kernel(up, mid, down, left, right, grad_mixed, small, *rest):
    pieces, (out, table_ref, total) = rest[:-3], rest[-3:]
    tile_rows, channels, _ = mid.shape
    lane = lane_ids(CT)

    def step(t, carry):
        at = pl.ds(pl.multiple_of(t * CT, CT), CT)
        rows = halo_rows(up, mid, down, left, right, at)
        grads = [grad_mixed[i, at, :] for i in range(tile_rows)]
        table = small[at, :]
        for b in range(KSIZE):
            shifted = [window(row, b - HALF) for row in rows]
            for a in range(KSIZE):
                accum = grads[0] * shifted[a]
                for i in range(1, tile_rows):
                    accum = accum + grads[i] * shifted[a + i]
                value = jnp.sum(accum, axis=1, keepdims=True)
                table = jnp.where(lane == a * KSIZE + b, value, table)
        table_ref[at, :] = table
        return carry

    lax.fori_loop(0, channels // CT, step, 0)
    half = channels // 2
    total[...] = table_ref[0:half, :] + rolled(table_ref[half:channels, :], LANES // 2)
    cols, height, _ = out.shape
    part = pieces[0].shape[0] // cols
    per = total.shape[0] // cols
    pad = height - part - 2 * per
    for c in range(cols):
        at = slice(c * part, (c + 1) * part)
        big = sum(x[at, :].astype(f32) for x in pieces)
        tile = [big, hi_lo(total[c * per : (c + 1) * per, :])]
        if pad:
            tile.append(jnp.zeros((pad, LANES), f32))
        out[c] = jnp.concatenate(tile, axis=0).astype(bf16)


def tap_grad(up, mid, down, left, right, grad_mixed, small, pieces, cols):
    channels = mid.shape[1]
    part, per = pieces[0].shape[0] // cols, channels // 2 // cols
    height = part + -(-2 * per // 8) * 8
    return vcall(
        tap_grad_kernel,
        out_shape=jax.ShapeDtypeStruct((cols, height, LANES), bf16),
        scratch_shapes=[pltpu.VMEM((channels, LANES), f32), pltpu.VMEM((channels // 2, LANES), f32)],
        name="tap_grad",
    )(up, mid, down, left, right, grad_mixed, small, *pieces)


def backward_kernel(up, mid, down, left, right, kern, cot, out):
    tile_rows, channels, _ = mid.shape

    def step(t, carry):
        at = pl.ds(pl.multiple_of(t * CT, CT), CT)
        rows = halo_rows(up, mid, down, left, right, at)
        accum = accumulate_taps(rows, kern, at, True)
        for i in range(tile_rows):
            out[i, at, :] = (cot[i, at, :].astype(f32) + accum[i]).astype(bf16)
        return carry

    lax.fori_loop(0, channels // CT, step, 0)


def backward(up, mid, down, left, right, kern, cot):
    return vcall(
        backward_kernel,
        out_shape=jax.ShapeDtypeStruct(cot.shape, bf16),
        name="backward",
    )(up, mid, down, left, right, kern, cot)


def hi_lo(x):
    hi = x.astype(bf16).astype(f32)
    return jnp.concatenate([hi, x - hi], axis=0)


def col_pack_kernel(per, recv, out):
    total = recv[0].astype(f32)
    for c in range(1, recv.shape[0]):
        total = total + recv[c].astype(f32)
    part = total.shape[0] - -(-2 * per // 8) * 8
    tail = hi_lo(total[part : part + per] + total[part + per : part + 2 * per])
    pad = total.shape[0] - part - 2 * per
    pieces = [total[0:part], tail] + ([jnp.zeros((pad, LANES), f32)] if pad else [])
    tile = jnp.concatenate(pieces, axis=0).astype(bf16)
    for c in range(out.shape[0]):
        out[c] = tile


def col_pack(recv, per):
    return vcall(
        functools.partial(col_pack_kernel, per),
        out_shape=jax.ShapeDtypeStruct(recv.shape, bf16),
        name="col_pack",
    )(recv)


def row_pack_kernel(per, recv, out, tile):
    cols, height, _ = recv.shape
    part = height - -(-2 * per // 8) * 8
    base = cols * part
    for c in range(cols):
        x = recv[c].astype(f32)
        tile[c * part : (c + 1) * part, :] = x[0:part]
        small = x[part : part + per] + x[part + per : part + 2 * per]
        tile[base + c * per : base + (c + 1) * per, :] = small
    x = tile[...].astype(bf16)
    for r in range(out.shape[0]):
        out[r] = x


def row_pack(recv, rows, per):
    cols, height, _ = recv.shape
    tall = cols * (height - -(-2 * per // 8) * 8 + per)
    return vcall(
        functools.partial(row_pack_kernel, per),
        out_shape=jax.ShapeDtypeStruct((rows, tall, LANES), bf16),
        scratch_shapes=[pltpu.VMEM((tall, LANES), f32)],
        name="row_pack",
    )(recv)


def final_kernel(scale, flat, exp_ref, red_ref, taps_ref, gain_ref, shift_ref, off_ref):
    rows = flat.shape[0]
    n = exp_ref.shape[0]
    per = taps_ref.shape[1] // 2
    size_all = 4 * n // rows
    for r in range(rows):
        x = flat[r].astype(f32) * scale
        block = x[0:size_all]
        tail = x[size_all : size_all + per]
        total = tail if r == 0 else total + tail
        start = row_chunk(r, rows) * size_all
        lo = 0
        while lo < size_all:
            which, at = divmod(start + lo, n)
            size = min(size_all - lo, n - at)
            ref = (exp_ref, red_ref)[which // 2]
            lane = (which % 2) * LANES
            ref[at : at + size, lane : lane + LANES] = block[lo : lo + size]
            lo += size
    x = total
    both = jnp.concatenate([x, rolled(x, LANES // 2)], axis=0)
    wide = jnp.concatenate([both, jnp.zeros((LANES - both.shape[0], LANES), f32)], axis=0)
    flip = jnp.transpose(wide)[:, 0 : both.shape[0]]
    taps_ref[...] = flip[0 : taps_ref.shape[0], :]
    gain_ref[...] = flip[GAIN : GAIN + 1]
    shift_ref[...] = flip[SHIFT : SHIFT + 1]
    channels = flip.shape[1]
    for j in range(off_ref.shape[1] // channels):
        off_ref[:, j * channels : (j + 1) * channels] = flip[OFFSET + j : OFFSET + j + 1]


def final(flat, scale, total, hid, channels, taps):
    return vcall(
        functools.partial(final_kernel, scale),
        out_shape=(
            jax.ShapeDtypeStruct((total, hid), f32),
            jax.ShapeDtypeStruct((hid, total), f32),
            jax.ShapeDtypeStruct((taps, channels), f32),
            jax.ShapeDtypeStruct((1, channels), f32),
            jax.ShapeDtypeStruct((1, channels), f32),
            jax.ShapeDtypeStruct((1, hid), f32),
        ),
        name="final",
    )(flat)


def neighbours(first, last, axis):
    size = lax.axis_size(axis)
    up = [(i, i + 1) for i in range(size - 1)]
    down = [(j, i) for i, j in up]
    return lax.ppermute(last, axis, up), lax.ppermute(first, axis, down)


def halo(x, gain, shift):
    rows = x.shape[0]
    up, down = neighbours(x[:HALF], x[rows - HALF :], "row")
    first, last, both = edges(up, x, down, gain, shift)
    left, right = neighbours(first, last, "col")
    return up, down, left, right, both


def exchange(x, axis):
    return lax.all_to_all(x, axis, 0, 0)


def reduce_cols(part, per):
    part = exchange(part, "col")
    flat = exchange(col_pack(part, per), "col")
    return exchange(row_pack(flat, lax.axis_size("row"), per), "row")


def body(
    image, depth_kernel, norm_gain, norm_shift, expand_weight, expand_bias, reduce_weight, cotangent
):
    channels, tile_rows, tile_cols = image.shape
    pixels = tile_rows * tile_cols
    parts = lax.axis_size("ch")
    hid = reduce_weight.shape[0]
    total = expand_weight.shape[0]
    img = jnp.transpose(image, (1, 0, 2))
    cot = jnp.transpose(cotangent, (1, 0, 2))
    gain = norm_gain.reshape(1, channels)
    shift = norm_shift.reshape(1, channels)
    bias = lax.dynamic_slice_in_dim(expand_bias, lax.axis_index("ch") * hid, hid).reshape(1, hid)
    up, down, left, right, affine = halo(img, gain, shift)
    mixed, send = forward(up, img, down, left, right, depth_kernel, affine, cot, parts)
    recv = exchange(send, "ch")
    send, stats, give, keep, off = mlp(recv, expand_weight, bias, reduce_weight)
    recv = exchange(send, "ch")
    pieces = reduce_rows(give, keep)
    result, grad_mixed, rounded, small = norm_back(recv, mixed, stats, gain, img, off)
    g_up, g_down, g_left, g_right, _ = halo(rounded, gain, shift)
    cols = lax.axis_size("col")
    part = tap_grad(up, img, down, left, right, grad_mixed, small, pieces, cols)
    grad_image = backward(g_up, rounded, g_down, g_left, g_right, depth_kernel, cot)
    flat = reduce_cols(part, channels // 2 // cols)
    pixels_all = pixels * lax.axis_size("row") * lax.axis_size("col")
    scale = float(pixels_all) ** (-0.5)
    grad_exp, grad_red, grad_taps, grad_gain, grad_shift, grad_off = final(
        flat, scale, total, hid, channels, depth_kernel.shape[1]
    )
    return (
        jnp.transpose(result, (1, 0, 2)),
        jnp.transpose(grad_image, (1, 0, 2)),
        jnp.transpose(grad_taps),
        grad_gain.reshape(channels),
        grad_shift.reshape(channels),
        grad_exp,
        grad_off.reshape(hid),
        grad_red,
    )


def solution(mesh):
    in_specs = (
        P("ch", "row", "col"),
        P("ch", None),
        P("ch"),
        P("ch"),
        P(None, "ch"),
        P(),
        P("ch", None),
        P("ch", "row", "col"),
    )
    out_specs = (
        P("ch", "row", "col"),
        P("ch", "row", "col"),
        P("ch", None),
        P("ch"),
        P("ch"),
        P(None, "ch"),
        P("ch"),
        P("ch", None),
    )

    return jax.shard_map(body, mesh=mesh, in_specs=in_specs, out_specs=out_specs, check_vma=False)
```

```python
import functools
import jax
import jax.numpy as jnp
from jax import lax
from jax.experimental import pallas as pl
from jax.experimental.pallas import tpu as pltpu
from jax.sharding import PartitionSpec as P

KSIZE = 7
HALF = 3
SPAN = KSIZE + HALF
epsilon = 1e-06
root_two_pi = 0.7978845608028654
cubic_coef = 0.044715
f32 = jnp.float32
bf16 = jnp.bfloat16
LANES = 128
CT = 16
GAIN = KSIZE * KSIZE
SHIFT = GAIN + 1
OFFSET = GAIN + 2


def vcall(kernel, out_shape, **kw):
    spec = pl.BlockSpec(memory_space=pltpu.VMEM)

    def call(*args):
        return pl.pallas_call(
            kernel,
            out_shape=out_shape,
            in_specs=[spec] * len(args),
            out_specs=jax.tree.map(lambda _: spec, out_shape),
            compiler_params=pltpu.CompilerParams(vmem_limit_bytes=8 << 20),
            **kw,
        )(*args)

    return call


def lane_ids(rows):
    return lax.broadcasted_iota(jnp.int32, (rows, LANES), 1)


def rolled(x, shift):
    shift = shift % LANES
    return x if shift == 0 else pltpu.roll(x, shift, 1)


def split3(x):
    hi = x.astype(bf16)
    rest = x - hi.astype(f32)
    mid = rest.astype(bf16)
    low = (rest - mid.astype(f32)).astype(bf16)
    return [hi.astype(f32), mid.astype(f32), low.astype(f32)]


def gelu_pair(hidden):
    inner = root_two_pi * (hidden + cubic_coef * hidden * hidden * hidden)
    tangent = jnp.tanh(inner)
    value = 0.5 * hidden * (1.0 + tangent)
    slope = 0.5 * (1.0 + tangent) + 0.5 * hidden * (1.0 - tangent * tangent) * root_two_pi * (
        1.0 + 3.0 * cubic_coef * hidden * hidden
    )
    return (value, slope)


def halo_rows(up, mid, down, left, right, at):
    lane = lane_ids(CT)
    l = left[at, :].astype(f32)
    r = right[at, :].astype(f32)
    rows = []
    for i in range(SPAN):
        if i < HALF:
            x = up[i, at, :]
        elif i < SPAN - HALF:
            x = mid[i - HALF, at, :]
        else:
            x = down[i - (SPAN - HALF), at, :]
        edge = jnp.where(
            lane >= 64, rolled(l, LANES - HALF - HALF * i), rolled(r, LANES - HALF * i)
        )
        rows.append((x.astype(f32), edge))
    return rows


def window(row, s):
    x, edge = row
    if s == 0:
        return x
    lane = lane_ids(CT)
    mask = (lane < s) if s > 0 else (lane >= LANES + s)
    return rolled(jnp.where(mask, edge, x), -s)


def edges_kernel(up, mid, down, gain, shift, first, last, both):
    both[...] = jnp.concatenate([gain[...], shift[...]], axis=1)
    channels = mid.shape[1]
    lane = lane_ids(CT)

    def step(t, carry):
        at = pl.ds(pl.multiple_of(t * CT, CT), CT)
        head = jnp.zeros((CT, LANES), f32)
        tail = jnp.zeros((CT, LANES), f32)
        for i in range(SPAN):
            if i < HALF:
                x = up[i, at, :]
            elif i < SPAN - HALF:
                x = mid[i - HALF, at, :]
            else:
                x = down[i - (SPAN - HALF), at, :]
            x = x.astype(f32)
            mask = (lane >= HALF * i) & (lane < HALF * i + HALF)
            head = jnp.where(mask, rolled(x, HALF * i), head)
            tail = jnp.where(mask, rolled(x, HALF * i + HALF), tail)
        first[at, :] = head.astype(bf16)
        last[at, :] = tail.astype(bf16)
        return carry

    lax.fori_loop(0, channels // CT, step, 0)


def edges(up, mid, down, gain, shift):
    channels = mid.shape[1]
    shape = jax.ShapeDtypeStruct((channels, LANES), bf16)
    return vcall(
        edges_kernel,
        out_shape=(shape, shape, jax.ShapeDtypeStruct((1, 2 * channels), f32)),
        name="edges",
    )(up, mid, down, gain, shift)


def accumulate_taps(rows, kern, at, flip):
    accum = [jnp.zeros((CT, LANES), f32) for _ in range(SPAN - KSIZE + 1)]
    weights = kern[at, :]
    for b in range(KSIZE):
        shifted = [window(row, b - HALF) for row in rows]
        for a in range(KSIZE):
            tap = a * KSIZE + b
            if flip:
                tap = KSIZE * KSIZE - 1 - tap
            w = jnp.broadcast_to(weights[:, tap : tap + 1], (CT, LANES))
            for i in range(len(accum)):
                accum[i] = accum[i] + w * shifted[i + a]
    return accum


def forward_kernel(up, mid, down, left, right, kern, affine, cot, mixed, payload):
    tile_rows, channels, _ = mid.shape

    def step(t, carry):
        at = pl.ds(pl.multiple_of(t * CT, CT), CT)
        rows = halo_rows(up, mid, down, left, right, at)
        accum = accumulate_taps(rows, kern, at, False)
        for i in range(tile_rows):
            mixed[at, i * LANES : (i + 1) * LANES] = accum[i]
        return carry

    lax.fori_loop(0, channels // CT, step, 0)
    for i in range(tile_rows):
        cols = slice(i * LANES, (i + 1) * LANES)
        x = mixed[:, cols]
        mean = jnp.sum(x, axis=0, keepdims=True) / channels
        dev = x - mean
        spread = jnp.sum(dev * dev, axis=0, keepdims=True)
        rows = split3(mean) + split3(spread)
        stats = jnp.concatenate(rows + [jnp.zeros((CT - 6, LANES), f32)], axis=0)
        if i == 0:
            row_id = lax.broadcasted_iota(jnp.int32, (CT, LANES), 0)
            for k, part in enumerate(split3(affine[...])):
                stats = jnp.where(row_id == 6 + k, jnp.broadcast_to(part, (CT, LANES)), stats)
        dev = dev.astype(bf16)
        stats = stats.astype(bf16)
        for d in range(payload.shape[0]):
            payload[d, 0:channels, cols] = dev
            payload[d, channels : 2 * channels, cols] = cot[i]
            payload[d, 2 * channels : 2 * channels + CT, cols] = stats


def forward(up, mid, down, left, right, kern, affine, cot, parts):
    tile_rows, channels, _ = mid.shape
    pixels = tile_rows * LANES
    return vcall(
        forward_kernel,
        out_shape=(
            jax.ShapeDtypeStruct((channels, pixels), f32),
            jax.ShapeDtypeStruct((parts, 2 * channels + CT, pixels), bf16),
        ),
        name="forward",
    )(up, mid, down, left, right, kern, affine, cot)


def column(row, n):
    i = lax.broadcasted_iota(jnp.int32, (n, n), 0)
    j = lax.broadcasted_iota(jnp.int32, (n, n), 1)
    return jnp.sum(jnp.where(i == j, jnp.broadcast_to(row, (n, n)), 0.0), axis=1, keepdims=True)


def dot(a, b, dims):
    return lax.dot_general(a, b, (dims, ((), ())), preferred_element_type=f32)


def row_chunk(r, size):
    return (r % 2) * (size // 2) + r // 2


def halves(ref, send, keep):
    n = send.shape[0]
    bit = lax.axis_index("row") % 2
    send[...] = ref[pl.ds(pl.multiple_of((1 - bit) * n, n), n), :]
    keep[...] = ref[pl.ds(pl.multiple_of(bit * n, n), n), :]


def spread_kernel(x, recv, *rest):
    outs, total = rest[:-1], rest[-1]
    total[...] = x[...] + recv[...]
    n = outs[0].shape[0]
    y = lax.axis_index("row") // 2
    for m, out in enumerate(outs):
        low, high = y % 2, y // 2
        low = 1 - low if m % 2 else low
        high = 1 - high if m // 2 else high
        out[...] = total[pl.ds(pl.multiple_of((2 * high + low) * n, n), n), :].astype(out.dtype)


def spread(x, recv, parts):
    shape = (x.shape[0] // parts, LANES)
    return vcall(
        spread_kernel,
        out_shape=tuple(jax.ShapeDtypeStruct(shape, bf16 if m else f32) for m in range(parts)),
        scratch_shapes=[pltpu.VMEM(x.shape, f32)],
        name="spread",
    )(x, recv)


def reduce_rows(send, keep):
    size = lax.axis_size("row")
    recv = lax.ppermute(send, "row", [(i, i ^ 1) for i in range(size)])
    if size == 2:
        return [keep, recv]
    chunks = spread(keep, recv, size // 2)
    out = [chunks[0]]
    for m in range(1, size // 2):
        out.append(lax.ppermute(chunks[m], "row", [(i, i ^ (2 * m)) for i in range(size)]))
    return out


def mlp_kernel(recv, w_exp, bias, w_red, payload, stats_out, send, keep, off, grads, s_norm, s_act, s_cot, s_gh):
    parts, height, pixels = recv.shape
    ch = (height - CT) // 2
    total = parts * ch
    width = 2 * LANES
    gains, shifts = [], []
    for k in range(parts):
        head = recv[k, 2 * ch : 2 * ch + CT, 0:LANES].astype(f32)
        both = head[6:7] + head[7:8] + head[8:9]
        gains.append(column(both[:, 0:ch], ch))
        shifts.append(column(both[:, ch : 2 * ch], ch))
    bias_col = column(bias[...], bias.shape[1])
    for blk in range(pixels // width):
        cols = slice(blk * width, (blk + 1) * width)
        means, spreads = [], []
        for k in range(parts):
            st = recv[k, 2 * ch : 2 * ch + CT, cols].astype(f32)
            means.append(st[0:1] + st[1:2] + st[2:3])
            spreads.append(st[3:4] + st[4:5] + st[5:6])
        centre = sum(means) / parts
        spread = sum(spreads)
        for k in range(parts):
            gap = means[k] - centre
            spread = spread + ch * gap * gap
        inverse = lax.rsqrt(spread / total + epsilon)
        stats_out[0:1, cols] = centre
        stats_out[1:2, cols] = inverse
        for k in range(parts):
            at = slice(k * ch, (k + 1) * ch)
            dev = recv[k, 0:ch, cols].astype(f32)
            normed = (dev + (means[k] - centre)) * inverse
            s_norm[at, cols] = (normed * gains[k] + shifts[k]).astype(bf16)
            s_cot[at, cols] = recv[k, ch : 2 * ch, cols]
        hidden = dot(w_exp[...], s_norm[:, cols], ((0,), (0,))) + bias_col
        value, slope = gelu_pair(hidden)
        active = value.astype(bf16)
        s_act[:, cols] = active
        gh = (dot(w_red[...], s_cot[:, cols], ((1,), (0,))) * slope).astype(bf16)
        s_gh[:, cols] = gh
        mlp = dot(w_red[...], active, ((0,), (0,)))
        part = dot(w_exp[...], gh, ((1,), (0,)))
        plain = jnp.zeros((1, width), f32)
        cross = jnp.zeros((1, width), f32)
        for k in range(parts):
            at = slice(k * ch, (k + 1) * ch)
            dev = recv[k, 0:ch, cols].astype(f32)
            normed = (dev + (means[k] - centre)) * inverse
            scaled = part[at] * gains[k]
            plain = plain + jnp.sum(scaled, axis=0, keepdims=True)
            cross = cross + jnp.sum(scaled * normed, axis=0, keepdims=True)
            payload[k, 0:ch, cols] = mlp[at].astype(bf16)
            payload[k, ch : 2 * ch, cols] = part[at].astype(bf16)
        sums = jnp.concatenate(
            split3(plain) + split3(cross) + [jnp.zeros((CT - 6, width), f32)], axis=0
        ).astype(bf16)
        for k in range(parts):
            payload[k, 2 * ch : 2 * ch + CT, cols] = sums
    last = ((1,), (1,))
    grad_exp = dot(s_norm[...], s_gh[...], last)
    grad_red = dot(s_act[...], s_cot[...], last)
    n = grad_exp.shape[0]
    grads[0:n, :] = grad_exp[:, 0:LANES]
    grads[n : 2 * n, :] = grad_exp[:, LANES:]
    grads[2 * n : 3 * n, :] = grad_red[:, 0:LANES]
    grads[3 * n : 4 * n, :] = grad_red[:, LANES:]
    halves(grads, send, keep)
    sums = dot(s_gh[...], jnp.ones((pixels, LANES), bf16), ((1,), (0,)))
    table = jnp.zeros((ch, LANES), f32)
    lane = lane_ids(ch)
    for j in range(sums.shape[0] // ch):
        table = jnp.where(lane == OFFSET + j, sums[j * ch : (j + 1) * ch], table)
    off[...] = table


def mlp(recv, w_exp, bias, w_red):
    _, _, pixels = recv.shape
    hid = w_red.shape[0]
    total = w_exp.shape[0]
    return vcall(
        mlp_kernel,
        out_shape=(
            jax.ShapeDtypeStruct(recv.shape, bf16),
            jax.ShapeDtypeStruct((2, pixels), f32),
            jax.ShapeDtypeStruct((2 * total, LANES), f32),
            jax.ShapeDtypeStruct((2 * total, LANES), f32),
            jax.ShapeDtypeStruct(((recv.shape[1] - CT) // 2, LANES), f32),
        ),
        scratch_shapes=[
            pltpu.VMEM((4 * total, LANES), f32),
            pltpu.VMEM((total, pixels), bf16),
            pltpu.VMEM((hid, pixels), bf16),
            pltpu.VMEM((total, pixels), bf16),
            pltpu.VMEM((hid, pixels), bf16),
        ],
        name="mlp",
    )(recv, w_exp, bias, w_red)


def norm_back_kernel(recv, mixed, stats, gain, image, off, result, grad_mixed, rounded, small):
    parts, height, _ = recv.shape
    ch = (height - CT) // 2
    tile_rows = image.shape[0]
    total = parts * ch
    gain_col = column(gain[...], ch)
    acc_gain = jnp.zeros((ch, LANES), f32)
    acc_shift = jnp.zeros((ch, LANES), f32)
    for i in range(tile_rows):
        cols = slice(i * LANES, (i + 1) * LANES)
        mlp_out = jnp.zeros((ch, LANES), f32)
        grad = jnp.zeros((ch, LANES), f32)
        sums = jnp.zeros((CT, LANES), f32)
        for k in range(parts):
            mlp_out = mlp_out + recv[k, 0:ch, cols].astype(f32)
            grad = grad + recv[k, ch : 2 * ch, cols].astype(f32)
            sums = sums + recv[k, 2 * ch : 2 * ch + CT, cols].astype(f32)
        result[i] = (image[i].astype(f32) + mlp_out).astype(bf16)
        plain = (sums[0:1] + sums[1:2] + sums[2:3]) / total
        cross = (sums[3:4] + sums[4:5] + sums[5:6]) / total
        inverse = stats[1:2, cols]
        normed = (mixed[:, cols] - stats[0:1, cols]) * inverse
        acc_gain = acc_gain + grad * normed
        acc_shift = acc_shift + grad
        out = inverse * (grad * gain_col - plain - normed * cross)
        grad_mixed[i] = out
        rounded[i] = out.astype(bf16)
    g = jnp.sum(acc_gain, axis=1, keepdims=True)
    s = jnp.sum(acc_shift, axis=1, keepdims=True)
    lane = lane_ids(ch)
    small[...] = jnp.where(lane == GAIN, g, jnp.where(lane == SHIFT, s, off[...]))


def norm_back(recv, mixed, stats, gain, image, off):
    _, channels, _ = image.shape
    return vcall(
        norm_back_kernel,
        out_shape=(
            jax.ShapeDtypeStruct(image.shape, bf16),
            jax.ShapeDtypeStruct(image.shape, f32),
            jax.ShapeDtypeStruct(image.shape, bf16),
            jax.ShapeDtypeStruct((channels, LANES), f32),
        ),
        name="norm_back",
    )(recv, mixed, stats, gain, image, off)


def tap_grad_kernel(up, mid, down, left, right, grad_mixed, small, *rest):
    pieces, (out, table_ref, total) = rest[:-3], rest[-3:]
    tile_rows, channels, _ = mid.shape
    lane = lane_ids(CT)

    def step(t, carry):
        at = pl.ds(pl.multiple_of(t * CT, CT), CT)
        rows = halo_rows(up, mid, down, left, right, at)
        grads = [grad_mixed[i, at, :] for i in range(tile_rows)]
        table = small[at, :]
        for b in range(KSIZE):
            shifted = [window(row, b - HALF) for row in rows]
            for a in range(KSIZE):
                accum = grads[0] * shifted[a]
                for i in range(1, tile_rows):
                    accum = accum + grads[i] * shifted[a + i]
                value = jnp.sum(accum, axis=1, keepdims=True)
                table = jnp.where(lane == a * KSIZE + b, value, table)
        table_ref[at, :] = table
        return carry

    lax.fori_loop(0, channels // CT, step, 0)
    half = channels // 2
    total[...] = table_ref[0:half, :] + rolled(table_ref[half:channels, :], LANES // 2)
    cols, height, _ = out.shape
    part = pieces[0].shape[0] // cols
    per = total.shape[0] // cols
    pad = height - part - 2 * per
    for c in range(cols):
        at = slice(c * part, (c + 1) * part)
        big = sum(x[at, :].astype(f32) for x in pieces)
        tile = [big, hi_lo(total[c * per : (c + 1) * per, :])]
        if pad:
            tile.append(jnp.zeros((pad, LANES), f32))
        out[c] = jnp.concatenate(tile, axis=0).astype(bf16)


def tap_grad(up, mid, down, left, right, grad_mixed, small, pieces, cols):
    channels = mid.shape[1]
    part, per = pieces[0].shape[0] // cols, channels // 2 // cols
    height = part + -(-2 * per // 8) * 8
    return vcall(
        tap_grad_kernel,
        out_shape=jax.ShapeDtypeStruct((cols, height, LANES), bf16),
        scratch_shapes=[pltpu.VMEM((channels, LANES), f32), pltpu.VMEM((channels // 2, LANES), f32)],
        name="tap_grad",
    )(up, mid, down, left, right, grad_mixed, small, *pieces)


def backward_kernel(up, mid, down, left, right, kern, cot, out):
    tile_rows, channels, _ = mid.shape

    def step(t, carry):
        at = pl.ds(pl.multiple_of(t * CT, CT), CT)
        rows = halo_rows(up, mid, down, left, right, at)
        accum = accumulate_taps(rows, kern, at, True)
        for i in range(tile_rows):
            out[i, at, :] = (cot[i, at, :].astype(f32) + accum[i]).astype(bf16)
        return carry

    lax.fori_loop(0, channels // CT, step, 0)


def backward(up, mid, down, left, right, kern, cot):
    return vcall(
        backward_kernel,
        out_shape=jax.ShapeDtypeStruct(cot.shape, bf16),
        name="backward",
    )(up, mid, down, left, right, kern, cot)


def hi_lo(x):
    hi = x.astype(bf16).astype(f32)
    return jnp.concatenate([hi, x - hi], axis=0)


def col_pack_kernel(per, recv, out):
    total = recv[0].astype(f32)
    for c in range(1, recv.shape[0]):
        total = total + recv[c].astype(f32)
    part = total.shape[0] - -(-2 * per // 8) * 8
    tail = hi_lo(total[part : part + per] + total[part + per : part + 2 * per])
    pad = total.shape[0] - part - 2 * per
    pieces = [total[0:part], tail] + ([jnp.zeros((pad, LANES), f32)] if pad else [])
    tile = jnp.concatenate(pieces, axis=0).astype(bf16)
    for c in range(out.shape[0]):
        out[c] = tile


def col_pack(recv, per):
    return vcall(
        functools.partial(col_pack_kernel, per),
        out_shape=jax.ShapeDtypeStruct(recv.shape, bf16),
        name="col_pack",
    )(recv)


def row_pack_kernel(per, recv, out, tile):
    cols, height, _ = recv.shape
    part = height - -(-2 * per // 8) * 8
    base = cols * part
    for c in range(cols):
        x = recv[c].astype(f32)
        tile[c * part : (c + 1) * part, :] = x[0:part]
        small = x[part : part + per] + x[part + per : part + 2 * per]
        tile[base + c * per : base + (c + 1) * per, :] = small
    x = tile[...].astype(bf16)
    for r in range(out.shape[0]):
        out[r] = x


def row_pack(recv, rows, per):
    cols, height, _ = recv.shape
    tall = cols * (height - -(-2 * per // 8) * 8 + per)
    return vcall(
        functools.partial(row_pack_kernel, per),
        out_shape=jax.ShapeDtypeStruct((rows, tall, LANES), bf16),
        scratch_shapes=[pltpu.VMEM((tall, LANES), f32)],
        name="row_pack",
    )(recv)


def final_kernel(scale, flat, exp_ref, red_ref, taps_ref, gain_ref, shift_ref, off_ref):
    rows = flat.shape[0]
    n = exp_ref.shape[0]
    per = taps_ref.shape[1] // 2
    size_all = 4 * n // rows
    for r in range(rows):
        x = flat[r].astype(f32) * scale
        block = x[0:size_all]
        tail = x[size_all : size_all + per]
        total = tail if r == 0 else total + tail
        start = row_chunk(r, rows) * size_all
        lo = 0
        while lo < size_all:
            which, at = divmod(start + lo, n)
            size = min(size_all - lo, n - at)
            ref = (exp_ref, red_ref)[which // 2]
            lane = (which % 2) * LANES
            ref[at : at + size, lane : lane + LANES] = block[lo : lo + size]
            lo += size
    x = total
    both = jnp.concatenate([x, rolled(x, LANES // 2)], axis=0)
    wide = jnp.concatenate([both, jnp.zeros((LANES - both.shape[0], LANES), f32)], axis=0)
    flip = jnp.transpose(wide)[:, 0 : both.shape[0]]
    taps_ref[...] = flip[0 : taps_ref.shape[0], :]
    gain_ref[...] = flip[GAIN : GAIN + 1]
    shift_ref[...] = flip[SHIFT : SHIFT + 1]
    channels = flip.shape[1]
    for j in range(off_ref.shape[1] // channels):
        off_ref[:, j * channels : (j + 1) * channels] = flip[OFFSET + j : OFFSET + j + 1]


def final(flat, scale, total, hid, channels, taps):
    return vcall(
        functools.partial(final_kernel, scale),
        out_shape=(
            jax.ShapeDtypeStruct((total, hid), f32),
            jax.ShapeDtypeStruct((hid, total), f32),
            jax.ShapeDtypeStruct((taps, channels), f32),
            jax.ShapeDtypeStruct((1, channels), f32),
            jax.ShapeDtypeStruct((1, channels), f32),
            jax.ShapeDtypeStruct((1, hid), f32),
        ),
        name="final",
    )(flat)


def neighbours(first, last, axis):
    size = lax.axis_size(axis)
    up = [(i, i + 1) for i in range(size - 1)]
    down = [(j, i) for i, j in up]
    return lax.ppermute(last, axis, up), lax.ppermute(first, axis, down)


def halo(x, gain, shift):
    rows = x.shape[0]
    up, down = neighbours(x[:HALF], x[rows - HALF :], "row")
    first, last, both = edges(up, x, down, gain, shift)
    left, right = neighbours(first, last, "col")
    return up, down, left, right, both


def exchange(x, axis):
    return lax.all_to_all(x, axis, 0, 0)


def reduce_cols(part, per):
    part = exchange(part, "col")
    flat = exchange(col_pack(part, per), "col")
    return exchange(row_pack(flat, lax.axis_size("row"), per), "row")


def body(
    image, depth_kernel, norm_gain, norm_shift, expand_weight, expand_bias, reduce_weight, cotangent
):
    channels, tile_rows, tile_cols = image.shape
    pixels = tile_rows * tile_cols
    parts = lax.axis_size("ch")
    hid = reduce_weight.shape[0]
    total = expand_weight.shape[0]
    img = jnp.transpose(image, (1, 0, 2))
    cot = jnp.transpose(cotangent, (1, 0, 2))
    gain = norm_gain.reshape(1, channels)
    shift = norm_shift.reshape(1, channels)
    bias = lax.dynamic_slice_in_dim(expand_bias, lax.axis_index("ch") * hid, hid).reshape(1, hid)
    up, down, left, right, affine = halo(img, gain, shift)
    mixed, send = forward(up, img, down, left, right, depth_kernel, affine, cot, parts)
    recv = exchange(send, "ch")
    send, stats, give, keep, off = mlp(recv, expand_weight, bias, reduce_weight)
    recv = exchange(send, "ch")
    pieces = reduce_rows(give, keep)
    result, grad_mixed, rounded, small = norm_back(recv, mixed, stats, gain, img, off)
    g_up, g_down, g_left, g_right, _ = halo(rounded, gain, shift)
    cols = lax.axis_size("col")
    part = tap_grad(up, img, down, left, right, grad_mixed, small, pieces, cols)
    grad_image = backward(g_up, rounded, g_down, g_left, g_right, depth_kernel, cot)
    flat = reduce_cols(part, channels // 2 // cols)
    pixels_all = pixels * lax.axis_size("row") * lax.axis_size("col")
    scale = float(pixels_all) ** (-0.5)
    grad_exp, grad_red, grad_taps, grad_gain, grad_shift, grad_off = final(
        flat, scale, total, hid, channels, depth_kernel.shape[1]
    )
    return (
        jnp.transpose(result, (1, 0, 2)),
        jnp.transpose(grad_image, (1, 0, 2)),
        jnp.transpose(grad_taps),
        grad_gain.reshape(channels),
        grad_shift.reshape(channels),
        grad_exp,
        grad_off.reshape(hid),
        grad_red,
    )


def solution(mesh):
    in_specs = (
        P("ch", "row", "col"),
        P("ch", None),
        P("ch"),
        P("ch"),
        P(None, "ch"),
        P(),
        P("ch", None),
        P("ch", "row", "col"),
    )
    out_specs = (
        P("ch", "row", "col"),
        P("ch", "row", "col"),
        P("ch", None),
        P("ch"),
        P("ch"),
        P(None, "ch"),
        P("ch"),
        P("ch", None),
    )

    return jax.shard_map(body, mesh=mesh, in_specs=in_specs, out_specs=out_specs, check_vma=False)
```
